128 devices in a mesh: dp: 4 (over x), ctx: 32 (over z, y, core).
Axes of the slice: x: 4, y: 4, z: 4, core: 2. Of those that a mesh axis runs over, the one named last changes fastest.
Arguments:
- queries: bfloat16 [4, 8192, 2048], P('dp', 'ctx'), may hold values from -6 to 6
- keys: bfloat16 [4, 8192, 2048], P('dp', 'ctx'), may hold values from -6 to 6
- values: bfloat16 [4, 8192, 2048], P('dp', 'ctx'), may hold values from -6 to 6
- gain: float32 [2048], replicated, may hold values from 0.1 to 1.9
- out_weight: bfloat16 [2048, 4096], P('dp'), may hold values from -0.125 to 0.125
- grad_out: bfloat16 [4, 8192, 4096], P('dp', 'ctx'), may hold values from -6 to 6
Outputs:
- layer_out: bfloat16 [4, 8192, 4096], P('dp', 'ctx')
- grad_queries: bfloat16 [4, 8192, 2048], P('dp', 'ctx')
- grad_keys: bfloat16 [4, 8192, 2048], P('dp', 'ctx')
- grad_values: bfloat16 [4, 8192, 2048], P('dp', 'ctx')
- grad_weight: float32 [2048, 4096], P(('dp', 'ctx'))
The draws below stay inside these ranges and needn't reach their ends.
All inputs are finite; a program needn't handle non-finite values.
Results may differ from the reference program's by a relative error of at most 0.015.
Values may be sent and summed in bfloat16 or wider, within the bound.
No kernel may reach another device: no remote copies, remote signals or barrier semaphores. Data moves between devices by JAX's collectives and lax.ppermute only.
A program may use at most 192 MiB of HBM per device.

```python
import math
import jax
import jax.numpy as jnp
from jax import lax

D = 4096
H = 16
HD = 128
TOK_DEV = 256
HF = 2048
SEQ = 8192
SEQS = 4
N_CTX = 32


def block_scale(stream_key, dims, shards, low, largest):
    def one(dim, parts):
        heights = jax.random.uniform(jax.random.fold_in(jax.random.fold_in(stream_key, 6), dim), (parts,), jnp.float32, low / len(shards), largest / len(shards))
        return jnp.repeat(jnp.exp(heights), dims[dim] // parts).reshape((-1,) + (1,) * (len(dims) - dim - 1))

    level = one(*shards[0])
    for cut in shards[1:]:
        level = level * one(*cut)
    return level


def gaussian(rng, dims, deviation, reach, cuts=(), held_as=jnp.bfloat16):
    result = deviation * jax.random.normal(rng, dims, jnp.float32)
    if cuts:
        result = result * block_scale(rng, dims, cuts, -0.22, 0.18)
    return jnp.clip(result, -reach, reach).astype(held_as)


def setup_inputs(seed: int = 0) -> dict:
    streams_of = jax.random.split(jax.random.key(seed), 7)
    queries = gaussian(streams_of[0], (SEQS, SEQ, HF), 1.0, 6.0, ((0, 4), (1, 32)))
    keys = gaussian(streams_of[1], (SEQS, SEQ, HF), 1.0, 6.0, ((0, 4), (1, 32)))
    values = gaussian(streams_of[2], (SEQS, SEQ, HF), 1.0, 6.0, ((0, 4), (1, 32)))
    gain = jnp.clip(1.0 + 0.18 * jax.random.normal(streams_of[3], (HF,), jnp.float32), 0.1, 1.9)
    out_weight = gaussian(streams_of[4], (HF, D), HF ** -0.5, 0.125, ((0, 4),))
    grad_out = gaussian(streams_of[5], (SEQS, SEQ, D), 1.0, 6.0, ((0, 4), (1, 32)))
    return {"queries": queries, "keys": keys, "values": values, "gain": gain, "out_weight": out_weight, "grad_out": grad_out}


EPSILON = 1e-06
HIGHEST = lax.Precision.HIGHEST

def to_blocks(array):
    return array.reshape(N_CTX, TOK_DEV, H, HD).astype(jnp.float32)

def causal_mask():
    row_index = jnp.arange(TOK_DEV)[:, None]
    col_index = jnp.arange(TOK_DEV)[None, :]
    return row_index >= col_index

def exclusive_sum(terms, reverse):
    empty = jnp.zeros_like(terms[:1])
    if reverse:
        running = jnp.cumsum(terms[::-1], axis=0)[::-1]
        return jnp.concatenate([running[1:], empty], axis=0)
    running = jnp.cumsum(terms, axis=0)
    return jnp.concatenate([empty, running[:-1]], axis=0)

def round_half(array):
    return lax.optimization_barrier(array.astype(jnp.bfloat16)).astype(jnp.float32)

def block_weights(query_blocks, key_blocks):
    scores = jnp.einsum('bthd,bshd->bhts', query_blocks, key_blocks, precision=HIGHEST)
    return round_half(jnp.where(causal_mask(), scores, 0.0))

def forward_sequence(inputs):
    query_blocks = to_blocks(inputs[0])
    key_blocks = to_blocks(inputs[1])
    value_blocks = to_blocks(inputs[2])
    weights = block_weights(query_blocks, key_blocks)
    local_out = jnp.einsum('bhts,bshd->bthd', weights, value_blocks, precision=HIGHEST)
    local_state = jnp.einsum('bshd,bshe->bhde', key_blocks, value_blocks, precision=HIGHEST)
    carried = exclusive_sum(local_state, False)
    state_out = jnp.einsum('bthd,bhde->bthe', query_blocks, carried, precision=HIGHEST)
    return (local_out + state_out).reshape(SEQ, H, HD)

def backward_sequence(inputs):
    query_blocks = to_blocks(inputs[0])
    key_blocks = to_blocks(inputs[1])
    value_blocks = to_blocks(inputs[2])
    grad_blocks = to_blocks(inputs[3])
    weights = block_weights(query_blocks, key_blocks)
    local_state = jnp.einsum('bshd,bshe->bhde', key_blocks, value_blocks, precision=HIGHEST)
    carried = exclusive_sum(local_state, False)
    grad_scores = jnp.einsum('bthe,bshe->bhts', grad_blocks, value_blocks, precision=HIGHEST)
    grad_scores = round_half(jnp.where(causal_mask(), grad_scores, 0.0))
    local_grad = jnp.einsum('bthd,bthe->bhde', query_blocks, grad_blocks, precision=HIGHEST)
    later = exclusive_sum(local_grad, True)
    grad_query = jnp.einsum('bhts,bshd->bthd', grad_scores, key_blocks, precision=HIGHEST)
    grad_query = grad_query + jnp.einsum('bthe,bhde->bthd', grad_blocks, carried, precision=HIGHEST)
    grad_key = jnp.einsum('bhts,bthd->bshd', grad_scores, query_blocks, precision=HIGHEST)
    grad_key = grad_key + jnp.einsum('bshe,bhde->bshd', value_blocks, later, precision=HIGHEST)
    grad_value = jnp.einsum('bhts,bthe->bshe', weights, grad_blocks, precision=HIGHEST)
    grad_value = grad_value + jnp.einsum('bshd,bhde->bshe', key_blocks, later, precision=HIGHEST)
    return (grad_query.reshape(SEQ, H * HD).astype(jnp.bfloat16), grad_key.reshape(SEQ, H * HD).astype(jnp.bfloat16), grad_value.reshape(SEQ, H * HD).astype(jnp.bfloat16))

def reference(queries, keys, values, gain, out_weight, grad_out):
    attended = lax.map(forward_sequence, (queries, keys, values))
    inv_rms = lax.rsqrt(lax.optimization_barrier(jnp.mean(attended * attended, axis=-1, keepdims=True)) + EPSILON)
    unit_out = attended * inv_rms
    gain_heads = gain.reshape(H, HD)
    normed = (unit_out * gain_heads).astype(jnp.bfloat16).reshape(SEQS * SEQ, H * HD)
    grad_rows = grad_out.reshape(SEQS * SEQ, D)
    layer_out = jnp.dot(normed, out_weight, preferred_element_type=jnp.float32)
    layer_out = layer_out.astype(jnp.bfloat16).reshape(SEQS, SEQ, D)
    grad_normed = jnp.dot(grad_rows, out_weight.T, preferred_element_type=jnp.float32)
    grad_unit = grad_normed.reshape(SEQS, SEQ, H, HD) * gain_heads
    grad_attn = inv_rms * (grad_unit - unit_out * lax.optimization_barrier(jnp.mean(grad_unit * unit_out, axis=-1, keepdims=True)))
    grad_attn = grad_attn.astype(jnp.bfloat16)
    grad_queries, grad_keys, grad_values = lax.map(backward_sequence, (queries, keys, values, grad_attn))
    grad_weight = jnp.dot(normed.T, grad_rows, preferred_element_type=jnp.float32)
    grad_weight = grad_weight * (1.0 / math.sqrt(SEQS * SEQ))
    return (layer_out, grad_queries, grad_keys, grad_values, grad_weight)
```

```python
import functools
import math

import jax
import jax.numpy as jnp
from jax import lax
from jax.experimental import pallas as pl
from jax.experimental.pallas import tpu as pltpu
from jax.sharding import Mesh, PartitionSpec as P

HD = 128
EPSILON = 1e-06
BF = jnp.bfloat16
F32 = jnp.float32
CTX = ("z", "y", "c")
CH = 4
HC = 4


def mm(a, b, ca, cb):
    return lax.dot_general(a, b, (((ca,), (cb,)), ((), ())), preferred_element_type=F32)


def cost(flops, nbytes):
    return pl.CostEstimate(flops=flops, bytes_accessed=nbytes, transcendentals=0)


def head(ref, h):
    return ref[:, h * HD : (h + 1) * HD]


def causal(n):
    return lax.broadcasted_iota(jnp.int32, (n, n), 0) >= lax.broadcasted_iota(
        jnp.int32, (n, n), 1
    )


def state_body(k_ref, v_ref, s_ref):
    for h in range(HC):
        s_ref[h] = mm(head(k_ref, h), head(v_ref, h), 0, 0).astype(BF)


def local_state(k, v):
    t, f = k.shape
    w = f // CH
    blk = pl.BlockSpec((t, w), lambda g: (0, g))
    return pl.pallas_call(
        state_body,
        grid=(CH,),
        in_specs=[blk, blk],
        out_specs=pl.BlockSpec((HC, HD, HD), lambda g: (g, 0, 0)),
        out_shape=jax.ShapeDtypeStruct((CH * HC, HD, HD), BF),
        cost_estimate=cost(2 * t * f * HD, 4 * t * f),
        name="local_state",
    )(k, v)


def scan_body(reverse, s_ref, o_ref):
    n = s_ref.shape[0]
    total = jnp.zeros(s_ref.shape[1:], F32)
    for step in range(n):
        at = n - 1 - step if reverse else step
        o_ref[at] = total.astype(BF)
        if step < n - 1:
            total = total + s_ref[at].astype(F32)


def scan_blocks(s, reverse):
    return pl.pallas_call(
        functools.partial(scan_body, reverse),
        out_shape=jax.ShapeDtypeStruct(s.shape, BF),
        cost_estimate=cost(s.size, 4 * s.size),
        name="scan_blocks",
    )(s)


def carry(state, reverse):
    n = lax.axis_size(CTX)
    parts = state.reshape(n, -1, HD)
    theirs = lax.all_to_all(parts, CTX, 0, 0, tiled=True)
    sums = scan_blocks(theirs, reverse)
    mine = lax.all_to_all(sums, CTX, 0, 0, tiled=True)
    return mine.reshape(state.shape)


def scores_body(q_ref, k_ref, v_ref, w_ref, o_ref):
    keep = causal(q_ref.shape[0])
    for h in range(HC):
        w = jnp.where(keep, mm(head(q_ref, h), head(k_ref, h), 1, 1), 0.0).astype(BF)
        w_ref[h] = w
        o_ref[:, h * HD : (h + 1) * HD] = mm(w, head(v_ref, h), 1, 0)


def local_scores(q, k, v):
    t, f = q.shape
    w = f // CH
    blk = pl.BlockSpec((t, w), lambda g: (0, g))
    return pl.pallas_call(
        scores_body,
        grid=(CH,),
        in_specs=[blk, blk, blk],
        out_specs=[pl.BlockSpec((HC, t, t), lambda g: (g, 0, 0)), blk],
        out_shape=[
            jax.ShapeDtypeStruct((CH * HC, t, t), BF),
            jax.ShapeDtypeStruct((t, f), F32),
        ],
        cost_estimate=cost(4 * t * t * f, 14 * t * f),
        name="local_scores",
    )(q, k, v)


def attend_body(q_ref, o_ref, c_ref, g_ref, n_ref, a_ref):
    for h in range(HC):
        cols = slice(h * HD, (h + 1) * HD)
        a = o_ref[:, cols] + mm(head(q_ref, h), c_ref[h], 1, 0)
        a_ref[0, :, cols] = a
        inv = lax.rsqrt(jnp.mean(a * a, axis=-1, keepdims=True) + EPSILON)
        n_ref[0, :, cols] = (a * inv * g_ref[:, cols]).astype(BF)


def attend(q, out, carried, gain):
    t, f = q.shape
    w = f // CH
    blk = pl.BlockSpec((t, w), lambda g: (0, g))
    st = pl.BlockSpec((HC, HD, HD), lambda g: (g, 0, 0))
    chunk = pl.BlockSpec((1, t, w), lambda g: (g, 0, 0))
    return pl.pallas_call(
        attend_body,
        grid=(CH,),
        in_specs=[blk, blk, st, pl.BlockSpec((1, w), lambda g: (0, g))],
        out_specs=[chunk, chunk],
        out_shape=[
            jax.ShapeDtypeStruct((CH, t, w), BF),
            jax.ShapeDtypeStruct((CH, t, w), F32),
        ],
        cost_estimate=cost(2 * t * f * HD, 12 * t * f),
        name="attend",
    )(q, out, carried, gain)


def grad_attn_body(i_ref, q_ref, a_ref, gn_ref, g_ref, ga_ref, lg_ref):
    for h in range(HC):
        cols = slice(h * HD, (h + 1) * HD)
        a = a_ref[0, :, cols]
        inv = lax.rsqrt(jnp.mean(a * a, axis=-1, keepdims=True) + EPSILON)
        unit = a * inv
        gu = gn_ref[:, cols] * g_ref[:, cols]
        ga = inv * (gu - unit * jnp.mean(gu * unit, axis=-1, keepdims=True))
        ga = ga.astype(BF)
        ga_ref[:, cols] = ga
        lg_ref[h] = mm(head(q_ref, h), ga, 0, 0).astype(BF)


def grad_attn(which, q, attended, gn, gain):
    t, f = q.shape
    w = f // CH
    whole = pl.BlockSpec((t, w), lambda g, i: (0, 0))
    return pl.pallas_call(
        grad_attn_body,
        grid_spec=pltpu.PrefetchScalarGridSpec(
            num_scalar_prefetch=1,
            grid=(1,),
            in_specs=[
                pl.BlockSpec((t, w), lambda g, i: (0, i[0])),
                pl.BlockSpec((1, t, w), lambda g, i: (i[0], 0, 0)),
                whole,
                pl.BlockSpec((1, w), lambda g, i: (0, i[0])),
            ],
            out_specs=[whole, pl.BlockSpec((HC, HD, HD), lambda g, i: (0, 0, 0))],
        ),
        out_shape=[
            jax.ShapeDtypeStruct((t, w), BF),
            jax.ShapeDtypeStruct((HC, HD, HD), BF),
        ],
        cost_estimate=cost(2 * t * w * HD, 12 * t * w),
        name="grad_attn",
    )(which, q, attended, gn, gain)


def grads_body(i_ref, q_ref, k_ref, v_ref, w_ref, ga_ref, c_ref, gq_ref, gk_ref, gv_ref):
    keep = causal(q_ref.shape[0])
    for h in range(HC):
        cols = slice(h * HD, (h + 1) * HD)
        ga = ga_ref[0, :, cols]
        gs = jnp.where(keep, mm(ga, head(v_ref, h), 1, 1), 0.0).astype(BF)
        gq = mm(gs, head(k_ref, h), 1, 0) + mm(ga, c_ref[h], 1, 1)
        gq_ref[:, cols] = gq.astype(BF)
        gk_ref[0, :, cols] = mm(gs, head(q_ref, h), 0, 0)
        gv_ref[0, :, cols] = mm(w_ref[h], ga, 0, 0)


def local_grads(order, q, k, v, weights, ga, carried):
    t, f = q.shape
    w = f // CH
    nat = pl.BlockSpec((t, w), lambda g, i: (0, i[g]))
    chunk = pl.BlockSpec((1, t, w), lambda g, i: (g, 0, 0))
    return pl.pallas_call(
        grads_body,
        grid_spec=pltpu.PrefetchScalarGridSpec(
            num_scalar_prefetch=1,
            grid=(CH,),
            in_specs=[
                nat,
                nat,
                nat,
                pl.BlockSpec((HC, t, t), lambda g, i: (i[g], 0, 0)),
                chunk,
                pl.BlockSpec((HC, HD, HD), lambda g, i: (i[g], 0, 0)),
            ],
            out_specs=[nat, chunk, chunk],
        ),
        out_shape=[
            jax.ShapeDtypeStruct((t, f), BF),
            jax.ShapeDtypeStruct((CH, t, w), F32),
            jax.ShapeDtypeStruct((CH, t, w), F32),
        ],
        cost_estimate=cost(8 * t * t * f, 24 * t * f),
        name="local_grads",
    )(order, q, k, v, weights, ga, carried)


def later_body(i_ref, k_ref, v_ref, l_ref, pk_ref, pv_ref, gk_ref, gv_ref):
    for h in range(HC):
        cols = slice(h * HD, (h + 1) * HD)
        gk = pk_ref[0, :, cols] + mm(head(v_ref, h), l_ref[h], 1, 1)
        gv = pv_ref[0, :, cols] + mm(head(k_ref, h), l_ref[h], 1, 0)
        gk_ref[:, cols] = gk.astype(BF)
        gv_ref[:, cols] = gv.astype(BF)


def later_grads(order, k, v, later, pk, pv):
    t, f = k.shape
    w = f // CH
    nat = pl.BlockSpec((t, w), lambda g, i: (0, i[g]))
    chunk = pl.BlockSpec((1, t, w), lambda g, i: (g, 0, 0))
    return pl.pallas_call(
        later_body,
        grid_spec=pltpu.PrefetchScalarGridSpec(
            num_scalar_prefetch=1,
            grid=(CH,),
            in_specs=[
                nat,
                nat,
                pl.BlockSpec((HC, HD, HD), lambda g, i: (g, 0, 0)),
                chunk,
                chunk,
            ],
            out_specs=[nat, nat],
        ),
        out_shape=[jax.ShapeDtypeStruct((t, f), BF)] * 2,
        cost_estimate=cost(4 * t * f * HD, 16 * t * f),
        name="later_grads",
    )(order, k, v, later, pk, pv)


def layer_body(i_ref, n_ref, *refs):
    o_ref = refs[-1]
    total = None
    for k in range(CH):
        part = mm(n_ref[i_ref[k]], refs[k][...], 1, 0)
        total = part if total is None else total + part
    o_ref[...] = total.astype(BF)


def layer_rows(order, normed, blocks):
    _, t, w = normed.shape
    d = blocks[0].shape[1]
    tile = 512
    return pl.pallas_call(
        layer_body,
        grid_spec=pltpu.PrefetchScalarGridSpec(
            num_scalar_prefetch=1,
            grid=(d // tile,),
            in_specs=[pl.BlockSpec((CH, t, w), lambda g, i: (0, 0, 0))]
            + [pl.BlockSpec((w, tile), lambda g, i: (0, g))] * CH,
            out_specs=pl.BlockSpec((t, tile), lambda g, i: (0, g)),
        ),
        out_shape=jax.ShapeDtypeStruct((t, d), BF),
        cost_estimate=cost(2 * t * CH * w * d, 2 * (CH * w * d + CH * t * w + t * d)),
        name="layer_rows",
    )(order, normed, *blocks)


def weight_body(add, h_ref, n_ref, *refs):
    g_refs, rest = refs[:CH], refs[CH:]
    o_ref, nt = rest[-2], rest[-1]

    @pl.when(pl.program_id(0) == 0)
    def _():
        for s in range(CH):
            nt[s] = n_ref[s].T

    total = None
    for s in range(CH):
        part = mm(nt[s], g_refs[s][...], 1, 0)
        total = part if total is None else total + part
    if add:
        total = total + rest[0][...].astype(F32)
    o_ref[...] = total.astype(BF)


def weight_half(half, normed_all, grads_all, extra):
    _, t, w = normed_all.shape
    d = grads_all[0].shape[1]
    tile = 512
    steps = d // 2 // tile
    own = pl.BlockSpec((w, tile), lambda g, i: (0, g))
    add = extra is not None
    return pl.pallas_call(
        functools.partial(weight_body, add),
        grid_spec=pltpu.PrefetchScalarGridSpec(
            num_scalar_prefetch=1,
            grid=(steps,),
            in_specs=[pl.BlockSpec((CH, t, w), lambda g, i: (0, 0, 0))]
            + [pl.BlockSpec((t, tile), lambda g, i: (0, i[0] * steps + g))] * CH
            + [own] * add,
            out_specs=own,
            scratch_shapes=[pltpu.VMEM((CH, w, t), BF)],
        ),
        out_shape=jax.ShapeDtypeStruct((w, d // 2), BF),
        cost_estimate=cost(CH * t * w * d, CH * t * d + 2 * CH * t * w + w * d),
        name="weight_half",
    )(half, normed_all, *grads_all, *([extra] if add else []))


def sum_body(scale, s_ref, o_ref):
    total = s_ref[0].astype(F32)
    for step in range(1, s_ref.shape[0]):
        total = total + s_ref[step].astype(F32)
    o_ref[...] = total * scale


def sum_parts(parts, scale):
    n, r, w = parts.shape
    return pl.pallas_call(
        functools.partial(sum_body, scale),
        out_shape=jax.ShapeDtypeStruct((r, w), F32),
        cost_estimate=cost(parts.size, 2 * parts.size),
        name="sum_parts",
    )(parts)


def shift(x, axis, by):
    n = lax.axis_size(axis)
    return lax.ppermute(x, axis, [((d + by) % n, d) for d in range(n)])


def shards(queries, keys, values, gain, out_weight, grad_out):
    tok_rows, feat_width = queries.shape[1:]
    model_width = grad_out.shape[2]
    q = queries.reshape(tok_rows, feat_width)
    k = keys.reshape(tok_rows, feat_width)
    v = values.reshape(tok_rows, feat_width)
    grad_rows = grad_out.reshape(tok_rows, model_width)
    gain_row = gain.reshape(1, feat_width)
    seqs = lax.axis_size("x")
    blocks_n = lax.axis_size(CTX)
    at_x = lax.axis_index("x")
    at_ctx = lax.axis_index(CTX)
    at_core = lax.axis_index("c")
    order = (at_x + jnp.arange(CH, dtype=jnp.int32)) % CH

    piece = out_weight.shape[0] // blocks_n
    own_piece = lax.dynamic_slice_in_dim(out_weight, at_ctx * piece, piece, 0)
    blocks = [out_weight]
    for by in range(1, CH):
        blocks.append(lax.all_gather(shift(own_piece, "x", by), CTX, axis=0, tiled=True))

    right = shift(grad_rows, "x", 1)
    left = shift(grad_rows, "x", 3)
    half_cols = model_width // 2
    far_a = shift(right[:, :half_cols], "x", 1)
    far_b = shift(left[:, half_cols:], "x", 3)
    far = jnp.concatenate([far_a, far_b], axis=1)

    carried = carry(local_state(k, v), False)
    weights, local_out = local_scores(q, k, v)
    normed, attended = attend(q, local_out, carried, gain_row)

    ga, lg = [], []
    for n in range(CH):
        gn = mm(grad_rows, blocks[n], 1, 1)
        one_ga, one_lg = grad_attn(order[n : n + 1], q, attended, gn, gain_row)
        ga.append(one_ga)
        lg.append(one_lg)
    later = carry(jnp.concatenate(lg, axis=0), True)
    grad_query, pk, pv = local_grads(order, q, k, v, weights, jnp.stack(ga), carried)
    grad_key, grad_value = later_grads(order, k, v, later, pk, pv)

    layer_out = layer_rows(order, normed, blocks)

    normed_all = lax.all_to_all(normed, "x", 0, 0, tiled=True)
    rel = (jnp.arange(CH, dtype=jnp.int32) + at_x) % seqs
    normed_rot = jnp.take(normed_all, rel, axis=0)
    grads_all = [grad_rows, right, far, left]
    mine = at_core.reshape(1).astype(jnp.int32)
    for_partner = weight_half(1 - mine, normed_rot, grads_all, None)
    from_partner = shift(for_partner, "c", 1)
    partial = weight_half(mine, normed_rot, grads_all, from_partner)
    chips = blocks_n // 2
    rows = partial.shape[0] // chips
    parts = lax.all_to_all(
        partial.reshape(chips, rows, half_cols), ("z", "y"), 0, 0, tiled=True
    )
    token_count = seqs * blocks_n * tok_rows
    summed = sum_parts(parts, 1.0 / math.sqrt(token_count))
    out_rows = rows // 2
    keep = lax.dynamic_slice_in_dim(summed, at_core * out_rows, out_rows, 0)
    give = lax.dynamic_slice_in_dim(summed, (1 - at_core) * out_rows, out_rows, 0)
    got = shift(give, "c", 1)
    first = at_core == 0
    grad_weight = jnp.concatenate(
        [jnp.where(first, keep, got), jnp.where(first, got, keep)], axis=1
    )
    out_shape = (1, tok_rows, feat_width)
    return (
        layer_out.reshape(1, tok_rows, model_width),
        grad_query.reshape(out_shape),
        grad_key.reshape(out_shape),
        grad_value.reshape(out_shape),
        grad_weight,
    )


def solution(mesh):
    mesh = Mesh(mesh.devices.reshape(4, 4, 4, 2), ("x",) + CTX)
    tokens = P("x", CTX, None)
    in_specs = (tokens, tokens, tokens, P(), P("x", None), tokens)
    out_specs = (tokens, tokens, tokens, tokens, P(("x",) + CTX, None))
    return jax.shard_map(shards, mesh=mesh, in_specs=in_specs, out_specs=out_specs, check_vma=False)
```

```python
import functools
import math

import jax
import jax.numpy as jnp
from jax import lax
from jax.experimental import pallas as pl
from jax.experimental.pallas import tpu as pltpu
from jax.sharding import Mesh, PartitionSpec as P

HD = 128
EPSILON = 1e-06
BF = jnp.bfloat16
F32 = jnp.float32
CTX = ("z", "y", "c")
CH = 4
HC = 4


def mm(a, b, ca, cb):
    return lax.dot_general(a, b, (((ca,), (cb,)), ((), ())), preferred_element_type=F32)


def cost(flops, nbytes):
    return pl.CostEstimate(flops=flops, bytes_accessed=nbytes, transcendentals=0)


def head(ref, h):
    return ref[:, h * HD : (h + 1) * HD]


def causal(n):
    return lax.broadcasted_iota(jnp.int32, (n, n), 0) >= lax.broadcasted_iota(
        jnp.int32, (n, n), 1
    )


def state_body(k_ref, v_ref, s_ref):
    for h in range(HC):
        s_ref[h] = mm(head(k_ref, h), head(v_ref, h), 0, 0).astype(BF)


def local_state(k, v):
    t, f = k.shape
    w = f // CH
    blk = pl.BlockSpec((t, w), lambda g: (0, g))
    return pl.pallas_call(
        state_body,
        grid=(CH,),
        in_specs=[blk, blk],
        out_specs=pl.BlockSpec((HC, HD, HD), lambda g: (g, 0, 0)),
        out_shape=jax.ShapeDtypeStruct((CH * HC, HD, HD), BF),
        cost_estimate=cost(2 * t * f * HD, 4 * t * f),
        compiler_params=pltpu.CompilerParams(vmem_limit_bytes=6 << 20),
        name="local_state",
    )(k, v)


def small_call(body, where, args, outs):
    return pl.pallas_call(
        body,
        in_specs=[pl.BlockSpec(memory_space=pltpu.SMEM)]
        + [pl.BlockSpec(memory_space=pltpu.VMEM)] * len(args),
        out_specs=[pl.BlockSpec(memory_space=pltpu.VMEM)] * len(outs),
        out_shape=outs,
        compiler_params=pltpu.CompilerParams(vmem_limit_bytes=6 << 20),
        cost_estimate=cost(1 << 18, 1 << 20),
    )(where, *args)


def chip_body(w_ref, s_ref, r_ref, own_ref, *out_refs):
    y, c = w_ref[6], w_ref[7]
    n = s_ref.shape[1]
    for k in range(n):
        at = lax.rem(y + k, n)
        part = s_ref[c, at].astype(F32) + r_ref[at].astype(F32)
        if k == 0:
            own_ref[...] = part
        else:
            out_refs[k - 1][...] = part.astype(BF)


def row_body(w_ref, own_ref, *refs):
    total = own_ref[...]
    for ref in refs[:-1]:
        total = total + ref[...].astype(F32)
    refs[-1][...] = total.astype(BF)


def plane_body(reverse, w_ref, own_ref, t1, t2, t3, z1, z2, z3, o_ref, o1, o2, o3):
    z, y = w_ref[5], w_ref[6]
    terms = [own_ref[...]] + [t[...].astype(F32) for t in (t1, t2, t3)]
    n = len(terms)
    base = jnp.zeros_like(terms[0])
    for k, ref in enumerate((z1, z2, z3), 1):
        use = z < k if reverse else z >= k
        base = base + jnp.where(use, ref[...].astype(F32), 0.0)
    for k in range(n):
        to = lax.rem(y + k, n)
        total = base
        for j in range(n):
            source = lax.rem(y - j + n, n)
            use = source > to if reverse else source < to
            total = total + jnp.where(use, terms[j], 0.0)
        if k == 0:
            o_ref[...] = total
        else:
            (o1, o2, o3)[k - 1][...] = total.astype(BF)


def core_body(reverse, w_ref, s_ref, r_ref, p0, p1, p2, p3, mine_ref, give_ref):
    y, c = w_ref[6], w_ref[7]
    n = s_ref.shape[1]
    first = c == (1 if reverse else 0)
    for j, p in enumerate((p0, p1, p2, p3)):
        at = lax.rem(y - j + n, n)
        base = p[...].astype(F32)
        mine_ref[at] = (base + jnp.where(first, 0.0, r_ref[at].astype(F32))).astype(BF)
        give_ref[at] = (base + jnp.where(first, s_ref[c, at].astype(F32), 0.0)).astype(BF)


def give_to(x, axis, by):
    n = lax.axis_size(axis)
    return lax.ppermute(x, axis, [(d, (d + by) % n) for d in range(n)])


def carry(state, where, core, reverse, fill_row, fill_plane, fill_core):
    heads, d, e = state.shape
    n = lax.axis_size("y")
    rows = heads * d // (2 * n)
    parts = state.reshape(2, n, rows, e)
    give = lax.dynamic_index_in_dim(parts, 1 - core, 0, False)
    other = give_to(give, "c", 1)
    one = jax.ShapeDtypeStruct((rows, e), F32)
    low = jax.ShapeDtypeStruct((rows, e), BF)
    half = jax.ShapeDtypeStruct((n, rows, e), BF)
    own, *out = small_call(chip_body, where, [parts, other], [one] + [low] * (n - 1))
    terms = [own] + [give_to(x, "y", k) for k, x in enumerate(out, 1)]
    filled_row = fill_row(out)
    terms = after(terms, filled_row)
    (row,) = small_call(row_body, where, terms, [low])
    rows_before = [give_to(row, "z", k) for k in range(1, n)]
    filled_plane = fill_plane(row, filled_row)
    rows_before = after(rows_before, filled_plane)
    own, *out = small_call(
        functools.partial(plane_body, reverse), where, terms + rows_before, [one] + [low] * (n - 1)
    )
    sums = [own] + [give_to(x, "y", k) for k, x in enumerate(out, 1)]
    filled_core = fill_core(out, filled_plane)
    mine, give = small_call(
        functools.partial(core_body, reverse), where, [parts, other] + sums, [half] * 2
    )
    filled_core = after(filled_core, give)
    got = give_to(give, "c", 1)
    shape = (heads // 2, d, e)
    return (mine.reshape(shape), got.reshape(shape)), filled_row, filled_plane, filled_core


def after(x, *others):
    return lax.optimization_barrier((x, others))[0]


def scores_body(q_ref, k_ref, v_ref, w_ref, o_ref):
    keep = causal(q_ref.shape[0])
    for h in range(HC):
        w = jnp.where(keep, mm(head(q_ref, h), head(k_ref, h), 1, 1), 0.0).astype(BF)
        w_ref[h] = w
        o_ref[:, h * HD : (h + 1) * HD] = mm(w, head(v_ref, h), 1, 0)


def local_scores(q, k, v):
    t, f = q.shape
    w = f // CH
    blk = pl.BlockSpec((t, w), lambda g: (0, g))
    return pl.pallas_call(
        scores_body,
        grid=(CH,),
        in_specs=[blk, blk, blk],
        out_specs=[pl.BlockSpec((HC, t, t), lambda g: (g, 0, 0)), blk],
        out_shape=[
            jax.ShapeDtypeStruct((CH * HC, t, t), BF),
            jax.ShapeDtypeStruct((t, f), F32),
        ],
        cost_estimate=cost(4 * t * t * f, 14 * t * f),
        compiler_params=pltpu.CompilerParams(vmem_limit_bytes=12 << 20),
        name="local_scores",
    )(q, k, v)


def pick(w_ref, chunk, m_ref, t_ref, h):
    return jnp.where(lax.div(chunk, CH // 2) == w_ref[7], m_ref[h], t_ref[h])


def attend_body(w_ref, q_ref, o_ref, m_ref, t_ref, g_ref, *refs):
    n_refs, a_ref = refs[:-1], refs[-1]
    g = pl.program_id(0)
    for h in range(HC):
        cols = slice(h * HD, (h + 1) * HD)
        state = pick(w_ref, w_ref[g], m_ref, t_ref, h)
        a = o_ref[:, cols] + mm(head(q_ref, h), state, 1, 0)
        a_ref[0, :, cols] = a
        inv = lax.rsqrt(jnp.mean(a * a, axis=-1, keepdims=True) + EPSILON)
        normed = (a * inv * g_ref[:, cols]).astype(BF)
        for k in range(CH):

            @pl.when(g == k)
            def _(k=k, normed=normed, cols=cols):
                n_refs[k][:, cols] = normed


def attend(where, q, out, carried, gain):
    t, f = q.shape
    w = f // CH
    blk = pl.BlockSpec((t, w), lambda g, i: (0, i[g]))
    st = pl.BlockSpec((HC, HD, HD), lambda g, i: (lax.rem(i[g], CH // 2), 0, 0))
    return pl.pallas_call(
        attend_body,
        grid_spec=pltpu.PrefetchScalarGridSpec(
            num_scalar_prefetch=1,
            grid=(CH,),
            in_specs=[blk, blk, st, st, pl.BlockSpec((1, w), lambda g, i: (0, i[g]))],
            out_specs=[pl.BlockSpec((t, w), lambda g, i: (0, 0))] * CH
            + [pl.BlockSpec((1, t, w), lambda g, i: (g, 0, 0))],
        ),
        out_shape=[jax.ShapeDtypeStruct((t, w), BF)] * CH
        + [jax.ShapeDtypeStruct((CH, t, w), F32)],
        cost_estimate=cost(2 * t * f * HD, 12 * t * f),
        compiler_params=pltpu.CompilerParams(vmem_limit_bytes=12 << 20),
        name="attend",
    )(where, q, out, *carried, gain)


def grad_attn_body(i_ref, q_ref, a_ref, gn_ref, g_ref, go_ref, w_ref, ga_ref, lg_ref):
    rows = w_ref.shape[0] * w_ref.shape[2]

    def finish(gn):
        for h in range(HC):
            cols = slice(h * HD, (h + 1) * HD)
            a = a_ref[0, :, cols]
            inv = lax.rsqrt(jnp.mean(a * a, axis=-1, keepdims=True) + EPSILON)
            unit = a * inv
            gu = gn[:, cols] * g_ref[:, cols]
            ga = inv * (gu - unit * jnp.mean(gu * unit, axis=-1, keepdims=True))
            ga = ga.astype(BF)
            ga_ref[0, :, cols] = ga
            lg_ref[h] = mm(head(q_ref, h), ga, 0, 0).astype(BF)

    @pl.when(pl.program_id(0) == 0)
    def _():
        finish(gn_ref[...])

    @pl.when(pl.program_id(0) > 0)
    def _():
        finish(mm(go_ref[...], w_ref[:, 0].reshape(rows, w_ref.shape[3]), 1, 1))


def grad_attn(order, q, attended, gn, gain, grad_rows, gathered):
    t, f = q.shape
    w = f // CH
    n, _, r, d = gathered.shape
    return pl.pallas_call(
        grad_attn_body,
        grid_spec=pltpu.PrefetchScalarGridSpec(
            num_scalar_prefetch=1,
            grid=(CH,),
            in_specs=[
                pl.BlockSpec((t, w), lambda g, i: (0, i[g])),
                pl.BlockSpec((1, t, w), lambda g, i: (g, 0, 0)),
                pl.BlockSpec((t, w), lambda g, i: (0, 0)),
                pl.BlockSpec((1, w), lambda g, i: (0, i[g])),
                pl.BlockSpec((t, d), lambda g, i: (0, 0)),
                pl.BlockSpec((n, 1, r, d), lambda g, i: (0, jnp.maximum(g - 1, 0), 0, 0)),
            ],
            out_specs=[
                pl.BlockSpec((1, t, w), lambda g, i: (g, 0, 0)),
                pl.BlockSpec((HC, HD, HD), lambda g, i: (g, 0, 0)),
            ],
        ),
        out_shape=[
            jax.ShapeDtypeStruct((CH, t, w), BF),
            jax.ShapeDtypeStruct((CH * HC, HD, HD), BF),
        ],
        cost_estimate=cost(2 * t * f * HD + 6 * t * w * d, 12 * t * f + 6 * w * d),
        compiler_params=pltpu.CompilerParams(vmem_limit_bytes=20 << 20),
        name="grad_attn",
    )(order, q, attended, gn, gain, grad_rows, gathered)


def grads_body(i_ref, q_ref, k_ref, v_ref, w_ref, ga_ref, m_ref, t_ref, gq_ref, gk_ref, gv_ref):
    chunk = i_ref[pl.program_id(0)]
    keep = causal(q_ref.shape[0])
    for h in range(HC):
        cols = slice(h * HD, (h + 1) * HD)
        ga = ga_ref[0, :, cols]
        gs = jnp.where(keep, mm(ga, head(v_ref, h), 1, 1), 0.0).astype(BF)
        gq = mm(gs, head(k_ref, h), 1, 0) + mm(ga, pick(i_ref, chunk, m_ref, t_ref, h), 1, 1)
        gq_ref[:, cols] = gq.astype(BF)
        gk_ref[0, :, cols] = mm(gs, head(q_ref, h), 0, 0)
        gv_ref[0, :, cols] = mm(w_ref[h], ga, 0, 0)


def local_grads(order, q, k, v, weights, ga, carried):
    t, f = q.shape
    w = f // CH
    nat = pl.BlockSpec((t, w), lambda g, i: (0, i[g]))
    chunk = pl.BlockSpec((1, t, w), lambda g, i: (g, 0, 0))
    return pl.pallas_call(
        grads_body,
        grid_spec=pltpu.PrefetchScalarGridSpec(
            num_scalar_prefetch=1,
            grid=(CH,),
            in_specs=[
                nat,
                nat,
                nat,
                pl.BlockSpec((HC, t, t), lambda g, i: (i[g], 0, 0)),
                chunk,
            ]
            + [pl.BlockSpec((HC, HD, HD), lambda g, i: (lax.rem(i[g], CH // 2), 0, 0))] * 2,
            out_specs=[nat, chunk, chunk],
        ),
        out_shape=[
            jax.ShapeDtypeStruct((t, f), BF),
            jax.ShapeDtypeStruct((CH, t, w), F32),
            jax.ShapeDtypeStruct((CH, t, w), F32),
        ],
        cost_estimate=cost(8 * t * t * f, 24 * t * f),
        compiler_params=pltpu.CompilerParams(vmem_limit_bytes=20 << 20),
        name="local_grads",
    )(order, q, k, v, weights, ga, *carried)


def later_body(i_ref, k_ref, v_ref, m_ref, t_ref, pk_ref, pv_ref, gk_ref, gv_ref):
    for h in range(HC):
        cols = slice(h * HD, (h + 1) * HD)
        state = pick(i_ref, pl.program_id(0), m_ref, t_ref, h)
        gk = pk_ref[0, :, cols] + mm(head(v_ref, h), state, 1, 1)
        gv = pv_ref[0, :, cols] + mm(head(k_ref, h), state, 1, 0)
        gk_ref[:, cols] = gk.astype(BF)
        gv_ref[:, cols] = gv.astype(BF)


def later_grads(order, k, v, later, pk, pv):
    t, f = k.shape
    w = f // CH
    nat = pl.BlockSpec((t, w), lambda g, i: (0, i[g]))
    chunk = pl.BlockSpec((1, t, w), lambda g, i: (g, 0, 0))
    return pl.pallas_call(
        later_body,
        grid_spec=pltpu.PrefetchScalarGridSpec(
            num_scalar_prefetch=1,
            grid=(CH,),
            in_specs=[
                nat,
                nat,
                pl.BlockSpec((HC, HD, HD), lambda g, i: (lax.rem(g, CH // 2), 0, 0)),
                pl.BlockSpec((HC, HD, HD), lambda g, i: (lax.rem(g, CH // 2), 0, 0)),
                chunk,
                chunk,
            ],
            out_specs=[nat, nat],
        ),
        out_shape=[jax.ShapeDtypeStruct((t, f), BF)] * 2,
        cost_estimate=cost(4 * t * f * HD, 16 * t * f),
        compiler_params=pltpu.CompilerParams(vmem_limit_bytes=12 << 20),
        name="later_grads",
    )(order, k, v, *later, pk, pv)


def layer_body(n0, n1, n2, n3, own_ref, w_ref, o_ref):
    normed = (n0, n1, n2, n3)
    total = mm(n0[...], own_ref[...], 1, 0)
    for k in range(1, CH):
        block = w_ref[:, k - 1].reshape(own_ref.shape)
        total = total + mm(normed[k][...], block, 1, 0)
    o_ref[...] = total.astype(BF)


def layer_rows(normed, own, gathered):
    t, w = normed[0].shape
    n, c, r, d = gathered.shape
    tile = 1024
    return pl.pallas_call(
        layer_body,
        grid=(d // tile,),
        in_specs=[pl.BlockSpec((t, w), lambda g: (0, 0))] * CH
        + [
            pl.BlockSpec((w, tile), lambda g: (0, g)),
            pl.BlockSpec((n, c, r, tile), lambda g: (0, 0, 0, g)),
        ],
        out_specs=pl.BlockSpec((t, tile), lambda g: (0, g)),
        out_shape=jax.ShapeDtypeStruct((t, d), BF),
        cost_estimate=cost(2 * t * CH * w * d, 2 * (CH * w * d + CH * t * w + t * d)),
        compiler_params=pltpu.CompilerParams(vmem_limit_bytes=20 << 20),
        name="layer_rows",
    )(*normed, own, gathered)


def weight_total(nt, g0_ref, g1_ref, fa_ref, fb_ref, g3_ref):
    total = mm(nt[0], g0_ref[...], 1, 0) + mm(nt[1], g1_ref[...], 1, 0)
    total = total + mm(nt[2], jnp.concatenate([fa_ref[...], fb_ref[...]], axis=0), 1, 0)
    return total + mm(nt[3], g3_ref[...], 1, 0)


def give_body(i_ref, n0, n1, n2, n3, *rest):
    *grads, o_ref, nt_ref = rest

    @pl.when(pl.program_id(0) == 0)
    def _():
        for s, n in enumerate((n0, n1, n2, n3)):
            nt_ref[s] = n[...].T

    o_ref[...] = weight_total(nt_ref, *grads).astype(BF)


def keep_body(i_ref, nt_ref, extra_ref, *rest):
    *grads, o_ref = rest
    o_ref[...] = (weight_total(nt_ref, *grads) + extra_ref[...].astype(F32)).astype(BF)


def weight_half(body, half, rows, grads_all, nt_out):
    t, d = grads_all[0].shape
    w = rows[0].shape[1]
    tile = 512
    steps = d // 2 // tile
    own = pl.BlockSpec((w, tile), lambda g, i: (0, g))
    whole = pl.BlockSpec((t, w), lambda g, i: (0, 0))
    turned = pl.BlockSpec((CH, w, t), lambda g, i: (0, 0, 0))
    out = jax.ShapeDtypeStruct((w, d // 2), BF)
    return pl.pallas_call(
        body,
        grid_spec=pltpu.PrefetchScalarGridSpec(
            num_scalar_prefetch=1,
            grid=(steps,),
            in_specs=([whole] * CH if nt_out else [turned, own])
            + [
                pl.BlockSpec((x.shape[0], tile), lambda g, i: (0, i[0] * steps + g))
                for x in grads_all
            ],
            out_specs=[own, turned] if nt_out else own,
        ),
        out_shape=[out, jax.ShapeDtypeStruct((CH, w, t), BF)] if nt_out else out,
        cost_estimate=cost(CH * t * w * d, CH * t * d + 2 * CH * t * w + w * d),
        compiler_params=pltpu.CompilerParams(vmem_limit_bytes=14 << 20),
        name="weight_half",
    )(half, *rows, *grads_all)


def sum_body(scale, s_ref, o_ref):
    total = s_ref[0].astype(F32)
    for step in range(1, s_ref.shape[0]):
        total = total + s_ref[step].astype(F32)
    o_ref[...] = total * scale


def sum_parts(parts, scale):
    _, r, w = parts.shape
    return pl.pallas_call(
        functools.partial(sum_body, scale),
        out_shape=jax.ShapeDtypeStruct((r, w), F32),
        cost_estimate=cost(parts.size, 2 * parts.size),
        compiler_params=pltpu.CompilerParams(vmem_limit_bytes=6 << 20),
        name="sum_parts",
    )(parts)


def shift(x, axis, by):
    n = lax.axis_size(axis)
    return lax.ppermute(x, axis, [((d + by) % n, d) for d in range(n)])


def layer(queries, keys, values, gain, out_weight, grad_out):
    tok_rows, feat_width = queries.shape[1:]
    model_width = grad_out.shape[2]
    q = queries.reshape(tok_rows, feat_width)
    k = keys.reshape(tok_rows, feat_width)
    v = values.reshape(tok_rows, feat_width)
    grad_rows = grad_out.reshape(tok_rows, model_width)
    gain_row = gain.reshape(1, feat_width)
    seqs = lax.axis_size("x")
    blocks_n = lax.axis_size(CTX)
    at_x = lax.axis_index("x")
    at_ctx = lax.axis_index(CTX)
    at_core = lax.axis_index("c")
    places = [at_x, lax.axis_index("z"), lax.axis_index("y"), at_core]
    order = [(at_x + n) % CH for n in range(CH)]
    where = jnp.stack(order + places).astype(jnp.int32)
    mine = at_core.reshape(1).astype(jnp.int32)
    others = 1 - mine

    piece = out_weight.shape[0] // blocks_n
    own_piece = lax.dynamic_slice_in_dim(out_weight, at_ctx * piece, piece, 0)
    pieces = [shift(own_piece, "x", by) for by in range(1, CH)]
    state = local_state(k, v)
    pieces, sent_rows, q_next = lax.optimization_barrier((pieces, grad_rows, q, state))[:3]
    gathered = lax.all_gather(jnp.concatenate(pieces, axis=0), CTX, axis=0, tiled=True)
    gathered = gathered.reshape(blocks_n, CH - 1, piece, model_width)
    gathered = pltpu.with_memory_space_constraint(gathered, pltpu.HBM)
    own_weight = pltpu.with_memory_space_constraint(out_weight, pltpu.HBM)

    right = shift(sent_rows, "x", 1)
    left = shift(sent_rows, "x", 3)
    half_rows = tok_rows // 2
    carried, (weights, local_out), gn, _ = carry(
        state,
        where,
        at_core,
        False,
        lambda sent: local_scores(after(q_next, sent), k, v),
        lambda sent, done: mm(after(sent_rows, sent, done), out_weight, 1, 1),
        lambda sent, done: (),
    )
    *normed, attended = attend(where, q, local_out, carried, gain_row)

    normed_all = [normed[0]] + [give_to(normed[n], "x", n) for n in range(1, CH)]
    right, left, attended = lax.optimization_barrier((right, left, attended))
    far_a = shift(right[:half_rows], "x", 1)
    far_b = shift(left[half_rows:], "x", 3)

    ga, lg = grad_attn(where, q, attended, gn, gain_row, grad_rows, gathered)
    half_cols = model_width // 2
    grads_all = [grad_rows, left, far_a, far_b, right]

    def first_half(sent, done):
        rows = after(normed_all, sent, done)
        return weight_half(give_body, others, rows, grads_all, True)

    def second_half(sent, done):
        for_partner, turned = done
        extra = give_to(for_partner, "c", 1)
        return weight_half(keep_body, mine, [after(turned, sent), extra], grads_all, False)

    later, (grad_query, pk, pv), _, partial = carry(
        lg,
        where,
        at_core,
        True,
        lambda sent: local_grads(where, q, k, v, weights, after(ga, sent), carried),
        first_half,
        second_half,
    )
    layer_out = layer_rows(after(normed, partial, later), own_weight, gathered)
    grad_key, grad_value = later_grads(where, k, v, later, pk, pv)

    chips = blocks_n // 2
    rows = partial.shape[0] // chips
    parts = lax.all_to_all(
        partial.reshape(chips, rows, half_cols), ("z", "y"), 0, 0, tiled=True
    )
    token_count = seqs * blocks_n * tok_rows
    parts = after(parts, layer_out, grad_key)
    summed = sum_parts(parts, 1.0 / math.sqrt(token_count))
    out_rows = rows // 2
    keep = lax.dynamic_slice_in_dim(summed, at_core * out_rows, out_rows, 0)
    give = lax.dynamic_slice_in_dim(summed, (1 - at_core) * out_rows, out_rows, 0)
    got = shift(give, "c", 1)
    first = at_core == 0
    grad_weight = jnp.concatenate(
        [jnp.where(first, keep, got), jnp.where(first, got, keep)], axis=1
    )
    out_shape = (1, tok_rows, feat_width)
    return (
        layer_out.reshape(1, tok_rows, model_width),
        grad_query.reshape(out_shape),
        grad_key.reshape(out_shape),
        grad_value.reshape(out_shape),
        grad_weight,
    )


def solution(mesh):
    mesh = Mesh(mesh.devices.reshape(4, 4, 4, 2), ("x",) + CTX)
    tokens = P("x", CTX, None)
    in_specs = (tokens, tokens, tokens, P(), P("x", None), tokens)
    out_specs = (tokens, tokens, tokens, tokens, P(("x",) + CTX, None))
    return jax.shard_map(layer, mesh=mesh, in_specs=in_specs, out_specs=out_specs, check_vma=False)
```

```python
import functools
import math

import jax
import jax.numpy as jnp
from jax import lax
from jax.experimental import pallas as pl
from jax.experimental.pallas import tpu as pltpu
from jax.sharding import Mesh, PartitionSpec as P

HD = 128
EPSILON = 1e-06
BF = jnp.bfloat16
F32 = jnp.float32
CTX = ("z", "y", "c")
CH = 4
HC = 4


def mm(a, b, ca, cb):
    return lax.dot_general(a, b, (((ca,), (cb,)), ((), ())), preferred_element_type=F32)


def cost(flops, nbytes):
    return pl.CostEstimate(flops=flops, bytes_accessed=nbytes, transcendentals=0)


def head(ref, h):
    return ref[:, h * HD : (h + 1) * HD]


def causal(n):
    return lax.broadcasted_iota(jnp.int32, (n, n), 0) >= lax.broadcasted_iota(
        jnp.int32, (n, n), 1
    )


def state_body(k_ref, v_ref, s_ref):
    for h in range(HC):
        s_ref[h] = mm(head(k_ref, h), head(v_ref, h), 0, 0).astype(BF)


def local_state(k, v):
    t, f = k.shape
    w = f // CH
    blk = pl.BlockSpec((t, w), lambda g: (0, g))
    return pl.pallas_call(
        state_body,
        grid=(CH,),
        in_specs=[blk, blk],
        out_specs=pl.BlockSpec((HC, HD, HD), lambda g: (g, 0, 0)),
        out_shape=jax.ShapeDtypeStruct((CH * HC, HD, HD), BF),
        cost_estimate=cost(2 * t * f * HD, 4 * t * f),
        compiler_params=pltpu.CompilerParams(vmem_limit_bytes=6 << 20),
        name="local_state",
    )(k, v)


def small_call(body, where, args, outs):
    return pl.pallas_call(
        body,
        in_specs=[pl.BlockSpec(memory_space=pltpu.SMEM)]
        + [pl.BlockSpec(memory_space=pltpu.VMEM)] * len(args),
        out_specs=[pl.BlockSpec(memory_space=pltpu.VMEM)] * len(outs),
        out_shape=outs,
        compiler_params=pltpu.CompilerParams(vmem_limit_bytes=6 << 20),
        cost_estimate=cost(1 << 18, 1 << 20),
    )(where, *args)


def chip_body(w_ref, s_ref, r_ref, own_ref, *out_refs):
    y, c = w_ref[6], w_ref[7]
    n = s_ref.shape[1]
    for k in range(n):
        at = lax.rem(y + k, n)
        part = s_ref[c, at].astype(F32) + r_ref[at].astype(F32)
        if k == 0:
            own_ref[...] = part
        else:
            out_refs[k - 1][...] = part.astype(BF)


def row_body(w_ref, own_ref, *refs):
    total = own_ref[...]
    for ref in refs[:-1]:
        total = total + ref[...].astype(F32)
    refs[-1][...] = total.astype(BF)


def plane_body(reverse, w_ref, own_ref, t1, t2, t3, z1, z2, z3, o_ref, o1, o2, o3):
    z, y = w_ref[5], w_ref[6]
    terms = [own_ref[...]] + [t[...].astype(F32) for t in (t1, t2, t3)]
    n = len(terms)
    base = jnp.zeros_like(terms[0])
    for k, ref in enumerate((z1, z2, z3), 1):
        use = z < k if reverse else z >= k
        base = base + jnp.where(use, ref[...].astype(F32), 0.0)
    for k in range(n):
        to = lax.rem(y + k, n)
        total = base
        for j in range(n):
            source = lax.rem(y - j + n, n)
            use = source > to if reverse else source < to
            total = total + jnp.where(use, terms[j], 0.0)
        if k == 0:
            o_ref[...] = total
        else:
            (o1, o2, o3)[k - 1][...] = total.astype(BF)


def core_body(reverse, w_ref, s_ref, r_ref, p0, p1, p2, p3, mine_ref, give_ref):
    y, c = w_ref[6], w_ref[7]
    n = s_ref.shape[1]
    first = c == (1 if reverse else 0)
    for j, p in enumerate((p0, p1, p2, p3)):
        at = lax.rem(y - j + n, n)
        base = p[...].astype(F32)
        mine_ref[at] = (base + jnp.where(first, 0.0, r_ref[at].astype(F32))).astype(BF)
        give_ref[at] = (base + jnp.where(first, s_ref[c, at].astype(F32), 0.0)).astype(BF)


def partner(x, axis, bits):
    return lax.ppermute(x, axis, [(d, d ^ bits) for d in range(lax.axis_size(axis))])


def give_to(x, axis, by):
    n = lax.axis_size(axis)
    return lax.ppermute(x, axis, [(d, (d + by) % n) for d in range(n)])


def carry(state, where, core, reverse, fill_row, fill_plane, fill_core):
    heads, d, e = state.shape
    n = lax.axis_size("y")
    rows = heads * d // (2 * n)
    parts = state.reshape(2, n, rows, e)
    give = lax.dynamic_index_in_dim(parts, 1 - core, 0, False)
    other = give_to(give, "c", 1)
    one = jax.ShapeDtypeStruct((rows, e), F32)
    low = jax.ShapeDtypeStruct((rows, e), BF)
    half = jax.ShapeDtypeStruct((n, rows, e), BF)
    own, *out = small_call(chip_body, where, [parts, other], [one] + [low] * (n - 1))
    terms = [own] + [give_to(x, "y", k) for k, x in enumerate(out, 1)]
    filled_row = fill_row(out)
    terms = after(terms, filled_row)
    (row,) = small_call(row_body, where, terms, [low])
    rows_before = [give_to(row, "z", k) for k in range(1, n)]
    filled_plane = fill_plane(row, filled_row)
    rows_before = after(rows_before, filled_plane)
    own, *out = small_call(
        functools.partial(plane_body, reverse),
        where,
        terms + rows_before,
        [one] + [low] * (n - 1),
    )
    sums = [own] + [give_to(x, "y", k) for k, x in enumerate(out, 1)]
    filled_core = fill_core(out, filled_plane)
    mine, give = small_call(
        functools.partial(core_body, reverse), where, [parts, other] + sums, [half] * 2
    )
    filled_core = after(filled_core, give)
    got = give_to(give, "c", 1)
    shape = (heads // 2, d, e)
    return (mine.reshape(shape), got.reshape(shape)), filled_row, filled_plane, filled_core


def after(x, *others):
    return lax.optimization_barrier((x, others))[0]


def scores_body(q_ref, k_ref, v_ref, w_ref, o_ref):
    keep = causal(q_ref.shape[0])
    for h in range(HC):
        w = jnp.where(keep, mm(head(q_ref, h), head(k_ref, h), 1, 1), 0.0).astype(BF)
        w_ref[h] = w
        o_ref[:, h * HD : (h + 1) * HD] = mm(w, head(v_ref, h), 1, 0)


def local_scores(q, k, v):
    t, f = q.shape
    w = f // CH
    blk = pl.BlockSpec((t, w), lambda g: (0, g))
    return pl.pallas_call(
        scores_body,
        grid=(CH,),
        in_specs=[blk, blk, blk],
        out_specs=[pl.BlockSpec((HC, t, t), lambda g: (g, 0, 0)), blk],
        out_shape=[
            jax.ShapeDtypeStruct((CH * HC, t, t), BF),
            jax.ShapeDtypeStruct((t, f), F32),
        ],
        cost_estimate=cost(4 * t * t * f, 14 * t * f),
        compiler_params=pltpu.CompilerParams(vmem_limit_bytes=12 << 20),
        name="local_scores",
    )(q, k, v)


def pick(w_ref, chunk, m_ref, t_ref, h):
    return jnp.where(lax.div(chunk, CH // 2) == w_ref[7], m_ref[h], t_ref[h])


def attend_body(w_ref, q_ref, o_ref, m_ref, t_ref, g_ref, near_ref, far_ref, a_ref):
    g = pl.program_id(0)
    normed = []
    for h in range(HC):
        cols = slice(h * HD, (h + 1) * HD)
        state = pick(w_ref, w_ref[g], m_ref, t_ref, h)
        a = o_ref[:, cols] + mm(head(q_ref, h), state, 1, 0)
        a_ref[0, :, cols] = a
        inv = lax.rsqrt(jnp.mean(a * a, axis=-1, keepdims=True) + EPSILON)
        normed.append((a * inv * g_ref[:, cols]).astype(BF))
    normed = jnp.concatenate(normed, axis=1)

    @pl.when(g < CH // 2)
    def _():
        near_ref[...] = normed

    @pl.when(g >= CH // 2)
    def _():
        far_ref[...] = normed


def attend(where, q, out, carried, gain):
    t, f = q.shape
    w = f // CH
    two = CH // 2
    blk = pl.BlockSpec((t, w), lambda g, i: (0, i[g]))
    st = pl.BlockSpec((HC, HD, HD), lambda g, i: (lax.rem(i[g], two), 0, 0))
    return pl.pallas_call(
        attend_body,
        grid_spec=pltpu.PrefetchScalarGridSpec(
            num_scalar_prefetch=1,
            grid=(CH,),
            in_specs=[blk, blk, st, st, pl.BlockSpec((1, w), lambda g, i: (0, i[g]))],
            out_specs=[
                pl.BlockSpec((t, w), lambda g, i: (0, jnp.minimum(g, two - 1))),
                pl.BlockSpec((t, w), lambda g, i: (0, jnp.maximum(g - two, 0))),
                pl.BlockSpec((1, t, w), lambda g, i: (i[g], 0, 0)),
            ],
        ),
        out_shape=[jax.ShapeDtypeStruct((t, two * w), BF)] * 2
        + [jax.ShapeDtypeStruct((CH, t, w), F32)],
        cost_estimate=cost(2 * t * f * HD, 12 * t * f),
        compiler_params=pltpu.CompilerParams(vmem_limit_bytes=12 << 20),
        name="attend",
    )(where, q, out, *carried, gain)


def grad_attn_body(i_ref, q_ref, a_ref, gn_ref, g_ref, go_ref, w_ref, ga_ref, lg_ref):
    rows = w_ref.shape[0] * w_ref.shape[2]

    def finish(gn):
        for h in range(HC):
            cols = slice(h * HD, (h + 1) * HD)
            a = a_ref[0, :, cols]
            inv = lax.rsqrt(jnp.mean(a * a, axis=-1, keepdims=True) + EPSILON)
            unit = a * inv
            gu = gn[:, cols] * g_ref[:, cols]
            ga = inv * (gu - unit * jnp.mean(gu * unit, axis=-1, keepdims=True))
            ga = ga.astype(BF)
            ga_ref[0, :, cols] = ga
            lg_ref[h] = mm(head(q_ref, h), ga, 0, 0).astype(BF)

    @pl.when(pl.program_id(0) == 0)
    def _():
        finish(gn_ref[...])

    @pl.when(pl.program_id(0) > 0)
    def _():
        finish(mm(go_ref[...], w_ref[:, 0].reshape(rows, w_ref.shape[3]), 1, 1))


def grad_attn(order, q, attended, gn, gain, grad_rows, gathered):
    t, f = q.shape
    w = f // CH
    n, _, r, d = gathered.shape
    return pl.pallas_call(
        grad_attn_body,
        grid_spec=pltpu.PrefetchScalarGridSpec(
            num_scalar_prefetch=1,
            grid=(CH,),
            in_specs=[
                pl.BlockSpec((t, w), lambda g, i: (0, i[g])),
                pl.BlockSpec((1, t, w), lambda g, i: (i[g], 0, 0)),
                pl.BlockSpec((t, w), lambda g, i: (0, 0)),
                pl.BlockSpec((1, w), lambda g, i: (0, i[g])),
                pl.BlockSpec((t, d), lambda g, i: (0, 0)),
                pl.BlockSpec((n, 1, r, d), lambda g, i: (0, jnp.maximum(g - 1, 0), 0, 0)),
            ],
            out_specs=[
                pl.BlockSpec((1, t, w), lambda g, i: (g, 0, 0)),
                pl.BlockSpec((HC, HD, HD), lambda g, i: (g, 0, 0)),
            ],
        ),
        out_shape=[
            jax.ShapeDtypeStruct((CH, t, w), BF),
            jax.ShapeDtypeStruct((CH * HC, HD, HD), BF),
        ],
        cost_estimate=cost(2 * t * f * HD + 6 * t * w * d, 12 * t * f + 6 * w * d),
        compiler_params=pltpu.CompilerParams(vmem_limit_bytes=20 << 20),
        name="grad_attn",
    )(order, q, attended, gn, gain, grad_rows, gathered)


def grads_body(i_ref, q_ref, k_ref, v_ref, w_ref, ga_ref, m_ref, t_ref, gq_ref, gk_ref, gv_ref):
    chunk = i_ref[pl.program_id(0)]
    keep = causal(q_ref.shape[0])
    for h in range(HC):
        cols = slice(h * HD, (h + 1) * HD)
        ga = ga_ref[0, :, cols]
        gs = jnp.where(keep, mm(ga, head(v_ref, h), 1, 1), 0.0).astype(BF)
        gq = mm(gs, head(k_ref, h), 1, 0) + mm(ga, pick(i_ref, chunk, m_ref, t_ref, h), 1, 1)
        gq_ref[:, cols] = gq.astype(BF)
        gk_ref[0, :, cols] = mm(gs, head(q_ref, h), 0, 0)
        gv_ref[0, :, cols] = mm(w_ref[h], ga, 0, 0)


def local_grads(order, q, k, v, weights, ga, carried):
    t, f = q.shape
    w = f // CH
    nat = pl.BlockSpec((t, w), lambda g, i: (0, i[g]))
    chunk = pl.BlockSpec((1, t, w), lambda g, i: (g, 0, 0))
    return pl.pallas_call(
        grads_body,
        grid_spec=pltpu.PrefetchScalarGridSpec(
            num_scalar_prefetch=1,
            grid=(CH,),
            in_specs=[
                nat,
                nat,
                nat,
                pl.BlockSpec((HC, t, t), lambda g, i: (i[g], 0, 0)),
                chunk,
            ]
            + [pl.BlockSpec((HC, HD, HD), lambda g, i: (lax.rem(i[g], CH // 2), 0, 0))] * 2,
            out_specs=[nat, chunk, chunk],
        ),
        out_shape=[
            jax.ShapeDtypeStruct((t, f), BF),
            jax.ShapeDtypeStruct((CH, t, w), F32),
            jax.ShapeDtypeStruct((CH, t, w), F32),
        ],
        cost_estimate=cost(8 * t * t * f, 24 * t * f),
        compiler_params=pltpu.CompilerParams(vmem_limit_bytes=20 << 20),
        name="local_grads",
    )(order, q, k, v, weights, ga, *carried)


def later_body(i_ref, k_ref, v_ref, m_ref, t_ref, pk_ref, pv_ref, gk_ref, gv_ref):
    for h in range(HC):
        cols = slice(h * HD, (h + 1) * HD)
        state = pick(i_ref, pl.program_id(0), m_ref, t_ref, h)
        gk = pk_ref[0, :, cols] + mm(head(v_ref, h), state, 1, 1)
        gv = pv_ref[0, :, cols] + mm(head(k_ref, h), state, 1, 0)
        gk_ref[:, cols] = gk.astype(BF)
        gv_ref[:, cols] = gv.astype(BF)


def later_grads(order, k, v, later, pk, pv):
    t, f = k.shape
    w = f // CH
    nat = pl.BlockSpec((t, w), lambda g, i: (0, i[g]))
    chunk = pl.BlockSpec((1, t, w), lambda g, i: (g, 0, 0))
    return pl.pallas_call(
        later_body,
        grid_spec=pltpu.PrefetchScalarGridSpec(
            num_scalar_prefetch=1,
            grid=(CH,),
            in_specs=[
                nat,
                nat,
                pl.BlockSpec((HC, HD, HD), lambda g, i: (lax.rem(g, CH // 2), 0, 0)),
                pl.BlockSpec((HC, HD, HD), lambda g, i: (lax.rem(g, CH // 2), 0, 0)),
                chunk,
                chunk,
            ],
            out_specs=[nat, nat],
        ),
        out_shape=[jax.ShapeDtypeStruct((t, f), BF)] * 2,
        cost_estimate=cost(4 * t * f * HD, 16 * t * f),
        compiler_params=pltpu.CompilerParams(vmem_limit_bytes=12 << 20),
        name="later_grads",
    )(order, k, v, *later, pk, pv)


def layer_body(i_ref, near_ref, far_ref, own_ref, w_ref, o_ref):
    w = own_ref.shape[0]
    mine = lax.div(i_ref[4], CH // 2)
    total = None
    for k in range(CH):
        chunk = i_ref[k]
        cols = pl.ds(pl.multiple_of(lax.rem(chunk, CH // 2) * w, w), w)
        is_near = lax.div(chunk, CH // 2) == mine
        rows = jnp.where(is_near, near_ref[:, cols], far_ref[:, cols])
        block = own_ref[...] if k == 0 else w_ref[:, k - 1].reshape(own_ref.shape)
        part = mm(rows, block, 1, 0)
        total = part if total is None else total + part
    o_ref[...] = total.astype(BF)


def layer_rows(where, near, far, own, gathered):
    t = near.shape[0]
    w = own.shape[0]
    n, c, r, d = gathered.shape
    tile = 1024
    half = pl.BlockSpec(near.shape, lambda g, i: (0, 0))
    return pl.pallas_call(
        layer_body,
        grid_spec=pltpu.PrefetchScalarGridSpec(
            num_scalar_prefetch=1,
            grid=(d // tile,),
            in_specs=[
                half,
                half,
                pl.BlockSpec((w, tile), lambda g, i: (0, g)),
                pl.BlockSpec((n, c, r, tile), lambda g, i: (0, 0, 0, g)),
            ],
            out_specs=pl.BlockSpec((t, tile), lambda g, i: (0, g)),
        ),
        out_shape=jax.ShapeDtypeStruct((t, d), BF),
        cost_estimate=cost(2 * t * CH * w * d, 2 * (CH * w * d + CH * t * w + t * d)),
        compiler_params=pltpu.CompilerParams(vmem_limit_bytes=20 << 20),
        name="layer_rows",
    )(where, near, far, own, gathered)


def weight_total(nt, grads, o_ref, extra_ref):
    total = None
    for s, g in enumerate(grads):
        part = mm(nt[s], g[...], 1, 0)
        total = part if total is None else total + part
    chips, blocks, rows, w = o_ref.shape
    span = chips * rows
    for b in range(blocks):
        one = total[b * span : (b + 1) * span].reshape(chips, rows, w)
        if extra_ref is not None:
            one = one + extra_ref[:, b].astype(F32)
        o_ref[:, b] = one.astype(BF)


def give_body(i_ref, n0, n1, n2, n3, *rest):
    *grads, o_ref, nt_ref = rest

    @pl.when(pl.program_id(0) == 0)
    def _():
        for s, n in enumerate((n0, n1, n2, n3)):
            nt_ref[s] = n[...].T

    weight_total(nt_ref, grads, o_ref, None)


def keep_body(i_ref, nt_ref, extra_ref, *rest):
    *grads, o_ref = rest
    weight_total(nt_ref, grads, o_ref, extra_ref)


def weight_half(body, half, rows, grads_all, shape, nt_out):
    t, d = grads_all[0].shape
    w = rows[0].shape[1]
    tile = 256
    steps = d // 2 // tile
    own = pl.BlockSpec(shape[:-1] + (tile,), lambda g, i: (0, 0, 0, g))
    whole = pl.BlockSpec((t, w), lambda g, i: (0, 0))
    turned = pl.BlockSpec((CH, w, t), lambda g, i: (0, 0, 0))
    out = jax.ShapeDtypeStruct(shape, BF)
    cols = pl.BlockSpec((t, tile), lambda g, i: (0, i[0] * steps + g))
    return pl.pallas_call(
        body,
        grid_spec=pltpu.PrefetchScalarGridSpec(
            num_scalar_prefetch=1,
            grid=(steps,),
            in_specs=([whole] * CH if nt_out else [turned, own]) + [cols] * CH,
            out_specs=[own, turned] if nt_out else own,
        ),
        out_shape=[out, jax.ShapeDtypeStruct((CH, w, t), BF)] if nt_out else out,
        cost_estimate=cost(CH * t * w * d, 2 * CH * t * d + 2 * CH * t * w + w * d),
        compiler_params=pltpu.CompilerParams(vmem_limit_bytes=20 << 20),
        name="weight_half",
    )(half, *rows, *grads_all)


def sum_body(scale, w_ref, s_ref, keep_ref, x_ref, c_ref, xc_ref, total):
    acc = s_ref[0].astype(F32)
    for step in range(1, s_ref.shape[0]):
        acc = acc + s_ref[step].astype(F32)
    total[...] = acc * scale
    rows = keep_ref.shape[0]
    block, c = lax.rem(w_ref[4], 2), w_ref[7]
    mine = pl.ds(pl.multiple_of(c * rows, rows), rows)
    other = pl.ds(pl.multiple_of((1 - c) * rows, rows), rows)
    keep_ref[...] = total[block, mine]
    x_ref[...] = total[1 - block, mine]
    c_ref[...] = total[block, other]
    xc_ref[...] = total[1 - block, other]


def sum_parts(where, parts, scale):
    _, b, r, w = parts.shape
    return pl.pallas_call(
        functools.partial(sum_body, scale),
        in_specs=[
            pl.BlockSpec(memory_space=pltpu.SMEM),
            pl.BlockSpec(memory_space=pltpu.VMEM),
        ],
        out_specs=[pl.BlockSpec(memory_space=pltpu.VMEM)] * 4,
        out_shape=[jax.ShapeDtypeStruct((r // 2, w), F32)] * 4,
        scratch_shapes=[pltpu.VMEM((b, r, w), F32)],
        cost_estimate=cost(parts.size, 2 * parts.size),
        compiler_params=pltpu.CompilerParams(vmem_limit_bytes=8 << 20),
        name="sum_parts",
    )(where, parts)


def join_body(w_ref, own_ref, x_ref, c_ref, xc_ref, o_ref):
    block, c = lax.rem(w_ref[4], 2), w_ref[7]
    w = own_ref.shape[1]
    for ref, b, h in (
        (own_ref, block, c),
        (x_ref, 1 - block, c),
        (c_ref, block, 1 - c),
        (xc_ref, 1 - block, 1 - c),
    ):
        o_ref[:, pl.ds(pl.multiple_of((2 * b + h) * w, w), w)] = ref[...]


def shift(x, axis, by):
    n = lax.axis_size(axis)
    return lax.ppermute(x, axis, [((d + by) % n, d) for d in range(n)])


def layer(queries, keys, values, gain, out_weight, grad_out):
    tok_rows, feat_width = queries.shape[1:]
    model_width = grad_out.shape[2]
    q = queries.reshape(tok_rows, feat_width)
    k = keys.reshape(tok_rows, feat_width)
    v = values.reshape(tok_rows, feat_width)
    grad_rows = grad_out.reshape(tok_rows, model_width)
    gain_row = gain.reshape(1, feat_width)
    seqs = lax.axis_size("x")
    blocks_n = lax.axis_size(CTX)
    at_x = lax.axis_index("x")
    at_ctx = lax.axis_index(CTX)
    at_core = lax.axis_index("c")
    places = [at_x, lax.axis_index("z"), lax.axis_index("y"), at_core]
    order = [(at_x + n) % CH for n in range(CH)]
    where = jnp.stack(order + places).astype(jnp.int32)
    row_half = at_x // 2
    turns = [2 * row_half, 2 * row_half + 1, 2 - 2 * row_half, 3 - 2 * row_half]
    turns = jnp.stack(turns + places).astype(jnp.int32)
    mine = at_core.reshape(1).astype(jnp.int32)
    others = 1 - mine

    piece = out_weight.shape[0] // blocks_n
    own_piece = lax.dynamic_slice_in_dim(out_weight, at_ctx * piece, piece, 0)
    pieces = [shift(own_piece, "x", by) for by in range(1, CH)]
    state = local_state(k, v)
    pieces, sent_rows, q_next = lax.optimization_barrier((pieces, grad_rows, q, state))[:3]
    gathered = lax.all_gather(jnp.concatenate(pieces, axis=0), CTX, axis=0, tiled=True)
    gathered = gathered.reshape(blocks_n, CH - 1, piece, model_width)
    gathered = pltpu.with_memory_space_constraint(gathered, pltpu.HBM)
    own_weight = pltpu.with_memory_space_constraint(out_weight, pltpu.HBM)

    half_cols = model_width // 2
    side = at_x % 2
    near_cols = lax.dynamic_slice_in_dim(sent_rows, side * half_cols, half_cols, 1)
    far_cols = lax.dynamic_slice_in_dim(sent_rows, (1 - side) * half_cols, half_cols, 1)
    grads_all = [
        near_cols,
        partner(far_cols, "x", 1),
        partner(near_cols, "x", 2),
        partner(far_cols, "x", 3),
    ]

    carried, (weights, local_out), gn, _ = carry(
        state,
        where,
        at_core,
        False,
        lambda sent: local_scores(after(q_next, sent), k, v),
        lambda sent, done: mm(after(sent_rows, sent, done), out_weight, 1, 1),
        lambda sent, done: (),
    )
    near, far, attended = attend(turns, q, local_out, carried, gain_row)
    normed_all = [
        near,
        partner(near, "x", 1),
        partner(far, "x", 2),
        partner(far, "x", 3),
    ]
    attended = pltpu.with_memory_space_constraint(attended, pltpu.HBM)
    gn = pltpu.with_memory_space_constraint(gn, pltpu.HBM)

    ga, lg = grad_attn(where, q, attended, gn, gain_row, grad_rows, gathered)
    chips = blocks_n // 2
    shape = (chips, 2, out_weight.shape[0] // chips, half_cols // 2)

    def first_half(sent):
        rows = after(normed_all, sent)
        return weight_half(give_body, others, rows, grads_all, shape, True)

    def second_half(sent, done):
        for_partner, turned = done
        extra = give_to(for_partner, "c", 1)
        return weight_half(
            keep_body, mine, [after(turned, sent), extra], grads_all, shape, False
        )

    later, _, _, partial = carry(
        lg, where, at_core, True, first_half, second_half, lambda sent, done: done
    )
    ga = after(ga, partial)
    grad_query, pk, pv = local_grads(where, q, k, v, weights, ga, carried)
    layer_out = layer_rows(where, near, after(far, partial, later), own_weight, gathered)
    grad_key, grad_value = later_grads(where, k, v, later, pk, pv)

    parts = lax.all_to_all(partial, ("z", "y"), 0, 0, tiled=True)
    parts = after(parts, layer_out, grad_key)
    token_count = seqs * blocks_n * tok_rows
    own, to_x, to_c, to_both = sum_parts(where, parts, 1.0 / math.sqrt(token_count))
    both = lax.ppermute(to_both, ("x", "c"), [(d, d ^ 3) for d in range(2 * seqs)])
    (grad_weight,) = small_call(
        join_body,
        where,
        [own, partner(to_x, "x", 1), partner(to_c, "c", 1), both],
        [jax.ShapeDtypeStruct((own.shape[0], model_width), F32)],
    )
    out_shape = (1, tok_rows, feat_width)
    return (
        layer_out.reshape(1, tok_rows, model_width),
        grad_query.reshape(out_shape),
        grad_key.reshape(out_shape),
        grad_value.reshape(out_shape),
        grad_weight,
    )


def solution(mesh):
    mesh = Mesh(mesh.devices.reshape(4, 4, 4, 2), ("x",) + CTX)
    tokens = P("x", CTX, None)
    in_specs = (tokens, tokens, tokens, P(), P("x", None), tokens)
    out_specs = (tokens, tokens, tokens, tokens, P(("x",) + CTX, None))
    return jax.shard_map(layer, mesh=mesh, in_specs=in_specs, out_specs=out_specs, check_vma=False)
```

```python
import functools
import math

import jax
import jax.numpy as jnp
from jax import lax
from jax.experimental import pallas as pl
from jax.experimental.pallas import tpu as pltpu
from jax.sharding import Mesh, PartitionSpec as P

HD = 128
EPSILON = 1e-06
BF = jnp.bfloat16
F32 = jnp.float32
CTX = ("z", "y", "c")
CH = 4
HC = 4


def mm(a, b, ca, cb):
    return lax.dot_general(a, b, (((ca,), (cb,)), ((), ())), preferred_element_type=F32)


def cost(flops, nbytes):
    return pl.CostEstimate(flops=flops, bytes_accessed=nbytes, transcendentals=0)


def head(ref, h):
    return ref[:, h * HD : (h + 1) * HD]


def causal(n):
    return lax.broadcasted_iota(jnp.int32, (n, n), 0) >= lax.broadcasted_iota(
        jnp.int32, (n, n), 1
    )


def state_body(k_ref, v_ref, s_ref):
    for h in range(HC):
        s_ref[h] = mm(head(k_ref, h), head(v_ref, h), 0, 0).astype(BF)


def local_state(k, v):
    t, f = k.shape
    w = f // CH
    blk = pl.BlockSpec((t, w), lambda g: (0, g))
    return pl.pallas_call(
        state_body,
        grid=(CH,),
        in_specs=[blk, blk],
        out_specs=pl.BlockSpec((HC, HD, HD), lambda g: (g, 0, 0)),
        out_shape=jax.ShapeDtypeStruct((CH * HC, HD, HD), BF),
        cost_estimate=cost(2 * t * f * HD, 4 * t * f),
        compiler_params=pltpu.CompilerParams(vmem_limit_bytes=6 << 20),
        name="local_state",
    )(k, v)


def small_call(body, where, args, outs):
    return pl.pallas_call(
        body,
        in_specs=[pl.BlockSpec(memory_space=pltpu.SMEM)]
        + [pl.BlockSpec(memory_space=pltpu.VMEM)] * len(args),
        out_specs=[pl.BlockSpec(memory_space=pltpu.VMEM)] * len(outs),
        out_shape=outs,
        compiler_params=pltpu.CompilerParams(vmem_limit_bytes=6 << 20),
        cost_estimate=cost(1 << 18, 1 << 20),
    )(where, *args)


def chip_body(w_ref, s_ref, r_ref, own_ref, *out_refs):
    y, c = w_ref[6], w_ref[7]
    n = s_ref.shape[1]
    for k in range(n):
        at = lax.rem(y + k, n)
        part = s_ref[c, at].astype(F32) + r_ref[at].astype(F32)
        if k == 0:
            own_ref[...] = part
        else:
            out_refs[k - 1][...] = part.astype(BF)


def row_body(w_ref, own_ref, *refs):
    total = own_ref[...]
    for ref in refs[:-1]:
        total = total + ref[...].astype(F32)
    refs[-1][...] = total.astype(BF)


def plane_body(reverse, w_ref, own_ref, t1, t2, t3, z1, z2, z3, o_ref, o1, o2, o3):
    z, y = w_ref[5], w_ref[6]
    terms = [own_ref[...]] + [t[...].astype(F32) for t in (t1, t2, t3)]
    n = len(terms)
    base = jnp.zeros_like(terms[0])
    for k, ref in enumerate((z1, z2, z3), 1):
        use = z < k if reverse else z >= k
        base = base + jnp.where(use, ref[...].astype(F32), 0.0)
    for k in range(n):
        to = lax.rem(y + k, n)
        total = base
        for j in range(n):
            source = lax.rem(y - j + n, n)
            use = source > to if reverse else source < to
            total = total + jnp.where(use, terms[j], 0.0)
        if k == 0:
            o_ref[...] = total
        else:
            (o1, o2, o3)[k - 1][...] = total.astype(BF)


def core_body(reverse, w_ref, s_ref, r_ref, p0, p1, p2, p3, mine_ref, give_ref):
    y, c = w_ref[6], w_ref[7]
    n = s_ref.shape[1]
    first = c == (1 if reverse else 0)
    for j, p in enumerate((p0, p1, p2, p3)):
        at = lax.rem(y - j + n, n)
        base = p[...].astype(F32)
        mine_ref[at] = (base + jnp.where(first, 0.0, r_ref[at].astype(F32))).astype(BF)
        give_ref[at] = (base + jnp.where(first, s_ref[c, at].astype(F32), 0.0)).astype(BF)


def partner(x, axis, bits):
    return lax.ppermute(x, axis, [(d, d ^ bits) for d in range(lax.axis_size(axis))])


def give_to(x, axis, by):
    n = lax.axis_size(axis)
    return lax.ppermute(x, axis, [(d, (d + by) % n) for d in range(n)])


def carry(state, where, core, reverse, fill_row, fill_plane, fill_core):
    heads, d, e = state.shape
    n = lax.axis_size("y")
    rows = heads * d // (2 * n)
    parts = state.reshape(2, n, rows, e)
    give = lax.dynamic_index_in_dim(parts, 1 - core, 0, False)
    other = give_to(give, "c", 1)
    one = jax.ShapeDtypeStruct((rows, e), F32)
    low = jax.ShapeDtypeStruct((rows, e), BF)
    half = jax.ShapeDtypeStruct((n, rows, e), BF)
    own, *out = small_call(chip_body, where, [parts, other], [one] + [low] * (n - 1))
    terms = [own] + [give_to(x, "y", k) for k, x in enumerate(out, 1)]
    filled_row = fill_row(out)
    terms = after(terms, filled_row)
    (row,) = small_call(row_body, where, terms, [low])
    rows_before = [give_to(row, "z", k) for k in range(1, n)]
    filled_plane = fill_plane(row, filled_row)
    rows_before = after(rows_before, filled_plane[-1] if reverse else filled_plane)
    own, *out = small_call(
        functools.partial(plane_body, reverse),
        where,
        terms + rows_before,
        [one] + [low] * (n - 1),
    )
    sums = [own] + [give_to(x, "y", k) for k, x in enumerate(out, 1)]
    filled_core = fill_core(out, filled_plane)
    sums = after(sums, filled_core)
    mine, give = small_call(
        functools.partial(core_body, reverse), where, [parts, other] + sums, [half] * 2
    )
    got = give_to(give, "c", 1)
    shape = (heads // 2, d, e)
    return (mine.reshape(shape), got.reshape(shape)), filled_row, filled_plane, filled_core


def after(x, *others):
    return lax.optimization_barrier((x, others))[0]


def scores_body(q_ref, k_ref, v_ref, w_ref, o_ref):
    keep = causal(q_ref.shape[0])
    for h in range(HC):
        w = jnp.where(keep, mm(head(q_ref, h), head(k_ref, h), 1, 1), 0.0).astype(BF)
        w_ref[h] = w
        o_ref[:, h * HD : (h + 1) * HD] = mm(w, head(v_ref, h), 1, 0)


def local_scores(q, k, v):
    t, f = q.shape
    w = f // CH
    blk = pl.BlockSpec((t, w), lambda g: (0, g))
    return pl.pallas_call(
        scores_body,
        grid=(CH,),
        in_specs=[blk, blk, blk],
        out_specs=[pl.BlockSpec((HC, t, t), lambda g: (g, 0, 0)), blk],
        out_shape=[
            jax.ShapeDtypeStruct((CH * HC, t, t), BF),
            jax.ShapeDtypeStruct((t, f), F32),
        ],
        cost_estimate=cost(4 * t * t * f, 14 * t * f),
        compiler_params=pltpu.CompilerParams(vmem_limit_bytes=12 << 20),
        name="local_scores",
    )(q, k, v)


def pick(w_ref, chunk, m_ref, t_ref, h):
    return jnp.where(lax.div(chunk, CH // 2) == w_ref[7], m_ref[h], t_ref[h])


def attend_body(w_ref, q_ref, o_ref, m_ref, t_ref, g_ref, near_ref, far_ref, a_ref):
    g = pl.program_id(0)
    normed = []
    for h in range(HC):
        cols = slice(h * HD, (h + 1) * HD)
        state = pick(w_ref, w_ref[g], m_ref, t_ref, h)
        a = o_ref[:, cols] + mm(head(q_ref, h), state, 1, 0)
        a_ref[0, :, cols] = a
        inv = lax.rsqrt(jnp.mean(a * a, axis=-1, keepdims=True) + EPSILON)
        normed.append((a * inv * g_ref[:, cols]).astype(BF))
    normed = jnp.concatenate(normed, axis=1)

    @pl.when(g < CH // 2)
    def _():
        near_ref[...] = normed

    @pl.when(g >= CH // 2)
    def _():
        far_ref[...] = normed


def attend(where, q, out, carried, gain):
    t, f = q.shape
    w = f // CH
    two = CH // 2
    blk = pl.BlockSpec((t, w), lambda g, i: (0, i[g]))
    st = pl.BlockSpec((HC, HD, HD), lambda g, i: (lax.rem(i[g], two), 0, 0))
    return pl.pallas_call(
        attend_body,
        grid_spec=pltpu.PrefetchScalarGridSpec(
            num_scalar_prefetch=1,
            grid=(CH,),
            in_specs=[blk, blk, st, st, pl.BlockSpec((1, w), lambda g, i: (0, i[g]))],
            out_specs=[
                pl.BlockSpec((t, w), lambda g, i: (0, jnp.minimum(g, two - 1))),
                pl.BlockSpec((t, w), lambda g, i: (0, jnp.maximum(g - two, 0))),
                pl.BlockSpec((1, t, w), lambda g, i: (i[g], 0, 0)),
            ],
        ),
        out_shape=[jax.ShapeDtypeStruct((t, two * w), BF)] * 2
        + [jax.ShapeDtypeStruct((CH, t, w), F32)],
        cost_estimate=cost(2 * t * f * HD, 12 * t * f),
        compiler_params=pltpu.CompilerParams(vmem_limit_bytes=12 << 20),
        name="attend",
    )(where, q, out, *carried, gain)


def grad_attn_body(i_ref, q_ref, a_ref, gn_ref, g_ref, go_ref, w_ref, ga_ref, lg_ref):
    rows = w_ref.shape[0] * w_ref.shape[2]

    def finish(gn):
        for h in range(HC):
            cols = slice(h * HD, (h + 1) * HD)
            a = a_ref[0, :, cols]
            inv = lax.rsqrt(jnp.mean(a * a, axis=-1, keepdims=True) + EPSILON)
            unit = a * inv
            gu = gn[:, cols] * g_ref[:, cols]
            ga = inv * (gu - unit * jnp.mean(gu * unit, axis=-1, keepdims=True))
            ga = ga.astype(BF)
            ga_ref[0, :, cols] = ga
            lg_ref[h] = mm(head(q_ref, h), ga, 0, 0).astype(BF)

    @pl.when(pl.program_id(0) == 0)
    def _():
        finish(gn_ref[...])

    @pl.when(pl.program_id(0) > 0)
    def _():
        finish(mm(go_ref[...], w_ref[:, 0].reshape(rows, w_ref.shape[3]), 1, 1))


def grad_attn(order, q, attended, gn, gain, grad_rows, gathered):
    t, f = q.shape
    w = f // CH
    n, _, r, d = gathered.shape
    return pl.pallas_call(
        grad_attn_body,
        grid_spec=pltpu.PrefetchScalarGridSpec(
            num_scalar_prefetch=1,
            grid=(CH,),
            in_specs=[
                pl.BlockSpec((t, w), lambda g, i: (0, i[g])),
                pl.BlockSpec((1, t, w), lambda g, i: (i[g], 0, 0)),
                pl.BlockSpec((t, w), lambda g, i: (0, 0)),
                pl.BlockSpec((1, w), lambda g, i: (0, i[g])),
                pl.BlockSpec((t, d), lambda g, i: (0, 0)),
                pl.BlockSpec((n, 1, r, d), lambda g, i: (0, jnp.maximum(g - 1, 0), 0, 0)),
            ],
            out_specs=[
                pl.BlockSpec((1, t, w), lambda g, i: (g, 0, 0)),
                pl.BlockSpec((HC, HD, HD), lambda g, i: (g, 0, 0)),
            ],
        ),
        out_shape=[
            jax.ShapeDtypeStruct((CH, t, w), BF),
            jax.ShapeDtypeStruct((CH * HC, HD, HD), BF),
        ],
        cost_estimate=cost(2 * t * f * HD + 6 * t * w * d, 12 * t * f + 6 * w * d),
        compiler_params=pltpu.CompilerParams(vmem_limit_bytes=20 << 20),
        name="grad_attn",
    )(order, q, attended, gn, gain, grad_rows, gathered)


def grads_body(i_ref, q_ref, k_ref, v_ref, w_ref, ga_ref, m_ref, t_ref, gq_ref, gk_ref, gv_ref):
    chunk = i_ref[pl.program_id(0)]
    keep = causal(q_ref.shape[0])
    for h in range(HC):
        cols = slice(h * HD, (h + 1) * HD)
        ga = ga_ref[0, :, cols]
        gs = jnp.where(keep, mm(ga, head(v_ref, h), 1, 1), 0.0).astype(BF)
        gq = mm(gs, head(k_ref, h), 1, 0) + mm(ga, pick(i_ref, chunk, m_ref, t_ref, h), 1, 1)
        gq_ref[:, cols] = gq.astype(BF)
        gk_ref[0, :, cols] = mm(gs, head(q_ref, h), 0, 0)
        gv_ref[0, :, cols] = mm(w_ref[h], ga, 0, 0)


def local_grads(order, q, k, v, weights, ga, carried):
    t, f = q.shape
    w = f // CH
    nat = pl.BlockSpec((t, w), lambda g, i: (0, i[g]))
    chunk = pl.BlockSpec((1, t, w), lambda g, i: (g, 0, 0))
    return pl.pallas_call(
        grads_body,
        grid_spec=pltpu.PrefetchScalarGridSpec(
            num_scalar_prefetch=1,
            grid=(CH,),
            in_specs=[
                nat,
                nat,
                nat,
                pl.BlockSpec((HC, t, t), lambda g, i: (i[g], 0, 0)),
                chunk,
            ]
            + [pl.BlockSpec((HC, HD, HD), lambda g, i: (lax.rem(i[g], CH // 2), 0, 0))] * 2,
            out_specs=[nat, chunk, chunk],
        ),
        out_shape=[
            jax.ShapeDtypeStruct((t, f), BF),
            jax.ShapeDtypeStruct((CH, t, w), F32),
            jax.ShapeDtypeStruct((CH, t, w), F32),
        ],
        cost_estimate=cost(8 * t * t * f, 24 * t * f),
        compiler_params=pltpu.CompilerParams(vmem_limit_bytes=20 << 20),
        name="local_grads",
    )(order, q, k, v, weights, ga, *carried)


def later_body(i_ref, k_ref, v_ref, m_ref, t_ref, pk_ref, pv_ref, gk_ref, gv_ref):
    for h in range(HC):
        cols = slice(h * HD, (h + 1) * HD)
        state = pick(i_ref, pl.program_id(0), m_ref, t_ref, h)
        gk = pk_ref[0, :, cols] + mm(head(v_ref, h), state, 1, 1)
        gv = pv_ref[0, :, cols] + mm(head(k_ref, h), state, 1, 0)
        gk_ref[:, cols] = gk.astype(BF)
        gv_ref[:, cols] = gv.astype(BF)


def later_grads(order, k, v, later, pk, pv):
    t, f = k.shape
    w = f // CH
    nat = pl.BlockSpec((t, w), lambda g, i: (0, i[g]))
    chunk = pl.BlockSpec((1, t, w), lambda g, i: (g, 0, 0))
    return pl.pallas_call(
        later_body,
        grid_spec=pltpu.PrefetchScalarGridSpec(
            num_scalar_prefetch=1,
            grid=(CH,),
            in_specs=[
                nat,
                nat,
                pl.BlockSpec((HC, HD, HD), lambda g, i: (lax.rem(g, CH // 2), 0, 0)),
                pl.BlockSpec((HC, HD, HD), lambda g, i: (lax.rem(g, CH // 2), 0, 0)),
                chunk,
                chunk,
            ],
            out_specs=[nat, nat],
        ),
        out_shape=[jax.ShapeDtypeStruct((t, f), BF)] * 2,
        cost_estimate=cost(4 * t * f * HD, 16 * t * f),
        compiler_params=pltpu.CompilerParams(vmem_limit_bytes=12 << 20),
        name="later_grads",
    )(order, k, v, *later, pk, pv)


def layer_body(i_ref, near_ref, far_ref, own_ref, w_ref, o_ref):
    w = own_ref.shape[0]
    mine = lax.div(i_ref[4], CH // 2)
    total = None
    for k in range(CH):
        chunk = i_ref[k]
        cols = pl.ds(pl.multiple_of(lax.rem(chunk, CH // 2) * w, w), w)
        is_near = lax.div(chunk, CH // 2) == mine
        rows = jnp.where(is_near, near_ref[:, cols], far_ref[:, cols])
        block = own_ref[...] if k == 0 else w_ref[:, k - 1].reshape(own_ref.shape)
        part = mm(rows, block, 1, 0)
        total = part if total is None else total + part
    o_ref[...] = total.astype(BF)


def layer_rows(where, near, far, own, gathered):
    t = near.shape[0]
    w = own.shape[0]
    n, c, r, d = gathered.shape
    tile = 1024
    half = pl.BlockSpec(near.shape, lambda g, i: (0, 0))
    return pl.pallas_call(
        layer_body,
        grid_spec=pltpu.PrefetchScalarGridSpec(
            num_scalar_prefetch=1,
            grid=(d // tile,),
            in_specs=[
                half,
                half,
                pl.BlockSpec((w, tile), lambda g, i: (0, g)),
                pl.BlockSpec((n, c, r, tile), lambda g, i: (0, 0, 0, g)),
            ],
            out_specs=pl.BlockSpec((t, tile), lambda g, i: (0, g)),
        ),
        out_shape=jax.ShapeDtypeStruct((t, d), BF),
        cost_estimate=cost(2 * t * CH * w * d, 2 * (CH * w * d + CH * t * w + t * d)),
        compiler_params=pltpu.CompilerParams(vmem_limit_bytes=20 << 20),
        name="layer_rows",
    )(where, near, far, own, gathered)


def weight_total(nt, grads, o_ref, extra_ref):
    total = None
    for s, g in enumerate(grads):
        part = mm(nt[s], g[...], 1, 0)
        total = part if total is None else total + part
    chips, blocks, rows, w = o_ref.shape
    span = chips * rows
    for b in range(blocks):
        one = total[b * span : (b + 1) * span].reshape(chips, rows, w)
        if extra_ref is not None:
            one = one + extra_ref[:, b].astype(F32)
        o_ref[:, b] = one.astype(BF)


def give_body(i_ref, n0, n1, n2, n3, *rest):
    *grads, o_ref, nt_ref = rest

    @pl.when(pl.program_id(0) == 0)
    def _():
        for s, n in enumerate((n0, n1, n2, n3)):
            nt_ref[s] = n[...].T

    weight_total(nt_ref, grads, o_ref, None)


def keep_body(i_ref, nt_ref, extra_ref, *rest):
    *grads, o_ref = rest
    weight_total(nt_ref, grads, o_ref, extra_ref)


def weight_half(body, half, rows, grads_all, shape, nt_out):
    t, d = grads_all[0].shape
    w = rows[0].shape[1]
    tile = 256
    steps = d // 2 // tile
    own = pl.BlockSpec(shape[:-1] + (tile,), lambda g, i: (0, 0, 0, g))
    whole = pl.BlockSpec((t, w), lambda g, i: (0, 0))
    turned = pl.BlockSpec((CH, w, t), lambda g, i: (0, 0, 0))
    out = jax.ShapeDtypeStruct(shape, BF)
    cols = pl.BlockSpec((t, tile), lambda g, i: (0, i[0] * steps + g))
    return pl.pallas_call(
        body,
        grid_spec=pltpu.PrefetchScalarGridSpec(
            num_scalar_prefetch=1,
            grid=(steps,),
            in_specs=([whole] * CH if nt_out else [turned, own]) + [cols] * CH,
            out_specs=[own, turned] if nt_out else own,
        ),
        out_shape=[out, jax.ShapeDtypeStruct((CH, w, t), BF)] if nt_out else out,
        cost_estimate=cost(CH * t * w * d, 2 * CH * t * d + 2 * CH * t * w + w * d),
        compiler_params=pltpu.CompilerParams(vmem_limit_bytes=20 << 20),
        name="weight_half",
    )(half, *rows, *grads_all)


def sum_body(scale, w_ref, s_ref, keep_ref, x_ref, c_ref, xc_ref, total):
    acc = s_ref[0].astype(F32)
    for step in range(1, s_ref.shape[0]):
        acc = acc + s_ref[step].astype(F32)
    total[...] = acc * scale
    rows = keep_ref.shape[0]
    block, c = lax.rem(w_ref[4], 2), w_ref[7]
    mine = pl.ds(pl.multiple_of(c * rows, rows), rows)
    other = pl.ds(pl.multiple_of((1 - c) * rows, rows), rows)
    keep_ref[...] = total[block, mine]
    x_ref[...] = total[1 - block, mine]
    c_ref[...] = total[block, other]
    xc_ref[...] = total[1 - block, other]


def sum_parts(where, parts, scale):
    _, b, r, w = parts.shape
    return pl.pallas_call(
        functools.partial(sum_body, scale),
        in_specs=[
            pl.BlockSpec(memory_space=pltpu.SMEM),
            pl.BlockSpec(memory_space=pltpu.VMEM),
        ],
        out_specs=[pl.BlockSpec(memory_space=pltpu.VMEM)] * 4,
        out_shape=[jax.ShapeDtypeStruct((r // 2, w), F32)] * 4,
        scratch_shapes=[pltpu.VMEM((b, r, w), F32)],
        cost_estimate=cost(parts.size, 2 * parts.size),
        compiler_params=pltpu.CompilerParams(vmem_limit_bytes=8 << 20),
        name="sum_parts",
    )(where, parts)


def join_body(w_ref, own_ref, x_ref, c_ref, xc_ref, o_ref):
    block, c = lax.rem(w_ref[4], 2), w_ref[7]
    w = own_ref.shape[1]
    for ref, b, h in (
        (own_ref, block, c),
        (x_ref, 1 - block, c),
        (c_ref, block, 1 - c),
        (xc_ref, 1 - block, 1 - c),
    ):
        o_ref[:, pl.ds(pl.multiple_of((2 * b + h) * w, w), w)] = ref[...]


def shift(x, axis, by):
    n = lax.axis_size(axis)
    return lax.ppermute(x, axis, [((d + by) % n, d) for d in range(n)])


def layer(queries, keys, values, gain, out_weight, grad_out):
    tok_rows, feat_width = queries.shape[1:]
    model_width = grad_out.shape[2]
    q = queries.reshape(tok_rows, feat_width)
    k = keys.reshape(tok_rows, feat_width)
    v = values.reshape(tok_rows, feat_width)
    grad_rows = grad_out.reshape(tok_rows, model_width)
    gain_row = gain.reshape(1, feat_width)
    seqs = lax.axis_size("x")
    blocks_n = lax.axis_size(CTX)
    at_x = lax.axis_index("x")
    at_ctx = lax.axis_index(CTX)
    at_core = lax.axis_index("c")
    places = [at_x, lax.axis_index("z"), lax.axis_index("y"), at_core]
    order = [(at_x + n) % CH for n in range(CH)]
    where = jnp.stack(order + places).astype(jnp.int32)
    row_half = at_x // 2
    turns = [2 * row_half, 2 * row_half + 1, 2 - 2 * row_half, 3 - 2 * row_half]
    turns = jnp.stack(turns + places).astype(jnp.int32)
    mine = at_core.reshape(1).astype(jnp.int32)
    others = 1 - mine

    piece = out_weight.shape[0] // blocks_n
    own_piece = lax.dynamic_slice_in_dim(out_weight, at_ctx * piece, piece, 0)
    pieces = [shift(own_piece, "x", by) for by in range(1, CH)]
    state = local_state(k, v)
    half_cols = model_width // 2
    side = at_x % 2
    near_cols = lax.dynamic_slice_in_dim(grad_rows, side * half_cols, half_cols, 1)
    far_cols = lax.dynamic_slice_in_dim(grad_rows, (1 - side) * half_cols, half_cols, 1)
    pieces, near_cols, far_cols, sent_rows, q_next = lax.optimization_barrier(
        (pieces, near_cols, far_cols, grad_rows, q, state)
    )[:5]
    gathered = lax.all_gather(jnp.concatenate(pieces, axis=0), CTX, axis=0, tiled=True)
    gathered = gathered.reshape(blocks_n, CH - 1, piece, model_width)
    gathered = pltpu.with_memory_space_constraint(gathered, pltpu.HBM)
    own_weight = pltpu.with_memory_space_constraint(out_weight, pltpu.HBM)

    grads_all = [
        near_cols,
        partner(far_cols, "x", 1),
        partner(near_cols, "x", 2),
        partner(far_cols, "x", 3),
    ]

    carried, (weights, local_out), gn, _ = carry(
        state,
        where,
        at_core,
        False,
        lambda sent: local_scores(after(q_next, sent), k, v),
        lambda sent, done: mm(after(sent_rows, sent, done), out_weight, 1, 1),
        lambda sent, done: (),
    )
    near, far, attended = attend(turns, q, local_out, carried, gain_row)
    normed_all = [
        near,
        partner(near, "x", 1),
        partner(far, "x", 2),
        partner(far, "x", 3),
    ]
    attended = pltpu.with_memory_space_constraint(attended, pltpu.HBM)
    gn = pltpu.with_memory_space_constraint(gn, pltpu.HBM)

    ga, lg = grad_attn(where, q, attended, gn, gain_row, grad_rows, gathered)
    chips = blocks_n // 2
    shape = (chips, 2, out_weight.shape[0] // chips, half_cols // 2)

    def first_half(sent):
        rows = after(normed_all, sent)
        return weight_half(give_body, others, rows, grads_all, shape, True)

    def second_half(sent, done):
        for_partner, turned = done
        extra = give_to(for_partner, "c", 1)
        return weight_half(
            keep_body, mine, [after(turned, sent), extra], grads_all, shape, False
        )

    def halves(sent, done):
        partial = second_half(sent, done)
        return lax.all_to_all(partial, ("z", "y"), 0, 0, tiled=True), partial

    def rest(sent, done):
        grads = local_grads(where, q, k, v, weights, after(ga, sent), carried)
        rows = layer_rows(where, near, after(far, grads), own_weight, gathered)
        return grads, rows

    later, _, (parts, _), (grads, layer_out) = carry(
        lg, where, at_core, True, first_half, halves, rest
    )
    grad_query, pk, pv = grads
    grad_key, grad_value = later_grads(where, k, v, later, pk, pv)

    parts = after(parts, layer_out, later[0])
    token_count = seqs * blocks_n * tok_rows
    own, to_x, to_c, to_both = sum_parts(where, parts, 1.0 / math.sqrt(token_count))
    both = lax.ppermute(to_both, ("x", "c"), [(d, d ^ 3) for d in range(2 * seqs)])
    (grad_weight,) = small_call(
        join_body,
        where,
        [own, partner(to_x, "x", 1), partner(to_c, "c", 1), both],
        [jax.ShapeDtypeStruct((own.shape[0], model_width), F32)],
    )
    out_shape = (1, tok_rows, feat_width)
    return (
        layer_out.reshape(1, tok_rows, model_width),
        grad_query.reshape(out_shape),
        grad_key.reshape(out_shape),
        grad_value.reshape(out_shape),
        grad_weight,
    )


def solution(mesh):
    mesh = Mesh(mesh.devices.reshape(4, 4, 4, 2), ("x",) + CTX)
    tokens = P("x", CTX, None)
    in_specs = (tokens, tokens, tokens, P(), P("x", None), tokens)
    out_specs = (tokens, tokens, tokens, tokens, P(("x",) + CTX, None))
    return jax.shard_map(layer, mesh=mesh, in_specs=in_specs, out_specs=out_specs, check_vma=False)
```

```python
import functools
import math

import jax
import jax.numpy as jnp
from jax import lax
from jax.experimental import pallas as pl
from jax.experimental.pallas import tpu as pltpu
from jax.sharding import Mesh, PartitionSpec as P

HD = 128
EPSILON = 1e-06
BF = jnp.bfloat16
F32 = jnp.float32
CTX = ("z", "y", "c")
CH = 4
HC = 4


def mm(a, b, ca, cb):
    return lax.dot_general(a, b, (((ca,), (cb,)), ((), ())), preferred_element_type=F32)


def cost(flops, nbytes):
    return pl.CostEstimate(flops=flops, bytes_accessed=nbytes, transcendentals=0)


def head(ref, h):
    return ref[:, h * HD : (h + 1) * HD]


def causal(n):
    return lax.broadcasted_iota(jnp.int32, (n, n), 0) >= lax.broadcasted_iota(
        jnp.int32, (n, n), 1
    )


def state_body(k_ref, v_ref, s_ref):
    for h in range(HC):
        s_ref[h] = mm(head(k_ref, h), head(v_ref, h), 0, 0).astype(BF)


def local_state(k, v):
    t, f = k.shape
    w = f // CH
    blk = pl.BlockSpec((t, w), lambda g: (0, g))
    return pl.pallas_call(
        state_body,
        grid=(CH,),
        in_specs=[blk, blk],
        out_specs=pl.BlockSpec((HC, HD, HD), lambda g: (g, 0, 0)),
        out_shape=jax.ShapeDtypeStruct((CH * HC, HD, HD), BF),
        cost_estimate=cost(2 * t * f * HD, 4 * t * f),
        compiler_params=pltpu.CompilerParams(vmem_limit_bytes=6 << 20),
        name="local_state",
    )(k, v)


def small_call(body, where, args, outs):
    return pl.pallas_call(
        body,
        in_specs=[pl.BlockSpec(memory_space=pltpu.SMEM)]
        + [pl.BlockSpec(memory_space=pltpu.VMEM)] * len(args),
        out_specs=[pl.BlockSpec(memory_space=pltpu.VMEM)] * len(outs),
        out_shape=outs,
        compiler_params=pltpu.CompilerParams(vmem_limit_bytes=6 << 20),
        cost_estimate=cost(1 << 18, 1 << 20),
    )(where, *args)


def chip_body(w_ref, s_ref, r_ref, own_ref, *out_refs):
    y, c = w_ref[6], w_ref[7]
    n = s_ref.shape[1]
    for k in range(n):
        at = lax.rem(y + k, n)
        part = s_ref[c, at].astype(F32) + r_ref[at].astype(F32)
        if k == 0:
            own_ref[...] = part
        else:
            out_refs[k - 1][...] = part.astype(BF)


def row_body(w_ref, own_ref, *refs):
    total = own_ref[...]
    for ref in refs[:-1]:
        total = total + ref[...].astype(F32)
    refs[-1][...] = total.astype(BF)


def plane_body(reverse, w_ref, own_ref, t1, t2, t3, z1, z2, z3, o_ref, o1, o2, o3):
    z, y = w_ref[5], w_ref[6]
    terms = [own_ref[...]] + [t[...].astype(F32) for t in (t1, t2, t3)]
    n = len(terms)
    base = jnp.zeros_like(terms[0])
    for k, ref in enumerate((z1, z2, z3), 1):
        use = z < k if reverse else z >= k
        base = base + jnp.where(use, ref[...].astype(F32), 0.0)
    for k in range(n):
        to = lax.rem(y + k, n)
        total = base
        for j in range(n):
            source = lax.rem(y - j + n, n)
            use = source > to if reverse else source < to
            total = total + jnp.where(use, terms[j], 0.0)
        if k == 0:
            o_ref[...] = total
        else:
            (o1, o2, o3)[k - 1][...] = total.astype(BF)


def core_body(reverse, w_ref, s_ref, r_ref, p0, p1, p2, p3, mine_ref, give_ref):
    y, c = w_ref[6], w_ref[7]
    n = s_ref.shape[1]
    first = c == (1 if reverse else 0)
    for j, p in enumerate((p0, p1, p2, p3)):
        at = lax.rem(y - j + n, n)
        base = p[...].astype(F32)
        mine_ref[at] = (base + jnp.where(first, 0.0, r_ref[at].astype(F32))).astype(BF)
        give_ref[at] = (base + jnp.where(first, s_ref[c, at].astype(F32), 0.0)).astype(BF)


def partner(x, axis, bits):
    return lax.ppermute(x, axis, [(d, d ^ bits) for d in range(lax.axis_size(axis))])


def give_to(x, axis, by):
    n = lax.axis_size(axis)
    return lax.ppermute(x, axis, [(d, (d + by) % n) for d in range(n)])


def carry(state, where, core, reverse, fill_row, fill_plane, fill_core):
    heads, d, e = state.shape
    n = lax.axis_size("y")
    rows = heads * d // (2 * n)
    parts = state.reshape(2, n, rows, e)
    give = lax.dynamic_index_in_dim(parts, 1 - core, 0, False)
    other = give_to(give, "c", 1)
    one = jax.ShapeDtypeStruct((rows, e), F32)
    low = jax.ShapeDtypeStruct((rows, e), BF)
    half = jax.ShapeDtypeStruct((n, rows, e), BF)
    own, *out = small_call(chip_body, where, [parts, other], [one] + [low] * (n - 1))
    terms = [own] + [give_to(x, "y", k) for k, x in enumerate(out, 1)]
    filled_row = fill_row(out)
    terms = after(terms, filled_row)
    (row,) = small_call(row_body, where, terms, [low])
    rows_before = [give_to(row, "z", k) for k in range(1, n)]
    filled_plane = fill_plane(row, filled_row)
    rows_before = after(rows_before, filled_plane)
    own, *out = small_call(
        functools.partial(plane_body, reverse),
        where,
        terms + rows_before,
        [one] + [low] * (n - 1),
    )
    sums = [own] + [give_to(x, "y", k) for k, x in enumerate(out, 1)]
    filled_core = fill_core(out, filled_plane)
    sums = after(sums, filled_core[-1] if reverse else filled_core)
    mine, give = small_call(
        functools.partial(core_body, reverse), where, [parts, other] + sums, [half] * 2
    )
    got = give_to(give, "c", 1)
    shape = (heads // 2, d, e)
    return (mine.reshape(shape), got.reshape(shape)), filled_row, filled_plane, filled_core


def hbm(x):
    return pltpu.with_memory_space_constraint(x, pltpu.HBM)


def after(x, *others):
    return lax.optimization_barrier((x, others))[0]


def scores_body(q_ref, k_ref, v_ref, w_ref, o_ref):
    keep = causal(q_ref.shape[0])
    for h in range(HC):
        w = jnp.where(keep, mm(head(q_ref, h), head(k_ref, h), 1, 1), 0.0).astype(BF)
        w_ref[h] = w
        o_ref[:, h * HD : (h + 1) * HD] = mm(w, head(v_ref, h), 1, 0)


def local_scores(q, k, v):
    t, f = q.shape
    w = f // CH
    blk = pl.BlockSpec((t, w), lambda g: (0, g))
    return pl.pallas_call(
        scores_body,
        grid=(CH,),
        in_specs=[blk, blk, blk],
        out_specs=[pl.BlockSpec((HC, t, t), lambda g: (g, 0, 0)), blk],
        out_shape=[
            pltpu.HBM((CH * HC, t, t), BF),
            pltpu.HBM((t, f), F32),
        ],
        cost_estimate=cost(4 * t * t * f, 14 * t * f),
        compiler_params=pltpu.CompilerParams(vmem_limit_bytes=12 << 20),
        name="local_scores",
    )(q, k, v)


def pick(w_ref, chunk, m_ref, t_ref, h):
    return jnp.where(lax.div(chunk, CH // 2) == w_ref[7], m_ref[h], t_ref[h])


def attend_body(w_ref, q_ref, o_ref, m_ref, t_ref, g_ref, near_ref, far_ref, a_ref):
    g = pl.program_id(0)
    normed = []
    for h in range(HC):
        cols = slice(h * HD, (h + 1) * HD)
        state = pick(w_ref, w_ref[g], m_ref, t_ref, h)
        a = o_ref[:, cols] + mm(head(q_ref, h), state, 1, 0)
        a_ref[0, :, cols] = a
        inv = lax.rsqrt(jnp.mean(a * a, axis=-1, keepdims=True) + EPSILON)
        normed.append((a * inv * g_ref[:, cols]).astype(BF))
    normed = jnp.concatenate(normed, axis=1)

    @pl.when(g < CH // 2)
    def _():
        near_ref[...] = normed

    @pl.when(g >= CH // 2)
    def _():
        far_ref[...] = normed


def attend(where, q, out, carried, gain):
    t, f = q.shape
    w = f // CH
    two = CH // 2
    blk = pl.BlockSpec((t, w), lambda g, i: (0, i[g]))
    st = pl.BlockSpec((HC, HD, HD), lambda g, i: (lax.rem(i[g], two), 0, 0))
    return pl.pallas_call(
        attend_body,
        grid_spec=pltpu.PrefetchScalarGridSpec(
            num_scalar_prefetch=1,
            grid=(CH,),
            in_specs=[blk, blk, st, st, pl.BlockSpec((1, w), lambda g, i: (0, i[g]))],
            out_specs=[
                pl.BlockSpec((t, w), lambda g, i: (0, jnp.minimum(g, two - 1))),
                pl.BlockSpec((t, w), lambda g, i: (0, jnp.maximum(g - two, 0))),
                pl.BlockSpec((1, t, w), lambda g, i: (i[g], 0, 0)),
            ],
        ),
        out_shape=[jax.ShapeDtypeStruct((t, two * w), BF)] * 2
        + [pltpu.HBM((CH, t, w), F32)],
        cost_estimate=cost(2 * t * f * HD, 12 * t * f),
        compiler_params=pltpu.CompilerParams(vmem_limit_bytes=12 << 20),
        name="attend",
    )(where, q, out, *carried, gain)


PARTS = 1
SLOTS = 3


def grad_attn_body(
    i_ref, q_ref, a_ref, gn_ref, g_ref, go_hbm, w_hbm, ga_ref, lg_ref, go, w, go_sem, w_sem
):
    g = pl.program_id(0)
    _, blocks, rows, d = w.shape
    last = PARTS * (CH - 1)

    def load(t):
        at = pl.ds(lax.rem(t, PARTS) * blocks, blocks)
        slot = lax.rem(t, SLOTS)
        source = w_hbm.at[at, lax.div(t, PARTS)]
        return pltpu.make_async_copy(source, w.at[slot], w_sem.at[slot])

    whole = pltpu.make_async_copy(go_hbm, go, go_sem)

    def finish(gn):
        for h in range(HC // PARTS):
            cols = slice(h * HD, (h + 1) * HD)
            a = a_ref[0, :, cols]
            inv = lax.rsqrt(jnp.mean(a * a, axis=-1, keepdims=True) + EPSILON)
            unit = a * inv
            gu = gn[:, cols] * g_ref[:, cols]
            ga = inv * (gu - unit * jnp.mean(gu * unit, axis=-1, keepdims=True))
            ga = ga.astype(BF)
            ga_ref[0, :, cols] = ga
            lg_ref[h] = mm(head(q_ref, h), ga, 0, 0).astype(BF)

    @pl.when(g == 0)
    def _():
        whole.start()
        for t in range(SLOTS):
            load(t).start()

    @pl.when(g < PARTS)
    def _():
        finish(gn_ref[...])

    @pl.when(g == PARTS)
    def _():
        whole.wait()

    @pl.when(g >= PARTS)
    def _():
        t = g - PARTS
        load(t).wait()
        finish(mm(go[...], w[lax.rem(t, SLOTS)].reshape(blocks * rows, d), 1, 1))

        @pl.when(t + SLOTS < last)
        def _():
            load(t + SLOTS).start()


def grad_attn(order, q, attended, gn, gain, grad_rows, gathered):
    t, f = q.shape
    w = f // CH // PARTS
    n, _, r, d = gathered.shape

    def nat(g, i):
        return (0, i[lax.div(g, PARTS)] * PARTS + lax.rem(g, PARTS))

    return pl.pallas_call(
        grad_attn_body,
        grid_spec=pltpu.PrefetchScalarGridSpec(
            num_scalar_prefetch=1,
            grid=(CH * PARTS,),
            in_specs=[
                pl.BlockSpec((t, w), nat),
                pl.BlockSpec(
                    (1, t, w), lambda g, i: (i[lax.div(g, PARTS)], 0, lax.rem(g, PARTS))
                ),
                pl.BlockSpec((t, w), lambda g, i: (0, jnp.minimum(g, PARTS - 1))),
                pl.BlockSpec((1, w), nat),
                pl.BlockSpec(memory_space=pltpu.HBM),
                pl.BlockSpec(memory_space=pltpu.HBM),
            ],
            out_specs=[
                pl.BlockSpec((1, t, w), lambda g, i: (lax.div(g, PARTS), 0, lax.rem(g, PARTS))),
                pl.BlockSpec((HC // PARTS, HD, HD), lambda g, i: (g, 0, 0)),
            ],
            scratch_shapes=[
                pltpu.VMEM((t, d), BF),
                pltpu.VMEM((SLOTS, n // PARTS, r, d), BF),
                pltpu.SemaphoreType.DMA(()),
                pltpu.SemaphoreType.DMA((SLOTS,)),
            ],
        ),
        out_shape=[
            pltpu.HBM((CH, t, f // CH), BF),
            jax.ShapeDtypeStruct((CH * HC, HD, HD), BF),
        ],
        cost_estimate=cost(2 * t * f * HD + 6 * t * w * d, 12 * t * f + 6 * w * d),
        compiler_params=pltpu.CompilerParams(vmem_limit_bytes=26 << 20),
        name="grad_attn",
    )(order, q, attended, gn, gain, grad_rows, gathered)


def grads_body(i_ref, q_ref, k_ref, v_ref, w_ref, ga_ref, m_ref, t_ref, gq_ref, gk_ref, gv_ref):
    chunk = i_ref[pl.program_id(0)]
    keep = causal(q_ref.shape[0])
    for h in range(HC):
        cols = slice(h * HD, (h + 1) * HD)
        ga = ga_ref[0, :, cols]
        gs = jnp.where(keep, mm(ga, head(v_ref, h), 1, 1), 0.0).astype(BF)
        gq = mm(gs, head(k_ref, h), 1, 0) + mm(ga, pick(i_ref, chunk, m_ref, t_ref, h), 1, 1)
        gq_ref[:, cols] = gq.astype(BF)
        gk_ref[0, :, cols] = mm(gs, head(q_ref, h), 0, 0)
        gv_ref[0, :, cols] = mm(w_ref[h], ga, 0, 0)


def local_grads(order, q, k, v, weights, ga, carried):
    t, f = q.shape
    w = f // CH
    nat = pl.BlockSpec((t, w), lambda g, i: (0, i[g]))
    chunk = pl.BlockSpec((1, t, w), lambda g, i: (g, 0, 0))
    return pl.pallas_call(
        grads_body,
        grid_spec=pltpu.PrefetchScalarGridSpec(
            num_scalar_prefetch=1,
            grid=(CH,),
            in_specs=[
                nat,
                nat,
                nat,
                pl.BlockSpec((HC, t, t), lambda g, i: (i[g], 0, 0)),
                chunk,
            ]
            + [pl.BlockSpec((HC, HD, HD), lambda g, i: (lax.rem(i[g], CH // 2), 0, 0))] * 2,
            out_specs=[nat, chunk, chunk],
        ),
        out_shape=[
            jax.ShapeDtypeStruct((t, f), BF),
            pltpu.HBM((CH, t, w), F32),
            pltpu.HBM((CH, t, w), F32),
        ],
        cost_estimate=cost(8 * t * t * f, 24 * t * f),
        compiler_params=pltpu.CompilerParams(vmem_limit_bytes=20 << 20),
        name="local_grads",
    )(order, q, k, v, weights, ga, *carried)


def later_body(i_ref, k_ref, v_ref, m_ref, t_ref, pk_ref, pv_ref, gk_ref, gv_ref):
    for h in range(HC):
        cols = slice(h * HD, (h + 1) * HD)
        state = pick(i_ref, pl.program_id(0), m_ref, t_ref, h)
        gk = pk_ref[0, :, cols] + mm(head(v_ref, h), state, 1, 1)
        gv = pv_ref[0, :, cols] + mm(head(k_ref, h), state, 1, 0)
        gk_ref[:, cols] = gk.astype(BF)
        gv_ref[:, cols] = gv.astype(BF)


def later_grads(order, k, v, later, pk, pv):
    t, f = k.shape
    w = f // CH
    nat = pl.BlockSpec((t, w), lambda g, i: (0, i[g]))
    chunk = pl.BlockSpec((1, t, w), lambda g, i: (g, 0, 0))
    return pl.pallas_call(
        later_body,
        grid_spec=pltpu.PrefetchScalarGridSpec(
            num_scalar_prefetch=1,
            grid=(CH,),
            in_specs=[
                nat,
                nat,
                pl.BlockSpec((HC, HD, HD), lambda g, i: (lax.rem(g, CH // 2), 0, 0)),
                pl.BlockSpec((HC, HD, HD), lambda g, i: (lax.rem(g, CH // 2), 0, 0)),
                chunk,
                chunk,
            ],
            out_specs=[nat, nat],
        ),
        out_shape=[jax.ShapeDtypeStruct((t, f), BF)] * 2,
        cost_estimate=cost(4 * t * f * HD, 16 * t * f),
        compiler_params=pltpu.CompilerParams(vmem_limit_bytes=12 << 20),
        name="later_grads",
    )(order, k, v, *later, pk, pv)


def layer_body(i_ref, near_ref, far_ref, own_ref, w_ref, o_ref):
    w = own_ref.shape[0]
    mine = lax.div(i_ref[4], CH // 2)
    total = None
    for k in range(CH):
        chunk = i_ref[k]
        cols = pl.ds(pl.multiple_of(lax.rem(chunk, CH // 2) * w, w), w)
        is_near = lax.div(chunk, CH // 2) == mine
        rows = jnp.where(is_near, near_ref[:, cols], far_ref[:, cols])
        block = own_ref[...] if k == 0 else w_ref[:, k - 1].reshape(own_ref.shape)
        part = mm(rows, block, 1, 0)
        total = part if total is None else total + part
    o_ref[...] = total.astype(BF)


def layer_rows(where, near, far, own, gathered):
    t = near.shape[0]
    w = own.shape[0]
    n, c, r, d = gathered.shape
    tile = 1024
    half = pl.BlockSpec(near.shape, lambda g, i: (0, 0))
    return pl.pallas_call(
        layer_body,
        grid_spec=pltpu.PrefetchScalarGridSpec(
            num_scalar_prefetch=1,
            grid=(d // tile,),
            in_specs=[
                half,
                half,
                pl.BlockSpec((w, tile), lambda g, i: (0, g)),
                pl.BlockSpec((n, c, r, tile), lambda g, i: (0, 0, 0, g)),
            ],
            out_specs=pl.BlockSpec((t, tile), lambda g, i: (0, g)),
        ),
        out_shape=jax.ShapeDtypeStruct((t, d), BF),
        cost_estimate=cost(2 * t * CH * w * d, 2 * (CH * w * d + CH * t * w + t * d)),
        compiler_params=pltpu.CompilerParams(vmem_limit_bytes=20 << 20),
        name="layer_rows",
    )(where, near, far, own, gathered)


def weight_total(nt, grads, o_ref, extra_ref):
    total = mm(nt[...], jnp.concatenate([g[...] for g in grads], axis=0), 1, 0)
    chips, blocks, rows, w = o_ref.shape
    span = chips * rows
    for b in range(blocks):
        one = total[b * span : (b + 1) * span].reshape(chips, rows, w)
        if extra_ref is not None:
            one = one + extra_ref[:, b].astype(F32)
        o_ref[:, b] = one.astype(BF)


def give_body(i_ref, n0, n1, n2, n3, *rest):
    *grads, o_ref, nt_ref = rest

    @pl.when(pl.program_id(0) == 0)
    def _():
        t = n0.shape[0]
        for s, n in enumerate((n0, n1, n2, n3)):
            nt_ref[:, s * t : (s + 1) * t] = n[...].T

    weight_total(nt_ref, grads, o_ref, None)


def keep_body(i_ref, nt_ref, extra_ref, *rest):
    *grads, o_ref = rest
    weight_total(nt_ref, grads, o_ref, extra_ref)


def weight_half(body, half, rows, grads_all, shape, nt_out):
    t, d = grads_all[0].shape
    w = rows[0].shape[1] if nt_out else rows[0].shape[0]
    tile = 256
    steps = d // 2 // tile
    own = pl.BlockSpec(shape[:-1] + (tile,), lambda g, i: (0, 0, 0, g))
    whole = pl.BlockSpec((t, w), lambda g, i: (0, 0))
    turned = pl.BlockSpec((w, CH * t), lambda g, i: (0, 0))
    out = pltpu.HBM(shape, BF)
    cols = pl.BlockSpec((t, tile), lambda g, i: (0, i[0] * steps + g))
    return pl.pallas_call(
        body,
        grid_spec=pltpu.PrefetchScalarGridSpec(
            num_scalar_prefetch=1,
            grid=(steps,),
            in_specs=([whole] * CH if nt_out else [turned, own]) + [cols] * CH,
            out_specs=[own, turned] if nt_out else own,
        ),
        out_shape=[out, jax.ShapeDtypeStruct((w, CH * t), BF)] if nt_out else out,
        cost_estimate=cost(CH * t * w * d, 2 * CH * t * d + 2 * CH * t * w + w * d),
        compiler_params=pltpu.CompilerParams(vmem_limit_bytes=20 << 20),
        name="weight_half",
    )(half, *rows, *grads_all)


def sum_body(scale, w_ref, s_ref, keep_ref, x_ref, c_ref, xc_ref, total):
    acc = s_ref[0].astype(F32)
    for step in range(1, s_ref.shape[0]):
        acc = acc + s_ref[step].astype(F32)
    total[...] = acc * scale
    rows = keep_ref.shape[0]
    block, c = lax.rem(w_ref[4], 2), w_ref[7]
    mine = pl.ds(pl.multiple_of(c * rows, rows), rows)
    other = pl.ds(pl.multiple_of((1 - c) * rows, rows), rows)
    keep_ref[...] = total[block, mine]
    x_ref[...] = total[1 - block, mine]
    c_ref[...] = total[block, other]
    xc_ref[...] = total[1 - block, other]


def sum_parts(where, parts, scale):
    _, b, r, w = parts.shape
    return pl.pallas_call(
        functools.partial(sum_body, scale),
        in_specs=[
            pl.BlockSpec(memory_space=pltpu.SMEM),
            pl.BlockSpec(memory_space=pltpu.VMEM),
        ],
        out_specs=[pl.BlockSpec(memory_space=pltpu.VMEM)] * 4,
        out_shape=[jax.ShapeDtypeStruct((r // 2, w), F32)] * 4,
        scratch_shapes=[pltpu.VMEM((b, r, w), F32)],
        cost_estimate=cost(parts.size, 2 * parts.size),
        compiler_params=pltpu.CompilerParams(vmem_limit_bytes=8 << 20),
        name="sum_parts",
    )(where, parts)


def join_body(w_ref, own_ref, x_ref, c_ref, xc_ref, o_ref):
    block, c = lax.rem(w_ref[4], 2), w_ref[7]
    w = own_ref.shape[1]
    for ref, b, h in (
        (own_ref, block, c),
        (x_ref, 1 - block, c),
        (c_ref, block, 1 - c),
        (xc_ref, 1 - block, 1 - c),
    ):
        o_ref[:, pl.ds(pl.multiple_of((2 * b + h) * w, w), w)] = ref[...]


def shift(x, axis, by):
    n = lax.axis_size(axis)
    return lax.ppermute(x, axis, [((d + by) % n, d) for d in range(n)])


def layer(queries, keys, values, gain, out_weight, grad_out):
    tok_rows, feat_width = queries.shape[1:]
    model_width = grad_out.shape[2]
    q = queries.reshape(tok_rows, feat_width)
    k = keys.reshape(tok_rows, feat_width)
    v = values.reshape(tok_rows, feat_width)
    grad_rows = grad_out.reshape(tok_rows, model_width)
    gain_row = gain.reshape(1, feat_width)
    seqs = lax.axis_size("x")
    blocks_n = lax.axis_size(CTX)
    at_x = lax.axis_index("x")
    at_ctx = lax.axis_index(CTX)
    at_core = lax.axis_index("c")
    places = [at_x, lax.axis_index("z"), lax.axis_index("y"), at_core]
    order = [(at_x + n) % CH for n in range(CH)]
    where = jnp.stack(order + places).astype(jnp.int32)
    row_half = at_x // 2
    turns = [2 * row_half, 2 * row_half + 1, 2 - 2 * row_half, 3 - 2 * row_half]
    turns = jnp.stack(turns + places).astype(jnp.int32)
    mine = at_core.reshape(1).astype(jnp.int32)
    others = 1 - mine

    piece = out_weight.shape[0] // blocks_n
    own_piece = lax.dynamic_slice_in_dim(out_weight, at_ctx * piece, piece, 0)
    pieces = [shift(own_piece, "x", by) for by in range(1, CH)]
    state = local_state(k, v)
    half_cols = model_width // 2
    side = at_x % 2
    pieces, sent_rows, q_next = lax.optimization_barrier((pieces, grad_rows, q, state))[:3]
    near_cols = lax.dynamic_slice_in_dim(sent_rows, side * half_cols, half_cols, 1)
    far_cols = lax.dynamic_slice_in_dim(sent_rows, (1 - side) * half_cols, half_cols, 1)
    gathered = lax.all_gather(jnp.concatenate(pieces, axis=0), CTX, axis=0, tiled=True)
    gathered = gathered.reshape(blocks_n, CH - 1, piece, model_width)
    gathered = pltpu.with_memory_space_constraint(gathered, pltpu.HBM)
    own_weight = pltpu.with_memory_space_constraint(out_weight, pltpu.HBM)

    grads_all = [
        near_cols,
        partner(far_cols, "x", 1),
        partner(near_cols, "x", 2),
        partner(far_cols, "x", 3),
    ]

    carried, (weights, local_out), _, _ = carry(
        state,
        where,
        at_core,
        False,
        lambda sent: local_scores(after(q_next, sent), k, v),
        lambda sent, done: (),
        lambda sent, done: (),
    )
    near, far, attended = attend(turns, q, local_out, carried, gain_row)
    normed_all = [
        near,
        partner(near, "x", 1),
        partner(far, "x", 2),
        partner(far, "x", 3),
    ]
    gn = hbm(mm(after(sent_rows, near), out_weight, 1, 1))

    ga, lg = grad_attn(where, q, attended, gn, gain_row, hbm(grad_rows), gathered)
    chips = blocks_n // 2
    shape = (chips, 2, out_weight.shape[0] // chips, half_cols // 2)

    def first_half(sent):
        rows = after(normed_all, sent)
        return weight_half(give_body, others, rows, grads_all, shape, True)

    def second_half(sent, done):
        for_partner, turned = done
        extra = give_to(for_partner, "c", 1)
        return weight_half(
            keep_body, mine, [after(turned, sent), extra], grads_all, shape, False
        )

    def rest(sent, partial):
        parts = lax.all_to_all(partial, ("z", "y"), 0, 0, tiled=True)
        grads = local_grads(where, q, k, v, weights, after(ga, sent), carried)
        rows = layer_rows(where, near, after(far, grads), own_weight, gathered)
        return parts, (grads, rows)

    later, _, _, (parts, (grads, layer_out)) = carry(
        lg, where, at_core, True, first_half, second_half, rest
    )
    grad_query, pk, pv = grads
    grad_key, grad_value = later_grads(where, k, v, later, pk, pv)

    parts = after(parts, layer_out, later[0])
    token_count = seqs * blocks_n * tok_rows
    own, to_x, to_c, to_both = sum_parts(where, parts, 1.0 / math.sqrt(token_count))
    both = lax.ppermute(to_both, ("x", "c"), [(d, d ^ 3) for d in range(2 * seqs)])
    (grad_weight,) = small_call(
        join_body,
        where,
        [own, partner(to_x, "x", 1), partner(to_c, "c", 1), both],
        [jax.ShapeDtypeStruct((own.shape[0], model_width), F32)],
    )
    out_shape = (1, tok_rows, feat_width)
    return (
        layer_out.reshape(1, tok_rows, model_width),
        grad_query.reshape(out_shape),
        grad_key.reshape(out_shape),
        grad_value.reshape(out_shape),
        grad_weight,
    )


def solution(mesh):
    mesh = Mesh(mesh.devices.reshape(4, 4, 4, 2), ("x",) + CTX)
    tokens = P("x", CTX, None)
    in_specs = (tokens, tokens, tokens, P(), P("x", None), tokens)
    out_specs = (tokens, tokens, tokens, tokens, P(("x",) + CTX, None))
    return jax.shard_map(layer, mesh=mesh, in_specs=in_specs, out_specs=out_specs, check_vma=False)
```

```python
import functools
import math

import jax
import jax.numpy as jnp
from jax import lax
from jax.experimental import pallas as pl
from jax.experimental.pallas import tpu as pltpu
from jax.sharding import Mesh, PartitionSpec as P

HD = 128
EPSILON = 1e-06
BF = jnp.bfloat16
F32 = jnp.float32
CTX = ("z", "y", "c")
CH = 4
HC = 4


def mm(a, b, ca, cb):
    return lax.dot_general(a, b, (((ca,), (cb,)), ((), ())), preferred_element_type=F32)


def cost(flops, nbytes):
    return pl.CostEstimate(flops=flops, bytes_accessed=nbytes, transcendentals=0)


def head(ref, h):
    return ref[:, h * HD : (h + 1) * HD]


def causal(n):
    return lax.broadcasted_iota(jnp.int32, (n, n), 0) >= lax.broadcasted_iota(
        jnp.int32, (n, n), 1
    )


def state_body(k_ref, v_ref, s_ref):
    for h in range(HC):
        s_ref[h] = mm(head(k_ref, h), head(v_ref, h), 0, 0).astype(BF)


def local_state(k, v):
    t, f = k.shape
    w = f // CH
    blk = pl.BlockSpec((t, w), lambda g: (0, g))
    return pl.pallas_call(
        state_body,
        grid=(CH,),
        in_specs=[blk, blk],
        out_specs=pl.BlockSpec((HC, HD, HD), lambda g: (g, 0, 0)),
        out_shape=jax.ShapeDtypeStruct((CH * HC, HD, HD), BF),
        cost_estimate=cost(2 * t * f * HD, 4 * t * f),
        compiler_params=pltpu.CompilerParams(vmem_limit_bytes=6 << 20),
        name="local_state",
    )(k, v)


def small_call(body, where, args, outs):
    return pl.pallas_call(
        body,
        in_specs=[pl.BlockSpec(memory_space=pltpu.SMEM)]
        + [pl.BlockSpec(memory_space=pltpu.VMEM)] * len(args),
        out_specs=[pl.BlockSpec(memory_space=pltpu.VMEM)] * len(outs),
        out_shape=outs,
        compiler_params=pltpu.CompilerParams(vmem_limit_bytes=6 << 20),
        cost_estimate=cost(1 << 18, 1 << 20),
    )(where, *args)


def chip_body(w_ref, s_ref, r_ref, own_ref, *out_refs):
    y, c = w_ref[6], w_ref[7]
    n = s_ref.shape[1]
    for k in range(n):
        at = lax.rem(y + k, n)
        part = s_ref[c, at].astype(F32) + r_ref[at].astype(F32)
        if k == 0:
            own_ref[...] = part
        else:
            out_refs[k - 1][...] = part.astype(BF)


def row_body(w_ref, own_ref, *refs):
    total = own_ref[...]
    for ref in refs[:-1]:
        total = total + ref[...].astype(F32)
    refs[-1][...] = total.astype(BF)


def plane_body(reverse, w_ref, own_ref, t1, t2, t3, z1, z2, z3, o_ref, o1, o2, o3):
    z, y = w_ref[5], w_ref[6]
    terms = [own_ref[...]] + [t[...].astype(F32) for t in (t1, t2, t3)]
    n = len(terms)
    base = jnp.zeros_like(terms[0])
    for k, ref in enumerate((z1, z2, z3), 1):
        use = z < k if reverse else z >= k
        base = base + jnp.where(use, ref[...].astype(F32), 0.0)
    for k in range(n):
        to = lax.rem(y + k, n)
        total = base
        for j in range(n):
            source = lax.rem(y - j + n, n)
            use = source > to if reverse else source < to
            total = total + jnp.where(use, terms[j], 0.0)
        if k == 0:
            o_ref[...] = total
        else:
            (o1, o2, o3)[k - 1][...] = total.astype(BF)


def core_body(reverse, w_ref, s_ref, r_ref, p0, p1, p2, p3, mine_ref, give_ref):
    y, c = w_ref[6], w_ref[7]
    n = s_ref.shape[1]
    first = c == (1 if reverse else 0)
    for j, p in enumerate((p0, p1, p2, p3)):
        at = lax.rem(y - j + n, n)
        base = p[...].astype(F32)
        mine_ref[at] = (base + jnp.where(first, 0.0, r_ref[at].astype(F32))).astype(BF)
        give_ref[at] = (base + jnp.where(first, s_ref[c, at].astype(F32), 0.0)).astype(BF)


def partner(x, axis, bits):
    return lax.ppermute(x, axis, [(d, d ^ bits) for d in range(lax.axis_size(axis))])


def give_to(x, axis, by):
    n = lax.axis_size(axis)
    return lax.ppermute(x, axis, [(d, (d + by) % n) for d in range(n)])


def carry(state, where, core, reverse, fill_row, fill_plane, fill_core):
    heads, d, e = state.shape
    n = lax.axis_size("y")
    rows = heads * d // (2 * n)
    parts = state.reshape(2, n, rows, e)
    give = lax.dynamic_index_in_dim(parts, 1 - core, 0, False)
    other = give_to(give, "c", 1)
    one = jax.ShapeDtypeStruct((rows, e), F32)
    low = jax.ShapeDtypeStruct((rows, e), BF)
    half = jax.ShapeDtypeStruct((n, rows, e), BF)
    own, *out = small_call(chip_body, where, [parts, other], [one] + [low] * (n - 1))
    terms = [own] + [give_to(x, "y", k) for k, x in enumerate(out, 1)]
    filled_row = fill_row(out)
    terms = after(terms, filled_row)
    (row,) = small_call(row_body, where, terms, [low])
    rows_before = [give_to(row, "z", k) for k in range(1, n)]
    filled_plane = fill_plane(row, filled_row)
    rows_before = after(rows_before, filled_plane)
    own, *out = small_call(
        functools.partial(plane_body, reverse), where, terms + rows_before, [one] + [low] * (n - 1)
    )
    sums = [own] + [give_to(x, "y", k) for k, x in enumerate(out, 1)]
    filled_core = fill_core(out, filled_plane)
    sums = after(sums, filled_core[-1] if reverse else filled_core)
    mine, give = small_call(
        functools.partial(core_body, reverse), where, [parts, other] + sums, [half] * 2
    )
    got = give_to(give, "c", 1)
    shape = (heads // 2, d, e)
    return (mine.reshape(shape), got.reshape(shape)), filled_row, filled_plane, filled_core


def hbm(x):
    return pltpu.with_memory_space_constraint(x, pltpu.HBM)


def after(x, *others):
    return lax.optimization_barrier((x, others))[0]


def scores_body(q_ref, k_ref, v_ref, w_ref, o_ref):
    keep = causal(q_ref.shape[0])
    for h in range(HC):
        w = jnp.where(keep, mm(head(q_ref, h), head(k_ref, h), 1, 1), 0.0).astype(BF)
        w_ref[h] = w
        o_ref[:, h * HD : (h + 1) * HD] = mm(w, head(v_ref, h), 1, 0)


def local_scores(q, k, v):
    t, f = q.shape
    w = f // CH
    blk = pl.BlockSpec((t, w), lambda g: (0, g))
    return pl.pallas_call(
        scores_body,
        grid=(CH,),
        in_specs=[blk, blk, blk],
        out_specs=[pl.BlockSpec((HC, t, t), lambda g: (g, 0, 0)), blk],
        out_shape=[
            pltpu.HBM((CH * HC, t, t), BF),
            pltpu.HBM((t, f), F32),
        ],
        cost_estimate=cost(4 * t * t * f, 14 * t * f),
        compiler_params=pltpu.CompilerParams(vmem_limit_bytes=12 << 20),
        name="local_scores",
    )(q, k, v)


def pick(w_ref, chunk, m_ref, t_ref, h):
    return jnp.where(lax.div(chunk, CH // 2) == w_ref[7], m_ref[h], t_ref[h])


def attend_body(w_ref, q_ref, o_ref, m_ref, t_ref, g_ref, near_ref, far_ref, a_ref):
    g = pl.program_id(0)
    normed = []
    for h in range(HC):
        cols = slice(h * HD, (h + 1) * HD)
        state = pick(w_ref, w_ref[g], m_ref, t_ref, h)
        a = o_ref[:, cols] + mm(head(q_ref, h), state, 1, 0)
        a_ref[0, :, cols] = a
        inv = lax.rsqrt(jnp.mean(a * a, axis=-1, keepdims=True) + EPSILON)
        normed.append((a * inv * g_ref[:, cols]).astype(BF))
    normed = jnp.concatenate(normed, axis=1)

    @pl.when(g < CH // 2)
    def _():
        near_ref[...] = normed

    @pl.when(g >= CH // 2)
    def _():
        far_ref[...] = normed


def attend(where, q, out, carried, gain):
    t, f = q.shape
    w = f // CH
    two = CH // 2
    blk = pl.BlockSpec((t, w), lambda g, i: (0, i[g]))
    st = pl.BlockSpec((HC, HD, HD), lambda g, i: (lax.rem(i[g], two), 0, 0))
    return pl.pallas_call(
        attend_body,
        grid_spec=pltpu.PrefetchScalarGridSpec(
            num_scalar_prefetch=1,
            grid=(CH,),
            in_specs=[blk, blk, st, st, pl.BlockSpec((1, w), lambda g, i: (0, i[g]))],
            out_specs=[
                pl.BlockSpec((t, w), lambda g, i: (0, jnp.minimum(g, two - 1))),
                pl.BlockSpec((t, w), lambda g, i: (0, jnp.maximum(g - two, 0))),
                pl.BlockSpec((1, t, w), lambda g, i: (i[g], 0, 0)),
            ],
        ),
        out_shape=[jax.ShapeDtypeStruct((t, two * w), BF)] * 2
        + [pltpu.HBM((CH, t, w), F32)],
        cost_estimate=cost(2 * t * f * HD, 12 * t * f),
        compiler_params=pltpu.CompilerParams(vmem_limit_bytes=12 << 20),
        name="attend",
    )(where, q, out, *carried, gain)


PARTS = 1
SLOTS = 2


def grad_attn_body(
    i_ref, q_ref, a_ref, gn_ref, g_ref, go_hbm, w_hbm, ga_ref, lg_ref, go, w, go_sem, w_sem
):
    g = pl.program_id(0)
    _, blocks, rows, d = w.shape
    last = PARTS * (CH - 1)

    def load(t):
        at = pl.ds(lax.rem(t, PARTS) * blocks, blocks)
        slot = lax.rem(t, SLOTS)
        source = w_hbm.at[at, lax.div(t, PARTS)]
        return pltpu.make_async_copy(source, w.at[slot], w_sem.at[slot])

    whole = pltpu.make_async_copy(go_hbm, go, go_sem)

    def finish(gn):
        for h in range(HC // PARTS):
            cols = slice(h * HD, (h + 1) * HD)
            a = a_ref[0, :, cols]
            inv = lax.rsqrt(jnp.mean(a * a, axis=-1, keepdims=True) + EPSILON)
            unit = a * inv
            gu = gn[:, cols] * g_ref[:, cols]
            ga = inv * (gu - unit * jnp.mean(gu * unit, axis=-1, keepdims=True))
            ga = ga.astype(BF)
            ga_ref[0, :, cols] = ga
            lg_ref[h] = mm(head(q_ref, h), ga, 0, 0).astype(BF)

    @pl.when(g == 0)
    def _():
        whole.start()
        load(0).start()

    @pl.when(g < PARTS)
    def _():
        finish(gn_ref[...])

    @pl.when(g == PARTS)
    def _():
        whole.wait()

    @pl.when(g >= PARTS)
    def _():
        t = g - PARTS
        load(t).wait()

        @pl.when(t + 1 < last)
        def _():
            load(t + 1).start()

        finish(mm(go[...], w[lax.rem(t, SLOTS)].reshape(blocks * rows, d), 1, 1))


def grad_attn(order, q, attended, gn, gain, grad_rows, gathered):
    t, f = q.shape
    w = f // CH // PARTS
    n, _, r, d = gathered.shape

    def nat(g, i):
        return (0, i[lax.div(g, PARTS)] * PARTS + lax.rem(g, PARTS))

    return pl.pallas_call(
        grad_attn_body,
        grid_spec=pltpu.PrefetchScalarGridSpec(
            num_scalar_prefetch=1,
            grid=(CH * PARTS,),
            in_specs=[
                pl.BlockSpec((t, w), nat),
                pl.BlockSpec(
                    (1, t, w), lambda g, i: (i[lax.div(g, PARTS)], 0, lax.rem(g, PARTS))
                ),
                pl.BlockSpec((t, w), lambda g, i: (0, jnp.minimum(g, PARTS - 1))),
                pl.BlockSpec((1, w), nat),
                pl.BlockSpec(memory_space=pltpu.HBM),
                pl.BlockSpec(memory_space=pltpu.HBM),
            ],
            out_specs=[
                pl.BlockSpec((1, t, w), lambda g, i: (lax.div(g, PARTS), 0, lax.rem(g, PARTS))),
                pl.BlockSpec((HC // PARTS, HD, HD), lambda g, i: (g, 0, 0)),
            ],
            scratch_shapes=[
                pltpu.VMEM((t, d), BF),
                pltpu.VMEM((SLOTS, n // PARTS, r, d), BF),
                pltpu.SemaphoreType.DMA(()),
                pltpu.SemaphoreType.DMA((SLOTS,)),
            ],
        ),
        out_shape=[
            pltpu.HBM((CH, t, f // CH), BF),
            jax.ShapeDtypeStruct((CH * HC, HD, HD), BF),
        ],
        cost_estimate=cost(2 * t * f * HD + 6 * t * w * d, 12 * t * f + 6 * w * d),
        compiler_params=pltpu.CompilerParams(vmem_limit_bytes=26 << 20),
        name="grad_attn",
    )(order, q, attended, gn, gain, grad_rows, gathered)


def grads_body(i_ref, q_ref, k_ref, v_ref, w_ref, ga_ref, m_ref, t_ref, gq_ref, gk_ref, gv_ref):
    chunk = i_ref[pl.program_id(0)]
    keep = causal(q_ref.shape[0])
    for h in range(HC):
        cols = slice(h * HD, (h + 1) * HD)
        ga = ga_ref[0, :, cols]
        gs = jnp.where(keep, mm(ga, head(v_ref, h), 1, 1), 0.0).astype(BF)
        gq = mm(gs, head(k_ref, h), 1, 0) + mm(ga, pick(i_ref, chunk, m_ref, t_ref, h), 1, 1)
        gq_ref[:, cols] = gq.astype(BF)
        gk_ref[0, :, cols] = mm(gs, head(q_ref, h), 0, 0)
        gv_ref[0, :, cols] = mm(w_ref[h], ga, 0, 0)


def local_grads(order, q, k, v, weights, ga, carried):
    t, f = q.shape
    w = f // CH
    nat = pl.BlockSpec((t, w), lambda g, i: (0, i[g]))
    chunk = pl.BlockSpec((1, t, w), lambda g, i: (g, 0, 0))
    return pl.pallas_call(
        grads_body,
        grid_spec=pltpu.PrefetchScalarGridSpec(
            num_scalar_prefetch=1,
            grid=(CH,),
            in_specs=[
                nat,
                nat,
                nat,
                pl.BlockSpec((HC, t, t), lambda g, i: (i[g], 0, 0)),
                chunk,
            ]
            + [pl.BlockSpec((HC, HD, HD), lambda g, i: (lax.rem(i[g], CH // 2), 0, 0))] * 2,
            out_specs=[nat, chunk, chunk],
        ),
        out_shape=[
            jax.ShapeDtypeStruct((t, f), BF),
            pltpu.HBM((CH, t, w), F32),
            pltpu.HBM((CH, t, w), F32),
        ],
        cost_estimate=cost(8 * t * t * f, 24 * t * f),
        compiler_params=pltpu.CompilerParams(vmem_limit_bytes=20 << 20),
        name="local_grads",
    )(order, q, k, v, weights, ga, *carried)


def later_body(i_ref, k_ref, v_ref, m_ref, t_ref, pk_ref, pv_ref, gk_ref, gv_ref):
    for h in range(HC):
        cols = slice(h * HD, (h + 1) * HD)
        state = pick(i_ref, pl.program_id(0), m_ref, t_ref, h)
        gk = pk_ref[0, :, cols] + mm(head(v_ref, h), state, 1, 1)
        gv = pv_ref[0, :, cols] + mm(head(k_ref, h), state, 1, 0)
        gk_ref[:, cols] = gk.astype(BF)
        gv_ref[:, cols] = gv.astype(BF)


def later_grads(order, k, v, later, pk, pv):
    t, f = k.shape
    w = f // CH
    nat = pl.BlockSpec((t, w), lambda g, i: (0, i[g]))
    chunk = pl.BlockSpec((1, t, w), lambda g, i: (g, 0, 0))
    return pl.pallas_call(
        later_body,
        grid_spec=pltpu.PrefetchScalarGridSpec(
            num_scalar_prefetch=1,
            grid=(CH,),
            in_specs=[
                nat,
                nat,
                pl.BlockSpec((HC, HD, HD), lambda g, i: (lax.rem(g, CH // 2), 0, 0)),
                pl.BlockSpec((HC, HD, HD), lambda g, i: (lax.rem(g, CH // 2), 0, 0)),
                chunk,
                chunk,
            ],
            out_specs=[nat, nat],
        ),
        out_shape=[jax.ShapeDtypeStruct((t, f), BF)] * 2,
        cost_estimate=cost(4 * t * f * HD, 16 * t * f),
        compiler_params=pltpu.CompilerParams(vmem_limit_bytes=12 << 20),
        name="later_grads",
    )(order, k, v, *later, pk, pv)


def layer_body(i_ref, near_ref, far_ref, own_ref, w_ref, o_ref):
    w = own_ref.shape[0]
    mine = lax.div(i_ref[4], CH // 2)
    total = None
    for k in range(CH):
        chunk = i_ref[k]
        cols = pl.ds(pl.multiple_of(lax.rem(chunk, CH // 2) * w, w), w)
        is_near = lax.div(chunk, CH // 2) == mine
        rows = jnp.where(is_near, near_ref[:, cols], far_ref[:, cols])
        block = own_ref[...] if k == 0 else w_ref[:, k - 1].reshape(own_ref.shape)
        part = mm(rows, block, 1, 0)
        total = part if total is None else total + part
    o_ref[...] = total.astype(BF)


def layer_rows(where, near, far, own, gathered):
    t = near.shape[0]
    w = own.shape[0]
    n, c, r, d = gathered.shape
    tile = 1024
    half = pl.BlockSpec(near.shape, lambda g, i: (0, 0))
    return pl.pallas_call(
        layer_body,
        grid_spec=pltpu.PrefetchScalarGridSpec(
            num_scalar_prefetch=1,
            grid=(d // tile,),
            in_specs=[
                half,
                half,
                pl.BlockSpec((w, tile), lambda g, i: (0, g)),
                pl.BlockSpec((n, c, r, tile), lambda g, i: (0, 0, 0, g)),
            ],
            out_specs=pl.BlockSpec((t, tile), lambda g, i: (0, g)),
        ),
        out_shape=jax.ShapeDtypeStruct((t, d), BF),
        cost_estimate=cost(2 * t * CH * w * d, 2 * (CH * w * d + CH * t * w + t * d)),
        compiler_params=pltpu.CompilerParams(vmem_limit_bytes=20 << 20),
        name="layer_rows",
    )(where, near, far, own, gathered)


def weight_total(nt, grads, o_ref, extra_ref):
    total = mm(nt[...], jnp.concatenate([g[...] for g in grads], axis=0), 1, 0)
    chips, blocks, rows, w = o_ref.shape
    span = chips * rows
    for b in range(blocks):
        one = total[b * span : (b + 1) * span].reshape(chips, rows, w)
        if extra_ref is not None:
            one = one + extra_ref[:, b].astype(F32)
        o_ref[:, b] = one.astype(BF)


def give_body(i_ref, n0, n1, n2, n3, *rest):
    *grads, o_ref, nt_ref = rest

    @pl.when(pl.program_id(0) == 0)
    def _():
        t = n0.shape[0]
        for s, n in enumerate((n0, n1, n2, n3)):
            nt_ref[:, s * t : (s + 1) * t] = n[...].T

    weight_total(nt_ref, grads, o_ref, None)


def keep_body(i_ref, nt_ref, extra_ref, *rest):
    *grads, o_ref = rest
    weight_total(nt_ref, grads, o_ref, extra_ref)


def weight_half(body, half, rows, grads_all, shape, nt_out):
    t, d = grads_all[0].shape
    w = rows[0].shape[1] if nt_out else rows[0].shape[0]
    tile = 256
    steps = d // 2 // tile
    own = pl.BlockSpec(shape[:-1] + (tile,), lambda g, i: (0, 0, 0, g))
    whole = pl.BlockSpec((t, w), lambda g, i: (0, 0))
    turned = pl.BlockSpec((w, CH * t), lambda g, i: (0, 0))
    out = pltpu.HBM(shape, BF)
    cols = pl.BlockSpec((t, tile), lambda g, i: (0, i[0] * steps + g))
    return pl.pallas_call(
        body,
        grid_spec=pltpu.PrefetchScalarGridSpec(
            num_scalar_prefetch=1,
            grid=(steps,),
            in_specs=([whole] * CH if nt_out else [turned, own]) + [cols] * CH,
            out_specs=[own, turned] if nt_out else own,
        ),
        out_shape=[out, jax.ShapeDtypeStruct((w, CH * t), BF)] if nt_out else out,
        cost_estimate=cost(CH * t * w * d, 2 * CH * t * d + 2 * CH * t * w + w * d),
        compiler_params=pltpu.CompilerParams(vmem_limit_bytes=20 << 20),
        name="weight_half",
    )(half, *rows, *grads_all)


def sum_body(scale, w_ref, s_ref, keep_ref, x_ref, c_ref, xc_ref, total):
    acc = s_ref[0].astype(F32)
    for step in range(1, s_ref.shape[0]):
        acc = acc + s_ref[step].astype(F32)
    total[...] = acc * scale
    rows = keep_ref.shape[0]
    block, c = lax.rem(w_ref[4], 2), w_ref[7]
    mine = pl.ds(pl.multiple_of(c * rows, rows), rows)
    other = pl.ds(pl.multiple_of((1 - c) * rows, rows), rows)
    keep_ref[...] = total[block, mine]
    x_ref[...] = total[1 - block, mine]
    c_ref[...] = total[block, other]
    xc_ref[...] = total[1 - block, other]


def sum_parts(where, parts, scale):
    _, b, r, w = parts.shape
    return pl.pallas_call(
        functools.partial(sum_body, scale),
        in_specs=[
            pl.BlockSpec(memory_space=pltpu.SMEM),
            pl.BlockSpec(memory_space=pltpu.VMEM),
        ],
        out_specs=[pl.BlockSpec(memory_space=pltpu.VMEM)] * 4,
        out_shape=[jax.ShapeDtypeStruct((r // 2, w), F32)] * 4,
        scratch_shapes=[pltpu.VMEM((b, r, w), F32)],
        cost_estimate=cost(parts.size, 2 * parts.size),
        compiler_params=pltpu.CompilerParams(vmem_limit_bytes=8 << 20),
        name="sum_parts",
    )(where, parts)


def join_body(w_ref, own_ref, x_ref, c_ref, xc_ref, o_ref):
    block, c = lax.rem(w_ref[4], 2), w_ref[7]
    w = own_ref.shape[1]
    for ref, b, h in (
        (own_ref, block, c),
        (x_ref, 1 - block, c),
        (c_ref, block, 1 - c),
        (xc_ref, 1 - block, 1 - c),
    ):
        o_ref[:, pl.ds(pl.multiple_of((2 * b + h) * w, w), w)] = ref[...]


def shift(x, axis, by):
    n = lax.axis_size(axis)
    return lax.ppermute(x, axis, [((d + by) % n, d) for d in range(n)])


def layer(queries, keys, values, gain, out_weight, grad_out):
    tok_rows, feat_width = queries.shape[1:]
    model_width = grad_out.shape[2]
    q = queries.reshape(tok_rows, feat_width)
    k = keys.reshape(tok_rows, feat_width)
    v = values.reshape(tok_rows, feat_width)
    grad_rows = grad_out.reshape(tok_rows, model_width)
    gain_row = gain.reshape(1, feat_width)
    seqs = lax.axis_size("x")
    blocks_n = lax.axis_size(CTX)
    at_x = lax.axis_index("x")
    at_ctx = lax.axis_index(CTX)
    at_core = lax.axis_index("c")
    places = [at_x, lax.axis_index("z"), lax.axis_index("y"), at_core]
    order = [(at_x + n) % CH for n in range(CH)]
    where = jnp.stack(order + places).astype(jnp.int32)
    row_half = at_x // 2
    turns = [2 * row_half, 2 * row_half + 1, 2 - 2 * row_half, 3 - 2 * row_half]
    turns = jnp.stack(turns + places).astype(jnp.int32)
    mine = at_core.reshape(1).astype(jnp.int32)
    others = 1 - mine

    piece = out_weight.shape[0] // blocks_n
    own_piece = lax.dynamic_slice_in_dim(out_weight, at_ctx * piece, piece, 0)
    pieces = [shift(own_piece, "x", by) for by in range(1, CH)]
    state = local_state(k, v)
    half_cols = model_width // 2
    side = at_x % 2
    pieces, sent_rows, q_next = lax.optimization_barrier((pieces, grad_rows, q, state))[:3]
    near_cols = lax.dynamic_slice_in_dim(sent_rows, side * half_cols, half_cols, 1)
    far_cols = lax.dynamic_slice_in_dim(sent_rows, (1 - side) * half_cols, half_cols, 1)
    gathered = lax.all_gather(jnp.concatenate(pieces, axis=0), CTX, axis=0, tiled=True)
    gathered = gathered.reshape(blocks_n, CH - 1, piece, model_width)
    gathered = pltpu.with_memory_space_constraint(gathered, pltpu.HBM)
    own_weight = pltpu.with_memory_space_constraint(out_weight, pltpu.HBM)

    grads_all = [
        near_cols,
        partner(far_cols, "x", 1),
        partner(near_cols, "x", 2),
        partner(far_cols, "x", 3),
    ]

    carried, (weights, local_out), _, _ = carry(
        state,
        where,
        at_core,
        False,
        lambda sent: local_scores(after(q_next, sent), k, v),
        lambda sent, done: (),
        lambda sent, done: (),
    )
    near, far, attended = attend(turns, q, hbm(local_out), carried, gain_row)
    normed_all = [
        near,
        partner(near, "x", 1),
        partner(far, "x", 2),
        partner(far, "x", 3),
    ]
    gn = hbm(mm(after(sent_rows, near), out_weight, 1, 1))

    ga, lg = grad_attn(where, q, hbm(attended), gn, gain_row, hbm(grad_rows), gathered)
    chips = blocks_n // 2
    shape = (chips, 2, out_weight.shape[0] // chips, half_cols // 2)

    def first_half(sent):
        rows = after(normed_all, sent)
        return weight_half(give_body, others, rows, grads_all, shape, True)

    def second_half(sent, done):
        for_partner, turned = done
        extra = give_to(for_partner, "c", 1)
        return weight_half(keep_body, mine, [after(turned, sent), extra], grads_all, shape, False)

    def rest(sent, partial):
        parts = lax.all_to_all(partial, ("z", "y"), 0, 0, tiled=True)
        grads = local_grads(where, q, k, v, hbm(weights), hbm(after(ga, sent)), carried)
        rows = layer_rows(where, near, after(far, grads), own_weight, gathered)
        return parts, (grads, rows)

    later, _, _, (parts, (grads, layer_out)) = carry(
        lg, where, at_core, True, first_half, second_half, rest
    )
    grad_query, pk, pv = grads
    grad_key, grad_value = later_grads(where, k, v, later, hbm(pk), hbm(pv))

    parts = after(parts, layer_out, later[0])
    token_count = seqs * blocks_n * tok_rows
    own, to_x, to_c, to_both = sum_parts(where, parts, 1.0 / math.sqrt(token_count))
    both = lax.ppermute(to_both, ("x", "c"), [(d, d ^ 3) for d in range(2 * seqs)])
    (grad_weight,) = small_call(
        join_body,
        where,
        [own, partner(to_x, "x", 1), partner(to_c, "c", 1), both],
        [jax.ShapeDtypeStruct((own.shape[0], model_width), F32)],
    )
    out_shape = (1, tok_rows, feat_width)
    return (
        layer_out.reshape(1, tok_rows, model_width),
        grad_query.reshape(out_shape),
        grad_key.reshape(out_shape),
        grad_value.reshape(out_shape),
        grad_weight,
    )


def solution(mesh):
    mesh = Mesh(mesh.devices.reshape(4, 4, 4, 2), ("x",) + CTX)
    tokens = P("x", CTX, None)
    in_specs = (tokens, tokens, tokens, P(), P("x", None), tokens)
    out_specs = (tokens, tokens, tokens, tokens, P(("x",) + CTX, None))
    return jax.shard_map(layer, mesh=mesh, in_specs=in_specs, out_specs=out_specs, check_vma=False)
```

```python
import functools
import math

import jax
import jax.numpy as jnp
from jax import lax
from jax.experimental import pallas as pl
from jax.experimental.pallas import tpu as pltpu
from jax.sharding import Mesh, PartitionSpec as P

HD = 128
EPSILON = 1e-06
BF = jnp.bfloat16
F32 = jnp.float32
CTX = ("z", "y", "c")
CH = 4
HC = 4


def mm(a, b, ca, cb):
    return lax.dot_general(a, b, (((ca,), (cb,)), ((), ())), preferred_element_type=F32)


def cost(flops, nbytes):
    return pl.CostEstimate(flops=flops, bytes_accessed=nbytes, transcendentals=0)


def head(ref, h):
    return ref[:, h * HD : (h + 1) * HD]


def causal(n):
    return lax.broadcasted_iota(jnp.int32, (n, n), 0) >= lax.broadcasted_iota(
        jnp.int32, (n, n), 1
    )


def state_body(k_ref, v_ref, s_ref):
    for h in range(HC):
        s_ref[h] = mm(head(k_ref, h), head(v_ref, h), 0, 0).astype(BF)


def local_state(k, v):
    t, f = k.shape
    w = f // CH
    blk = pl.BlockSpec((t, w), lambda g: (0, g))
    return pl.pallas_call(
        state_body,
        grid=(CH,),
        in_specs=[blk, blk],
        out_specs=pl.BlockSpec((HC, HD, HD), lambda g: (g, 0, 0)),
        out_shape=jax.ShapeDtypeStruct((CH * HC, HD, HD), BF),
        cost_estimate=cost(2 * t * f * HD, 4 * t * f),
        compiler_params=pltpu.CompilerParams(vmem_limit_bytes=6 << 20),
        name="local_state",
    )(k, v)


def small_call(body, where, args, outs):
    return pl.pallas_call(
        body,
        in_specs=[pl.BlockSpec(memory_space=pltpu.SMEM)]
        + [pl.BlockSpec(memory_space=pltpu.VMEM)] * len(args),
        out_specs=[pl.BlockSpec(memory_space=pltpu.VMEM)] * len(outs),
        out_shape=outs,
        compiler_params=pltpu.CompilerParams(vmem_limit_bytes=6 << 20),
        cost_estimate=cost(1 << 18, 1 << 20),
    )(where, *args)


def chip_body(w_ref, s_ref, r_ref, own_ref, *out_refs):
    y, c = w_ref[6], w_ref[7]
    n = s_ref.shape[1]
    for k in range(n):
        at = lax.rem(y + k, n)
        part = s_ref[c, at].astype(F32) + r_ref[at].astype(F32)
        if k == 0:
            own_ref[...] = part
        else:
            out_refs[k - 1][...] = part.astype(BF)


def row_body(w_ref, own_ref, *refs):
    total = own_ref[...]
    for ref in refs[:-1]:
        total = total + ref[...].astype(F32)
    refs[-1][...] = total.astype(BF)


def plane_body(reverse, w_ref, own_ref, t1, t2, t3, z1, z2, z3, o_ref, o1, o2, o3):
    z, y = w_ref[5], w_ref[6]
    terms = [own_ref[...]] + [t[...].astype(F32) for t in (t1, t2, t3)]
    n = len(terms)
    base = jnp.zeros_like(terms[0])
    for k, ref in enumerate((z1, z2, z3), 1):
        use = z < k if reverse else z >= k
        base = base + jnp.where(use, ref[...].astype(F32), 0.0)
    for k in range(n):
        to = lax.rem(y + k, n)
        total = base
        for j in range(n):
            source = lax.rem(y - j + n, n)
            use = source > to if reverse else source < to
            total = total + jnp.where(use, terms[j], 0.0)
        if k == 0:
            o_ref[...] = total
        else:
            (o1, o2, o3)[k - 1][...] = total.astype(BF)


def core_body(reverse, w_ref, s_ref, r_ref, p0, p1, p2, p3, mine_ref, give_ref):
    y, c = w_ref[6], w_ref[7]
    n = s_ref.shape[1]
    first = c == (1 if reverse else 0)
    for j, p in enumerate((p0, p1, p2, p3)):
        at = lax.rem(y - j + n, n)
        base = p[...].astype(F32)
        mine_ref[at] = (base + jnp.where(first, 0.0, r_ref[at].astype(F32))).astype(BF)
        give_ref[at] = (base + jnp.where(first, s_ref[c, at].astype(F32), 0.0)).astype(BF)


def partner(x, axis, bits):
    return lax.ppermute(x, axis, [(d, d ^ bits) for d in range(lax.axis_size(axis))])


def give_to(x, axis, by):
    n = lax.axis_size(axis)
    return lax.ppermute(x, axis, [(d, (d + by) % n) for d in range(n)])


def carry(state, where, core, reverse, fill_row, fill_plane, fill_core):
    heads, d, e = state.shape
    n = lax.axis_size("y")
    rows = heads * d // (2 * n)
    parts = state.reshape(2, n, rows, e)
    give = lax.dynamic_index_in_dim(parts, 1 - core, 0, False)
    other = give_to(give, "c", 1)
    one = jax.ShapeDtypeStruct((rows, e), F32)
    low = jax.ShapeDtypeStruct((rows, e), BF)
    half = jax.ShapeDtypeStruct((n, rows, e), BF)
    own, *out = small_call(chip_body, where, [parts, other], [one] + [low] * (n - 1))
    terms = [own] + [give_to(x, "y", k) for k, x in enumerate(out, 1)]
    filled_row = fill_row(out)
    terms = after(terms, filled_row)
    (row,) = small_call(row_body, where, terms, [low])
    rows_before = [give_to(row, "z", k) for k in range(1, n)]
    filled_plane = fill_plane(row, filled_row)
    rows_before = after(rows_before, filled_plane)
    own, *out = small_call(
        functools.partial(plane_body, reverse), where, terms + rows_before, [one] + [low] * (n - 1)
    )
    sums = [own] + [give_to(x, "y", k) for k, x in enumerate(out, 1)]
    filled_core = fill_core(out, filled_plane)
    sums = after(sums, filled_core[-1] if reverse else filled_core)
    mine, give = small_call(
        functools.partial(core_body, reverse), where, [parts, other] + sums, [half] * 2
    )
    got = give_to(give, "c", 1)
    shape = (heads // 2, d, e)
    return (mine.reshape(shape), got.reshape(shape)), filled_row, filled_plane, filled_core


def hbm(x):
    return pltpu.with_memory_space_constraint(x, pltpu.HBM)


def after(x, *others):
    return lax.optimization_barrier((x, others))[0]


def scores_body(q_ref, k_ref, v_ref, w_ref, o_ref):
    keep = causal(q_ref.shape[0])
    for h in range(HC):
        w = jnp.where(keep, mm(head(q_ref, h), head(k_ref, h), 1, 1), 0.0).astype(BF)
        w_ref[h] = w
        o_ref[:, h * HD : (h + 1) * HD] = mm(w, head(v_ref, h), 1, 0)


def local_scores(q, k, v):
    t, f = q.shape
    w = f // CH
    blk = pl.BlockSpec((t, w), lambda g: (0, g))
    return pl.pallas_call(
        scores_body,
        grid=(CH,),
        in_specs=[blk, blk, blk],
        out_specs=[pl.BlockSpec((HC, t, t), lambda g: (g, 0, 0)), blk],
        out_shape=[
            pltpu.HBM((CH * HC, t, t), BF),
            pltpu.HBM((t, f), F32),
        ],
        cost_estimate=cost(4 * t * t * f, 14 * t * f),
        compiler_params=pltpu.CompilerParams(vmem_limit_bytes=12 << 20),
        name="local_scores",
    )(q, k, v)


def pick(w_ref, chunk, m_ref, t_ref, h):
    return jnp.where(lax.div(chunk, CH // 2) == w_ref[7], m_ref[h], t_ref[h])


def attend_body(w_ref, q_ref, o_ref, m_ref, t_ref, g_ref, near_ref, far_ref, a_ref):
    g = pl.program_id(0)
    normed = []
    for h in range(HC):
        cols = slice(h * HD, (h + 1) * HD)
        state = pick(w_ref, w_ref[g], m_ref, t_ref, h)
        a = o_ref[:, cols] + mm(head(q_ref, h), state, 1, 0)
        a_ref[0, :, cols] = a
        inv = lax.rsqrt(jnp.mean(a * a, axis=-1, keepdims=True) + EPSILON)
        normed.append((a * inv * g_ref[:, cols]).astype(BF))
    normed = jnp.concatenate(normed, axis=1)

    @pl.when(g < CH // 2)
    def _():
        near_ref[...] = normed

    @pl.when(g >= CH // 2)
    def _():
        far_ref[...] = normed


def attend(where, q, out, carried, gain):
    t, f = q.shape
    w = f // CH
    two = CH // 2
    blk = pl.BlockSpec((t, w), lambda g, i: (0, i[g]))
    st = pl.BlockSpec((HC, HD, HD), lambda g, i: (lax.rem(i[g], two), 0, 0))
    return pl.pallas_call(
        attend_body,
        grid_spec=pltpu.PrefetchScalarGridSpec(
            num_scalar_prefetch=1,
            grid=(CH,),
            in_specs=[blk, blk, st, st, pl.BlockSpec((1, w), lambda g, i: (0, i[g]))],
            out_specs=[
                pl.BlockSpec((t, w), lambda g, i: (0, jnp.minimum(g, two - 1))),
                pl.BlockSpec((t, w), lambda g, i: (0, jnp.maximum(g - two, 0))),
                pl.BlockSpec((1, t, w), lambda g, i: (i[g], 0, 0)),
            ],
        ),
        out_shape=[jax.ShapeDtypeStruct((t, two * w), BF)] * 2
        + [pltpu.HBM((CH, t, w), F32)],
        cost_estimate=cost(2 * t * f * HD, 12 * t * f),
        compiler_params=pltpu.CompilerParams(vmem_limit_bytes=12 << 20),
        name="attend",
    )(where, q, out, *carried, gain)


PARTS = 1
SLOTS = 2


def grad_attn_body(
    i_ref, q_ref, a_ref, gn_ref, g_ref, go_hbm, w_hbm, ga_ref, lg_ref, go, w, go_sem, w_sem
):
    g = pl.program_id(0)
    _, blocks, rows, d = w.shape
    last = PARTS * (CH - 1)

    def load(t):
        at = pl.ds(lax.rem(t, PARTS) * blocks, blocks)
        slot = lax.rem(t, SLOTS)
        source = w_hbm.at[at, lax.div(t, PARTS)]
        return pltpu.make_async_copy(source, w.at[slot], w_sem.at[slot])

    whole = pltpu.make_async_copy(go_hbm, go, go_sem)

    def finish(gn):
        for h in range(HC // PARTS):
            cols = slice(h * HD, (h + 1) * HD)
            a = a_ref[0, :, cols]
            inv = lax.rsqrt(jnp.mean(a * a, axis=-1, keepdims=True) + EPSILON)
            unit = a * inv
            gu = gn[:, cols] * g_ref[:, cols]
            ga = inv * (gu - unit * jnp.mean(gu * unit, axis=-1, keepdims=True))
            ga = ga.astype(BF)
            ga_ref[0, :, cols] = ga
            lg_ref[h] = mm(head(q_ref, h), ga, 0, 0).astype(BF)

    @pl.when(g == 0)
    def _():
        whole.start()
        load(0).start()

    @pl.when(g < PARTS)
    def _():
        finish(gn_ref[...])

    @pl.when(g == PARTS)
    def _():
        whole.wait()

    @pl.when(g >= PARTS)
    def _():
        t = g - PARTS
        load(t).wait()

        @pl.when(t + 1 < last)
        def _():
            load(t + 1).start()

        finish(mm(go[...], w[lax.rem(t, SLOTS)].reshape(blocks * rows, d), 1, 1))


def grad_attn(order, q, attended, gn, gain, grad_rows, gathered):
    t, f = q.shape
    w = f // CH // PARTS
    n, _, r, d = gathered.shape

    def nat(g, i):
        return (0, i[lax.div(g, PARTS)] * PARTS + lax.rem(g, PARTS))

    return pl.pallas_call(
        grad_attn_body,
        grid_spec=pltpu.PrefetchScalarGridSpec(
            num_scalar_prefetch=1,
            grid=(CH * PARTS,),
            in_specs=[
                pl.BlockSpec((t, w), nat),
                pl.BlockSpec(
                    (1, t, w), lambda g, i: (i[lax.div(g, PARTS)], 0, lax.rem(g, PARTS))
                ),
                pl.BlockSpec((t, w), lambda g, i: (0, jnp.minimum(g, PARTS - 1))),
                pl.BlockSpec((1, w), nat),
                pl.BlockSpec(memory_space=pltpu.HBM),
                pl.BlockSpec(memory_space=pltpu.HBM),
            ],
            out_specs=[
                pl.BlockSpec((1, t, w), lambda g, i: (lax.div(g, PARTS), 0, lax.rem(g, PARTS))),
                pl.BlockSpec((HC // PARTS, HD, HD), lambda g, i: (g, 0, 0)),
            ],
            scratch_shapes=[
                pltpu.VMEM((t, d), BF),
                pltpu.VMEM((SLOTS, n // PARTS, r, d), BF),
                pltpu.SemaphoreType.DMA(()),
                pltpu.SemaphoreType.DMA((SLOTS,)),
            ],
        ),
        out_shape=[
            pltpu.HBM((CH, t, f // CH), BF),
            jax.ShapeDtypeStruct((CH * HC, HD, HD), BF),
        ],
        cost_estimate=cost(2 * t * f * HD + 6 * t * w * d, 12 * t * f + 6 * w * d),
        compiler_params=pltpu.CompilerParams(vmem_limit_bytes=26 << 20),
        name="grad_attn",
    )(order, q, attended, gn, gain, grad_rows, gathered)


def grads_body(i_ref, q_ref, k_ref, v_ref, w_ref, ga_ref, m_ref, t_ref, gq_ref, gk_ref, gv_ref):
    chunk = i_ref[pl.program_id(0)]
    keep = causal(q_ref.shape[0])
    for h in range(HC):
        cols = slice(h * HD, (h + 1) * HD)
        ga = ga_ref[0, :, cols]
        gs = jnp.where(keep, mm(ga, head(v_ref, h), 1, 1), 0.0).astype(BF)
        gq = mm(gs, head(k_ref, h), 1, 0) + mm(ga, pick(i_ref, chunk, m_ref, t_ref, h), 1, 1)
        gq_ref[:, cols] = gq.astype(BF)
        gk_ref[0, :, cols] = mm(gs, head(q_ref, h), 0, 0).astype(BF)
        gv_ref[0, :, cols] = mm(w_ref[h], ga, 0, 0).astype(BF)


def local_grads(order, q, k, v, weights, ga, carried):
    t, f = q.shape
    w = f // CH
    nat = pl.BlockSpec((t, w), lambda g, i: (0, i[g]))
    chunk = pl.BlockSpec((1, t, w), lambda g, i: (g, 0, 0))
    return pl.pallas_call(
        grads_body,
        grid_spec=pltpu.PrefetchScalarGridSpec(
            num_scalar_prefetch=1,
            grid=(CH,),
            in_specs=[
                nat,
                nat,
                nat,
                pl.BlockSpec((HC, t, t), lambda g, i: (i[g], 0, 0)),
                chunk,
            ]
            + [pl.BlockSpec((HC, HD, HD), lambda g, i: (lax.rem(i[g], CH // 2), 0, 0))] * 2,
            out_specs=[nat, chunk, chunk],
        ),
        out_shape=[
            jax.ShapeDtypeStruct((t, f), BF),
            jax.ShapeDtypeStruct((CH, t, w), BF),
            jax.ShapeDtypeStruct((CH, t, w), BF),
        ],
        cost_estimate=cost(8 * t * t * f, 24 * t * f),
        compiler_params=pltpu.CompilerParams(vmem_limit_bytes=20 << 20),
        name="local_grads",
    )(order, q, k, v, weights, ga, *carried)


def later_body(i_ref, k_ref, v_ref, m_ref, t_ref, pk_ref, pv_ref, gk_ref, gv_ref):
    for h in range(HC):
        cols = slice(h * HD, (h + 1) * HD)
        state = pick(i_ref, pl.program_id(0), m_ref, t_ref, h)
        gk = pk_ref[0, :, cols].astype(F32) + mm(head(v_ref, h), state, 1, 1)
        gv = pv_ref[0, :, cols].astype(F32) + mm(head(k_ref, h), state, 1, 0)
        gk_ref[:, cols] = gk.astype(BF)
        gv_ref[:, cols] = gv.astype(BF)


def later_grads(order, k, v, later, pk, pv):
    t, f = k.shape
    w = f // CH
    nat = pl.BlockSpec((t, w), lambda g, i: (0, i[g]))
    chunk = pl.BlockSpec((1, t, w), lambda g, i: (g, 0, 0))
    return pl.pallas_call(
        later_body,
        grid_spec=pltpu.PrefetchScalarGridSpec(
            num_scalar_prefetch=1,
            grid=(CH,),
            in_specs=[
                nat,
                nat,
                pl.BlockSpec((HC, HD, HD), lambda g, i: (lax.rem(g, CH // 2), 0, 0)),
                pl.BlockSpec((HC, HD, HD), lambda g, i: (lax.rem(g, CH // 2), 0, 0)),
                chunk,
                chunk,
            ],
            out_specs=[nat, nat],
        ),
        out_shape=[jax.ShapeDtypeStruct((t, f), BF)] * 2,
        cost_estimate=cost(4 * t * f * HD, 16 * t * f),
        compiler_params=pltpu.CompilerParams(vmem_limit_bytes=12 << 20),
        name="later_grads",
    )(order, k, v, *later, pk, pv)


def layer_body(i_ref, near_ref, far_ref, own_ref, w_ref, o_ref):
    w = own_ref.shape[0]
    mine = lax.div(i_ref[4], CH // 2)
    total = None
    for k in range(CH):
        chunk = i_ref[k]
        cols = pl.ds(pl.multiple_of(lax.rem(chunk, CH // 2) * w, w), w)
        is_near = lax.div(chunk, CH // 2) == mine
        rows = jnp.where(is_near, near_ref[:, cols], far_ref[:, cols])
        block = own_ref[...] if k == 0 else w_ref[:, k - 1].reshape(own_ref.shape)
        part = mm(rows, block, 1, 0)
        total = part if total is None else total + part
    o_ref[...] = total.astype(BF)


def layer_rows(where, near, far, own, gathered):
    t = near.shape[0]
    w = own.shape[0]
    n, c, r, d = gathered.shape
    tile = 1024
    half = pl.BlockSpec(near.shape, lambda g, i: (0, 0))
    return pl.pallas_call(
        layer_body,
        grid_spec=pltpu.PrefetchScalarGridSpec(
            num_scalar_prefetch=1,
            grid=(d // tile,),
            in_specs=[
                half,
                half,
                pl.BlockSpec((w, tile), lambda g, i: (0, g)),
                pl.BlockSpec((n, c, r, tile), lambda g, i: (0, 0, 0, g)),
            ],
            out_specs=pl.BlockSpec((t, tile), lambda g, i: (0, g)),
        ),
        out_shape=jax.ShapeDtypeStruct((t, d), BF),
        cost_estimate=cost(2 * t * CH * w * d, 2 * (CH * w * d + CH * t * w + t * d)),
        compiler_params=pltpu.CompilerParams(vmem_limit_bytes=20 << 20),
        name="layer_rows",
    )(where, near, far, own, gathered)


def weight_total(nt, grads, o_ref, extra_ref):
    total = mm(nt[...], jnp.concatenate([g[...] for g in grads], axis=0), 1, 0)
    chips, blocks, rows, w = o_ref.shape
    span = chips * rows
    for b in range(blocks):
        one = total[b * span : (b + 1) * span].reshape(chips, rows, w)
        if extra_ref is not None:
            one = one + extra_ref[:, b].astype(F32)
        o_ref[:, b] = one.astype(BF)


def give_body(i_ref, n0, n1, n2, n3, *rest):
    *grads, o_ref, nt_ref = rest

    @pl.when(pl.program_id(0) == 0)
    def _():
        t = n0.shape[0]
        for s, n in enumerate((n0, n1, n2, n3)):
            nt_ref[:, s * t : (s + 1) * t] = n[...].T

    weight_total(nt_ref, grads, o_ref, None)


def keep_body(i_ref, nt_ref, extra_ref, *rest):
    *grads, o_ref = rest
    weight_total(nt_ref, grads, o_ref, extra_ref)


def weight_half(body, half, rows, grads_all, shape, nt_out):
    t, d = grads_all[0].shape
    w = rows[0].shape[1] if nt_out else rows[0].shape[0]
    tile = 256
    steps = d // 2 // tile
    own = pl.BlockSpec(shape[:-1] + (tile,), lambda g, i: (0, 0, 0, g))
    whole = pl.BlockSpec((t, w), lambda g, i: (0, 0))
    turned = pl.BlockSpec((w, CH * t), lambda g, i: (0, 0))
    out = pltpu.HBM(shape, BF)
    cols = pl.BlockSpec((t, tile), lambda g, i: (0, i[0] * steps + g))
    return pl.pallas_call(
        body,
        grid_spec=pltpu.PrefetchScalarGridSpec(
            num_scalar_prefetch=1,
            grid=(steps,),
            in_specs=([whole] * CH if nt_out else [turned, own]) + [cols] * CH,
            out_specs=[own, turned] if nt_out else own,
        ),
        out_shape=[out, jax.ShapeDtypeStruct((w, CH * t), BF)] if nt_out else out,
        cost_estimate=cost(CH * t * w * d, 2 * CH * t * d + 2 * CH * t * w + w * d),
        compiler_params=pltpu.CompilerParams(vmem_limit_bytes=20 << 20),
        name="weight_half",
    )(half, *rows, *grads_all)


def sum_body(scale, w_ref, s_ref, keep_ref, x_ref, c_ref, xc_ref, total):
    acc = s_ref[0].astype(F32)
    for step in range(1, s_ref.shape[0]):
        acc = acc + s_ref[step].astype(F32)
    total[...] = acc * scale
    rows = keep_ref.shape[0]
    block, c = lax.rem(w_ref[4], 2), w_ref[7]
    mine = pl.ds(pl.multiple_of(c * rows, rows), rows)
    other = pl.ds(pl.multiple_of((1 - c) * rows, rows), rows)
    keep_ref[...] = total[block, mine]
    x_ref[...] = total[1 - block, mine]
    c_ref[...] = total[block, other]
    xc_ref[...] = total[1 - block, other]


def sum_parts(where, parts, scale):
    _, b, r, w = parts.shape
    return pl.pallas_call(
        functools.partial(sum_body, scale),
        in_specs=[
            pl.BlockSpec(memory_space=pltpu.SMEM),
            pl.BlockSpec(memory_space=pltpu.VMEM),
        ],
        out_specs=[pl.BlockSpec(memory_space=pltpu.VMEM)] * 4,
        out_shape=[jax.ShapeDtypeStruct((r // 2, w), F32)] * 4,
        scratch_shapes=[pltpu.VMEM((b, r, w), F32)],
        cost_estimate=cost(parts.size, 2 * parts.size),
        compiler_params=pltpu.CompilerParams(vmem_limit_bytes=8 << 20),
        name="sum_parts",
    )(where, parts)


def join_body(w_ref, own_ref, x_ref, c_ref, xc_ref, o_ref):
    block, c = lax.rem(w_ref[4], 2), w_ref[7]
    w = own_ref.shape[1]
    for ref, b, h in (
        (own_ref, block, c),
        (x_ref, 1 - block, c),
        (c_ref, block, 1 - c),
        (xc_ref, 1 - block, 1 - c),
    ):
        o_ref[:, pl.ds(pl.multiple_of((2 * b + h) * w, w), w)] = ref[...]


def shift(x, axis, by):
    n = lax.axis_size(axis)
    return lax.ppermute(x, axis, [((d + by) % n, d) for d in range(n)])


def layer(queries, keys, values, gain, out_weight, grad_out):
    tok_rows, feat_width = queries.shape[1:]
    model_width = grad_out.shape[2]
    q = queries.reshape(tok_rows, feat_width)
    k = keys.reshape(tok_rows, feat_width)
    v = values.reshape(tok_rows, feat_width)
    grad_rows = grad_out.reshape(tok_rows, model_width)
    gain_row = gain.reshape(1, feat_width)
    seqs = lax.axis_size("x")
    blocks_n = lax.axis_size(CTX)
    at_x = lax.axis_index("x")
    at_ctx = lax.axis_index(CTX)
    at_core = lax.axis_index("c")
    places = [at_x, lax.axis_index("z"), lax.axis_index("y"), at_core]
    order = [(at_x + n) % CH for n in range(CH)]
    where = jnp.stack(order + places).astype(jnp.int32)
    row_half = at_x // 2
    turns = [2 * row_half, 2 * row_half + 1, 2 - 2 * row_half, 3 - 2 * row_half]
    turns = jnp.stack(turns + places).astype(jnp.int32)
    mine = at_core.reshape(1).astype(jnp.int32)
    others = 1 - mine

    piece = out_weight.shape[0] // blocks_n
    own_piece = lax.dynamic_slice_in_dim(out_weight, at_ctx * piece, piece, 0)
    pieces = [shift(own_piece, "x", by) for by in range(1, CH)]
    state = local_state(k, v)
    half_cols = model_width // 2
    side = at_x % 2
    pieces, sent_rows, q_next = lax.optimization_barrier((pieces, grad_rows, q, state))[:3]
    near_cols = lax.dynamic_slice_in_dim(sent_rows, side * half_cols, half_cols, 1)
    far_cols = lax.dynamic_slice_in_dim(sent_rows, (1 - side) * half_cols, half_cols, 1)
    gathered = lax.all_gather(jnp.concatenate(pieces, axis=0), CTX, axis=0, tiled=True)
    gathered = gathered.reshape(blocks_n, CH - 1, piece, model_width)
    gathered = pltpu.with_memory_space_constraint(gathered, pltpu.HBM)
    own_weight = pltpu.with_memory_space_constraint(out_weight, pltpu.HBM)

    grads_all = [
        near_cols,
        partner(far_cols, "x", 1),
        partner(near_cols, "x", 2),
        partner(far_cols, "x", 3),
    ]

    carried, (weights, local_out), _, _ = carry(
        state,
        where,
        at_core,
        False,
        lambda sent: local_scores(after(q_next, sent), k, v),
        lambda sent, done: (),
        lambda sent, done: (),
    )
    near, far, attended = attend(turns, q, hbm(local_out), carried, gain_row)
    normed_all = [
        near,
        partner(near, "x", 1),
        partner(far, "x", 2),
        partner(far, "x", 3),
    ]
    gn = hbm(mm(after(sent_rows, near), out_weight, 1, 1))

    ga, lg = grad_attn(where, q, hbm(attended), gn, gain_row, hbm(grad_rows), gathered)
    chips = blocks_n // 2
    shape = (chips, 2, out_weight.shape[0] // chips, half_cols // 2)

    def first_half(sent):
        rows = after(normed_all, sent)
        return weight_half(give_body, others, rows, grads_all, shape, True)

    def second_half(sent, done):
        for_partner, turned = done
        extra = give_to(for_partner, "c", 1)
        return weight_half(keep_body, mine, [after(turned, sent), extra], grads_all, shape, False)

    def rest(sent, partial):
        parts = lax.all_to_all(partial, ("z", "y"), 0, 0, tiled=True)
        grads = local_grads(where, q, k, v, hbm(weights), hbm(after(ga, sent)), carried)
        rows = layer_rows(where, near, after(far, grads), own_weight, gathered)
        return parts, (grads, rows)

    later, _, _, (parts, (grads, layer_out)) = carry(
        lg, where, at_core, True, first_half, second_half, rest
    )
    grad_query, pk, pv = grads
    grad_key, grad_value = later_grads(where, k, v, later, pk, pv)

    parts = after(parts, layer_out, later[0])
    token_count = seqs * blocks_n * tok_rows
    own, to_x, to_c, to_both = sum_parts(where, parts, 1.0 / math.sqrt(token_count))
    both = lax.ppermute(to_both, ("x", "c"), [(d, d ^ 3) for d in range(2 * seqs)])
    (grad_weight,) = small_call(
        join_body,
        where,
        [own, partner(to_x, "x", 1), partner(to_c, "c", 1), both],
        [jax.ShapeDtypeStruct((own.shape[0], model_width), F32)],
    )
    out_shape = (1, tok_rows, feat_width)
    return (
        layer_out.reshape(1, tok_rows, model_width),
        grad_query.reshape(out_shape),
        grad_key.reshape(out_shape),
        grad_value.reshape(out_shape),
        grad_weight,
    )


def solution(mesh):
    mesh = Mesh(mesh.devices.reshape(4, 4, 4, 2), ("x",) + CTX)
    tokens = P("x", CTX, None)
    in_specs = (tokens, tokens, tokens, P(), P("x", None), tokens)
    out_specs = (tokens, tokens, tokens, tokens, P(("x",) + CTX, None))
    return jax.shard_map(layer, mesh=mesh, in_specs=in_specs, out_specs=out_specs, check_vma=False)
```

```python
import functools
import math

import jax
import jax.numpy as jnp
from jax import lax
from jax.experimental import pallas as pl
from jax.experimental.pallas import tpu as pltpu
from jax.sharding import Mesh, PartitionSpec as P

HD = 128
EPSILON = 1e-06
BF = jnp.bfloat16
F32 = jnp.float32
CTX = ("z", "y", "c")
CH = 4
HC = 4


def mm(a, b, ca, cb):
    return lax.dot_general(a, b, (((ca,), (cb,)), ((), ())), preferred_element_type=F32)


def cost(flops, nbytes):
    return pl.CostEstimate(flops=flops, bytes_accessed=nbytes, transcendentals=0)


def head(ref, h):
    return ref[:, h * HD : (h + 1) * HD]


def causal(n):
    return lax.broadcasted_iota(jnp.int32, (n, n), 0) >= lax.broadcasted_iota(
        jnp.int32, (n, n), 1
    )


def state_body(k_ref, v_ref, s_ref):
    for h in range(HC):
        s_ref[h] = mm(head(k_ref, h), head(v_ref, h), 0, 0).astype(BF)


def local_state(k, v):
    t, f = k.shape
    w = f // CH
    blk = pl.BlockSpec((t, w), lambda g: (0, g))
    return pl.pallas_call(
        state_body,
        grid=(CH,),
        in_specs=[blk, blk],
        out_specs=pl.BlockSpec((HC, HD, HD), lambda g: (g, 0, 0)),
        out_shape=jax.ShapeDtypeStruct((CH * HC, HD, HD), BF),
        cost_estimate=cost(2 * t * f * HD, 4 * t * f),
        compiler_params=pltpu.CompilerParams(vmem_limit_bytes=6 << 20),
        name="local_state",
    )(k, v)


def small_call(body, where, args, outs):
    return pl.pallas_call(
        body,
        in_specs=[pl.BlockSpec(memory_space=pltpu.SMEM)]
        + [pl.BlockSpec(memory_space=pltpu.VMEM)] * len(args),
        out_specs=[pl.BlockSpec(memory_space=pltpu.VMEM)] * len(outs),
        out_shape=outs,
        compiler_params=pltpu.CompilerParams(vmem_limit_bytes=6 << 20),
        cost_estimate=cost(1 << 18, 1 << 20),
    )(where, *args)


def chip_body(w_ref, s_ref, r_ref, own_ref, *out_refs):
    y, c = w_ref[6], w_ref[7]
    n = s_ref.shape[1]
    for k in range(n):
        at = lax.rem(y + k, n)
        part = s_ref[c, at].astype(F32) + r_ref[at].astype(F32)
        if k == 0:
            own_ref[...] = part
        else:
            out_refs[k - 1][...] = part.astype(BF)


def row_body(w_ref, own_ref, *refs):
    total = own_ref[...]
    for ref in refs[:-1]:
        total = total + ref[...].astype(F32)
    refs[-1][...] = total.astype(BF)


def plane_body(reverse, w_ref, own_ref, t1, t2, t3, z1, z2, z3, o_ref, o1, o2, o3):
    z, y = w_ref[5], w_ref[6]
    terms = [own_ref[...]] + [t[...].astype(F32) for t in (t1, t2, t3)]
    n = len(terms)
    base = jnp.zeros_like(terms[0])
    for k, ref in enumerate((z1, z2, z3), 1):
        use = z < k if reverse else z >= k
        base = base + jnp.where(use, ref[...].astype(F32), 0.0)
    for k in range(n):
        to = lax.rem(y + k, n)
        total = base
        for j in range(n):
            source = lax.rem(y - j + n, n)
            use = source > to if reverse else source < to
            total = total + jnp.where(use, terms[j], 0.0)
        if k == 0:
            o_ref[...] = total
        else:
            (o1, o2, o3)[k - 1][...] = total.astype(BF)


def core_body(reverse, w_ref, s_ref, r_ref, p0, p1, p2, p3, mine_ref, give_ref):
    y, c = w_ref[6], w_ref[7]
    n = s_ref.shape[1]
    first = c == (1 if reverse else 0)
    for j, p in enumerate((p0, p1, p2, p3)):
        at = lax.rem(y - j + n, n)
        base = p[...].astype(F32)
        mine_ref[at] = (base + jnp.where(first, 0.0, r_ref[at].astype(F32))).astype(BF)
        give_ref[at] = (base + jnp.where(first, s_ref[c, at].astype(F32), 0.0)).astype(BF)


def partner(x, axis, bits):
    return lax.ppermute(x, axis, [(d, d ^ bits) for d in range(lax.axis_size(axis))])


def give_to(x, axis, by):
    n = lax.axis_size(axis)
    return lax.ppermute(x, axis, [(d, (d + by) % n) for d in range(n)])


def carry(state, where, core, reverse, fill_row, fill_plane, fill_core):
    heads, d, e = state.shape
    n = lax.axis_size("y")
    rows = heads * d // (2 * n)
    parts = state.reshape(2, n, rows, e)
    give = lax.dynamic_index_in_dim(parts, 1 - core, 0, False)
    other = give_to(give, "c", 1)
    one = jax.ShapeDtypeStruct((rows, e), F32)
    low = jax.ShapeDtypeStruct((rows, e), BF)
    half = jax.ShapeDtypeStruct((n, rows, e), BF)
    own, *out = small_call(chip_body, where, [parts, other], [one] + [low] * (n - 1))
    terms = [own] + [give_to(x, "y", k) for k, x in enumerate(out, 1)]
    filled_row = fill_row(out)
    terms = after(terms, filled_row)
    (row,) = small_call(row_body, where, terms, [low])
    rows_before = [give_to(row, "z", k) for k in range(1, n)]
    filled_plane = fill_plane(row, filled_row)
    rows_before = after(rows_before, filled_plane)
    own, *out = small_call(
        functools.partial(plane_body, reverse), where, terms + rows_before, [one] + [low] * (n - 1)
    )
    sums = [own] + [give_to(x, "y", k) for k, x in enumerate(out, 1)]
    filled_core = fill_core(out, filled_plane)
    sums = after(sums, filled_core[-1] if reverse else filled_core)
    mine, give = small_call(
        functools.partial(core_body, reverse), where, [parts, other] + sums, [half] * 2
    )
    got = give_to(give, "c", 1)
    shape = (heads // 2, d, e)
    return (mine.reshape(shape), got.reshape(shape)), filled_row, filled_plane, filled_core


def hbm(x):
    return pltpu.with_memory_space_constraint(x, pltpu.HBM)


def after(x, *others):
    return lax.optimization_barrier((x, others))[0]


def scores_body(q_ref, k_ref, v_ref, w_ref, o_ref):
    keep = causal(q_ref.shape[0])
    for h in range(HC):
        w = jnp.where(keep, mm(head(q_ref, h), head(k_ref, h), 1, 1), 0.0).astype(BF)
        w_ref[h] = w
        o_ref[:, h * HD : (h + 1) * HD] = mm(w, head(v_ref, h), 1, 0)


def local_scores(q, k, v):
    t, f = q.shape
    w = f // CH
    blk = pl.BlockSpec((t, w), lambda g: (0, g))
    return pl.pallas_call(
        scores_body,
        grid=(CH,),
        in_specs=[blk, blk, blk],
        out_specs=[pl.BlockSpec((HC, t, t), lambda g: (g, 0, 0)), blk],
        out_shape=[
            pltpu.HBM((CH * HC, t, t), BF),
            pltpu.HBM((t, f), F32),
        ],
        cost_estimate=cost(4 * t * t * f, 14 * t * f),
        compiler_params=pltpu.CompilerParams(vmem_limit_bytes=12 << 20),
        name="local_scores",
    )(q, k, v)


def pick(w_ref, chunk, m_ref, t_ref, h):
    return jnp.where(lax.div(chunk, CH // 2) == w_ref[7], m_ref[h], t_ref[h])


def attend_body(w_ref, q_ref, o_ref, m_ref, t_ref, g_ref, near_ref, far_ref, near_t_ref, far_t_ref, a_ref):
    g = pl.program_id(0)
    normed = []
    for h in range(HC):
        cols = slice(h * HD, (h + 1) * HD)
        state = pick(w_ref, w_ref[g], m_ref, t_ref, h)
        a = o_ref[:, cols] + mm(head(q_ref, h), state, 1, 0)
        a_ref[0, :, cols] = a
        inv = lax.rsqrt(jnp.mean(a * a, axis=-1, keepdims=True) + EPSILON)
        normed.append((a * inv * g_ref[:, cols]).astype(BF))
    normed = jnp.concatenate(normed, axis=1)

    @pl.when(g < CH // 2)
    def _():
        near_ref[...] = normed
        near_t_ref[...] = normed.T

    @pl.when(g >= CH // 2)
    def _():
        far_ref[...] = normed
        far_t_ref[...] = normed.T


def attend(where, q, out, carried, gain):
    t, f = q.shape
    w = f // CH
    two = CH // 2
    blk = pl.BlockSpec((t, w), lambda g, i: (0, i[g]))
    st = pl.BlockSpec((HC, HD, HD), lambda g, i: (lax.rem(i[g], two), 0, 0))
    return pl.pallas_call(
        attend_body,
        grid_spec=pltpu.PrefetchScalarGridSpec(
            num_scalar_prefetch=1,
            grid=(CH,),
            in_specs=[blk, blk, st, st, pl.BlockSpec((1, w), lambda g, i: (0, i[g]))],
            out_specs=[
                pl.BlockSpec((t, w), lambda g, i: (0, jnp.minimum(g, two - 1))),
                pl.BlockSpec((t, w), lambda g, i: (0, jnp.maximum(g - two, 0))),
                pl.BlockSpec((w, t), lambda g, i: (jnp.minimum(g, two - 1), 0)),
                pl.BlockSpec((w, t), lambda g, i: (jnp.maximum(g - two, 0), 0)),
                pl.BlockSpec((1, t, w), lambda g, i: (i[g], 0, 0)),
            ],
        ),
        out_shape=[jax.ShapeDtypeStruct((t, two * w), BF)] * 2
        + [jax.ShapeDtypeStruct((two * w, t), BF)] * 2
        + [pltpu.HBM((CH, t, w), F32)],
        cost_estimate=cost(2 * t * f * HD, 12 * t * f),
        compiler_params=pltpu.CompilerParams(vmem_limit_bytes=12 << 20),
        name="attend",
    )(where, q, out, *carried, gain)


PARTS = 1
SLOTS = 2


def grad_attn_body(
    i_ref, q_ref, a_ref, gn_ref, g_ref, go_hbm, w_hbm, ga_ref, lg_ref, go, w, go_sem, w_sem
):
    g = pl.program_id(0)
    _, blocks, rows, d = w.shape
    last = PARTS * (CH - 1)

    def load(t):
        at = pl.ds(lax.rem(t, PARTS) * blocks, blocks)
        slot = lax.rem(t, SLOTS)
        source = w_hbm.at[at, lax.div(t, PARTS)]
        return pltpu.make_async_copy(source, w.at[slot], w_sem.at[slot])

    whole = pltpu.make_async_copy(go_hbm, go, go_sem)

    def finish(gn):
        for h in range(HC // PARTS):
            cols = slice(h * HD, (h + 1) * HD)
            a = a_ref[0, :, cols]
            inv = lax.rsqrt(jnp.mean(a * a, axis=-1, keepdims=True) + EPSILON)
            unit = a * inv
            gu = gn[:, cols] * g_ref[:, cols]
            ga = inv * (gu - unit * jnp.mean(gu * unit, axis=-1, keepdims=True))
            ga = ga.astype(BF)
            ga_ref[0, :, cols] = ga
            lg_ref[h] = mm(head(q_ref, h), ga, 0, 0).astype(BF)

    @pl.when(g == 0)
    def _():
        whole.start()
        load(0).start()

    @pl.when(g < PARTS)
    def _():
        finish(gn_ref[...])

    @pl.when(g == PARTS)
    def _():
        whole.wait()

    @pl.when(g >= PARTS)
    def _():
        t = g - PARTS
        load(t).wait()

        @pl.when(t + 1 < last)
        def _():
            load(t + 1).start()

        finish(mm(go[...], w[lax.rem(t, SLOTS)].reshape(blocks * rows, d), 1, 1))


def grad_attn(order, q, attended, gn, gain, grad_rows, gathered):
    t, f = q.shape
    w = f // CH // PARTS
    n, _, r, d = gathered.shape

    def nat(g, i):
        return (0, i[lax.div(g, PARTS)] * PARTS + lax.rem(g, PARTS))

    return pl.pallas_call(
        grad_attn_body,
        grid_spec=pltpu.PrefetchScalarGridSpec(
            num_scalar_prefetch=1,
            grid=(CH * PARTS,),
            in_specs=[
                pl.BlockSpec((t, w), nat),
                pl.BlockSpec(
                    (1, t, w), lambda g, i: (i[lax.div(g, PARTS)], 0, lax.rem(g, PARTS))
                ),
                pl.BlockSpec((t, w), lambda g, i: (0, jnp.minimum(g, PARTS - 1))),
                pl.BlockSpec((1, w), nat),
                pl.BlockSpec(memory_space=pltpu.HBM),
                pl.BlockSpec(memory_space=pltpu.HBM),
            ],
            out_specs=[
                pl.BlockSpec((1, t, w), lambda g, i: (lax.div(g, PARTS), 0, lax.rem(g, PARTS))),
                pl.BlockSpec((HC // PARTS, HD, HD), lambda g, i: (g, 0, 0)),
            ],
            scratch_shapes=[
                pltpu.VMEM((t, d), BF),
                pltpu.VMEM((SLOTS, n // PARTS, r, d), BF),
                pltpu.SemaphoreType.DMA(()),
                pltpu.SemaphoreType.DMA((SLOTS,)),
            ],
        ),
        out_shape=[
            pltpu.HBM((CH, t, f // CH), BF),
            jax.ShapeDtypeStruct((CH * HC, HD, HD), BF),
        ],
        cost_estimate=cost(2 * t * f * HD + 6 * t * w * d, 12 * t * f + 6 * w * d),
        compiler_params=pltpu.CompilerParams(vmem_limit_bytes=26 << 20),
        name="grad_attn",
    )(order, q, attended, gn, gain, grad_rows, gathered)


def grads_body(i_ref, q_ref, k_ref, v_ref, w_ref, ga_ref, m_ref, t_ref, gq_ref, gk_ref, gv_ref):
    chunk = i_ref[pl.program_id(0)]
    keep = causal(q_ref.shape[0])
    for h in range(HC):
        cols = slice(h * HD, (h + 1) * HD)
        ga = ga_ref[0, :, cols]
        gs = jnp.where(keep, mm(ga, head(v_ref, h), 1, 1), 0.0).astype(BF)
        gq = mm(gs, head(k_ref, h), 1, 0) + mm(ga, pick(i_ref, chunk, m_ref, t_ref, h), 1, 1)
        gq_ref[:, cols] = gq.astype(BF)
        gk_ref[0, :, cols] = mm(gs, head(q_ref, h), 0, 0)
        gv_ref[0, :, cols] = mm(w_ref[h], ga, 0, 0)


def local_grads(order, q, k, v, weights, ga, carried):
    t, f = q.shape
    w = f // CH
    nat = pl.BlockSpec((t, w), lambda g, i: (0, i[g]))
    chunk = pl.BlockSpec((1, t, w), lambda g, i: (g, 0, 0))
    return pl.pallas_call(
        grads_body,
        grid_spec=pltpu.PrefetchScalarGridSpec(
            num_scalar_prefetch=1,
            grid=(CH,),
            in_specs=[
                nat,
                nat,
                nat,
                pl.BlockSpec((HC, t, t), lambda g, i: (i[g], 0, 0)),
                chunk,
            ]
            + [pl.BlockSpec((HC, HD, HD), lambda g, i: (lax.rem(i[g], CH // 2), 0, 0))] * 2,
            out_specs=[nat, chunk, chunk],
        ),
        out_shape=[
            jax.ShapeDtypeStruct((t, f), BF),
            pltpu.HBM((CH, t, w), F32),
            pltpu.HBM((CH, t, w), F32),
        ],
        cost_estimate=cost(8 * t * t * f, 24 * t * f),
        compiler_params=pltpu.CompilerParams(vmem_limit_bytes=20 << 20),
        name="local_grads",
    )(order, q, k, v, weights, ga, *carried)


def later_body(i_ref, k_ref, v_ref, m_ref, t_ref, pk_ref, pv_ref, gk_ref, gv_ref):
    for h in range(HC):
        cols = slice(h * HD, (h + 1) * HD)
        state = pick(i_ref, pl.program_id(0), m_ref, t_ref, h)
        gk = pk_ref[0, :, cols] + mm(head(v_ref, h), state, 1, 1)
        gv = pv_ref[0, :, cols] + mm(head(k_ref, h), state, 1, 0)
        gk_ref[:, cols] = gk.astype(BF)
        gv_ref[:, cols] = gv.astype(BF)


def later_grads(order, k, v, later, pk, pv):
    t, f = k.shape
    w = f // CH
    nat = pl.BlockSpec((t, w), lambda g, i: (0, i[g]))
    chunk = pl.BlockSpec((1, t, w), lambda g, i: (g, 0, 0))
    return pl.pallas_call(
        later_body,
        grid_spec=pltpu.PrefetchScalarGridSpec(
            num_scalar_prefetch=1,
            grid=(CH,),
            in_specs=[
                nat,
                nat,
                pl.BlockSpec((HC, HD, HD), lambda g, i: (lax.rem(g, CH // 2), 0, 0)),
                pl.BlockSpec((HC, HD, HD), lambda g, i: (lax.rem(g, CH // 2), 0, 0)),
                chunk,
                chunk,
            ],
            out_specs=[nat, nat],
        ),
        out_shape=[jax.ShapeDtypeStruct((t, f), BF)] * 2,
        cost_estimate=cost(4 * t * f * HD, 16 * t * f),
        compiler_params=pltpu.CompilerParams(vmem_limit_bytes=12 << 20),
        name="later_grads",
    )(order, k, v, *later, pk, pv)


def layer_body(i_ref, near_ref, far_ref, own_ref, w_ref, o_ref):
    w = own_ref.shape[0]
    mine = lax.div(i_ref[4], CH // 2)
    total = None
    for k in range(CH):
        chunk = i_ref[k]
        cols = pl.ds(pl.multiple_of(lax.rem(chunk, CH // 2) * w, w), w)
        is_near = lax.div(chunk, CH // 2) == mine
        rows = jnp.where(is_near, near_ref[:, cols], far_ref[:, cols])
        block = own_ref[...] if k == 0 else w_ref[:, k - 1].reshape(own_ref.shape)
        part = mm(rows, block, 1, 0)
        total = part if total is None else total + part
    o_ref[...] = total.astype(BF)


def layer_rows(where, near, far, own, gathered):
    t = near.shape[0]
    w = own.shape[0]
    n, c, r, d = gathered.shape
    tile = 1024
    half = pl.BlockSpec(near.shape, lambda g, i: (0, 0))
    return pl.pallas_call(
        layer_body,
        grid_spec=pltpu.PrefetchScalarGridSpec(
            num_scalar_prefetch=1,
            grid=(d // tile,),
            in_specs=[
                half,
                half,
                pl.BlockSpec((w, tile), lambda g, i: (0, g)),
                pl.BlockSpec((n, c, r, tile), lambda g, i: (0, 0, 0, g)),
            ],
            out_specs=pl.BlockSpec((t, tile), lambda g, i: (0, g)),
        ),
        out_shape=jax.ShapeDtypeStruct((t, d), BF),
        cost_estimate=cost(2 * t * CH * w * d, 2 * (CH * w * d + CH * t * w + t * d)),
        compiler_params=pltpu.CompilerParams(vmem_limit_bytes=20 << 20),
        name="layer_rows",
    )(where, near, far, own, gathered)


def weight_body(add, i_ref, *refs):
    rows, grads = refs[:CH], refs[CH : 2 * CH]
    o_ref = refs[-1]
    left = jnp.concatenate([n[...] for n in rows], axis=1)
    total = mm(left, jnp.concatenate([g[...] for g in grads], axis=0), 1, 0)
    chips, blocks, r, w = o_ref.shape
    span = chips * r
    for b in range(blocks):
        one = total[b * span : (b + 1) * span].reshape(chips, r, w)
        if add:
            one = one + refs[2 * CH][:, b].astype(F32)
        o_ref[:, b] = one.astype(BF)


def weight_half(half, rows, grads_all, shape, extra):
    t, d = grads_all[0].shape
    w = rows[0].shape[0]
    tile = 256
    steps = d // 2 // tile
    add = extra is not None
    own = pl.BlockSpec(shape[:-1] + (tile,), lambda g, i: (0, 0, 0, g))
    whole = pl.BlockSpec((w, t), lambda g, i: (0, 0))
    cols = pl.BlockSpec((t, tile), lambda g, i: (0, i[0] * steps + g))
    return pl.pallas_call(
        functools.partial(weight_body, add),
        grid_spec=pltpu.PrefetchScalarGridSpec(
            num_scalar_prefetch=1,
            grid=(steps,),
            in_specs=[whole] * CH + [cols] * CH + [own] * add,
            out_specs=own,
        ),
        out_shape=pltpu.HBM(shape, BF),
        cost_estimate=cost(CH * t * w * d, 2 * CH * t * d + 2 * CH * t * w + w * d),
        compiler_params=pltpu.CompilerParams(vmem_limit_bytes=20 << 20),
        name="weight_half",
    )(half, *rows, *grads_all, *([extra] if add else []))


def sum_body(scale, w_ref, s_ref, keep_ref, x_ref, c_ref, xc_ref, total):
    acc = s_ref[0].astype(F32)
    for step in range(1, s_ref.shape[0]):
        acc = acc + s_ref[step].astype(F32)
    total[...] = acc * scale
    rows = keep_ref.shape[0]
    block, c = lax.rem(w_ref[4], 2), w_ref[7]
    mine = pl.ds(pl.multiple_of(c * rows, rows), rows)
    other = pl.ds(pl.multiple_of((1 - c) * rows, rows), rows)
    keep_ref[...] = total[block, mine]
    x_ref[...] = total[1 - block, mine]
    c_ref[...] = total[block, other]
    xc_ref[...] = total[1 - block, other]


def sum_parts(where, parts, scale):
    _, b, r, w = parts.shape
    return pl.pallas_call(
        functools.partial(sum_body, scale),
        in_specs=[
            pl.BlockSpec(memory_space=pltpu.SMEM),
            pl.BlockSpec(memory_space=pltpu.VMEM),
        ],
        out_specs=[pl.BlockSpec(memory_space=pltpu.VMEM)] * 4,
        out_shape=[jax.ShapeDtypeStruct((r // 2, w), F32)] * 4,
        scratch_shapes=[pltpu.VMEM((b, r, w), F32)],
        cost_estimate=cost(parts.size, 2 * parts.size),
        compiler_params=pltpu.CompilerParams(vmem_limit_bytes=8 << 20),
        name="sum_parts",
    )(where, parts)


def join_body(w_ref, own_ref, x_ref, c_ref, xc_ref, o_ref):
    block, c = lax.rem(w_ref[4], 2), w_ref[7]
    w = own_ref.shape[1]
    for ref, b, h in (
        (own_ref, block, c),
        (x_ref, 1 - block, c),
        (c_ref, block, 1 - c),
        (xc_ref, 1 - block, 1 - c),
    ):
        o_ref[:, pl.ds(pl.multiple_of((2 * b + h) * w, w), w)] = ref[...]


def shift(x, axis, by):
    n = lax.axis_size(axis)
    return lax.ppermute(x, axis, [((d + by) % n, d) for d in range(n)])


def layer(queries, keys, values, gain, out_weight, grad_out):
    tok_rows, feat_width = queries.shape[1:]
    model_width = grad_out.shape[2]
    q = queries.reshape(tok_rows, feat_width)
    k = keys.reshape(tok_rows, feat_width)
    v = values.reshape(tok_rows, feat_width)
    grad_rows = grad_out.reshape(tok_rows, model_width)
    gain_row = gain.reshape(1, feat_width)
    seqs = lax.axis_size("x")
    blocks_n = lax.axis_size(CTX)
    at_x = lax.axis_index("x")
    at_ctx = lax.axis_index(CTX)
    at_core = lax.axis_index("c")
    places = [at_x, lax.axis_index("z"), lax.axis_index("y"), at_core]
    order = [(at_x + n) % CH for n in range(CH)]
    where = jnp.stack(order + places).astype(jnp.int32)
    row_half = at_x // 2
    turns = [2 * row_half, 2 * row_half + 1, 2 - 2 * row_half, 3 - 2 * row_half]
    turns = jnp.stack(turns + places).astype(jnp.int32)
    mine = at_core.reshape(1).astype(jnp.int32)
    others = 1 - mine

    piece = out_weight.shape[0] // blocks_n
    own_piece = lax.dynamic_slice_in_dim(out_weight, at_ctx * piece, piece, 0)
    pieces = [shift(own_piece, "x", by) for by in range(1, CH)]
    state = local_state(k, v)
    half_cols = model_width // 2
    side = at_x % 2
    pieces, sent_rows, q_next = lax.optimization_barrier((pieces, grad_rows, q, state))[:3]
    near_cols = lax.dynamic_slice_in_dim(sent_rows, side * half_cols, half_cols, 1)
    far_cols = lax.dynamic_slice_in_dim(sent_rows, (1 - side) * half_cols, half_cols, 1)
    gathered = lax.all_gather(jnp.concatenate(pieces, axis=0), CTX, axis=0, tiled=True)
    gathered = gathered.reshape(blocks_n, CH - 1, piece, model_width)
    gathered = pltpu.with_memory_space_constraint(gathered, pltpu.HBM)
    own_weight = pltpu.with_memory_space_constraint(out_weight, pltpu.HBM)

    grads_all = [
        near_cols,
        partner(far_cols, "x", 1),
        partner(near_cols, "x", 2),
        partner(far_cols, "x", 3),
    ]

    carried, (weights, local_out), _, _ = carry(
        state,
        where,
        at_core,
        False,
        lambda sent: local_scores(after(q_next, sent), k, v),
        lambda sent, done: (),
        lambda sent, done: (),
    )
    near, far, near_t, far_t, attended = attend(turns, q, hbm(local_out), carried, gain_row)
    normed_all = [near_t, partner(near_t, "x", 1), partner(far_t, "x", 2), partner(far_t, "x", 3)]
    gn = hbm(mm(after(sent_rows, near), out_weight, 1, 1))

    ga, lg = grad_attn(where, q, hbm(attended), gn, gain_row, hbm(grad_rows), gathered)
    chips = blocks_n // 2
    shape = (chips, 2, out_weight.shape[0] // chips, half_cols // 2)

    def first_half(sent):
        rows = after(normed_all, sent)
        return weight_half(others, rows, grads_all, shape, None)

    def second_half(sent, for_partner):
        extra = give_to(for_partner, "c", 1)
        rows = after(normed_all, sent)
        return weight_half(mine, rows, grads_all, shape, extra)

    def rest(sent, partial):
        parts = lax.all_to_all(partial, ("z", "y"), 0, 0, tiled=True)
        grads = local_grads(where, q, k, v, hbm(weights), hbm(after(ga, sent)), carried)
        rows = layer_rows(where, near, after(far, grads), own_weight, gathered)
        return parts, (grads, rows)

    later, _, _, (parts, (grads, layer_out)) = carry(
        lg, where, at_core, True, first_half, second_half, rest
    )
    grad_query, pk, pv = grads
    grad_key, grad_value = later_grads(where, k, v, later, hbm(pk), hbm(pv))

    parts = after(parts, layer_out, later[0])
    token_count = seqs * blocks_n * tok_rows
    own, to_x, to_c, to_both = sum_parts(where, parts, 1.0 / math.sqrt(token_count))
    both = lax.ppermute(to_both, ("x", "c"), [(d, d ^ 3) for d in range(2 * seqs)])
    (grad_weight,) = small_call(
        join_body,
        where,
        [own, partner(to_x, "x", 1), partner(to_c, "c", 1), both],
        [jax.ShapeDtypeStruct((own.shape[0], model_width), F32)],
    )
    out_shape = (1, tok_rows, feat_width)
    return (
        layer_out.reshape(1, tok_rows, model_width),
        grad_query.reshape(out_shape),
        grad_key.reshape(out_shape),
        grad_value.reshape(out_shape),
        grad_weight,
    )


def solution(mesh):
    mesh = Mesh(mesh.devices.reshape(4, 4, 4, 2), ("x",) + CTX)
    tokens = P("x", CTX, None)
    in_specs = (tokens, tokens, tokens, P(), P("x", None), tokens)
    out_specs = (tokens, tokens, tokens, tokens, P(("x",) + CTX, None))
    return jax.shard_map(layer, mesh=mesh, in_specs=in_specs, out_specs=out_specs, check_vma=False)
```

```python
import functools
import math

import jax
import jax.numpy as jnp
from jax import lax
from jax.experimental import pallas as pl
from jax.experimental.pallas import tpu as pltpu
from jax.sharding import Mesh, PartitionSpec as P

HD = 128
EPSILON = 1e-06
BF = jnp.bfloat16
F32 = jnp.float32
CTX = ("z", "y", "c")
CH = 4
HC = 4


def mm(a, b, ca, cb):
    return lax.dot_general(a, b, (((ca,), (cb,)), ((), ())), preferred_element_type=F32)


def cost(flops, nbytes):
    return pl.CostEstimate(flops=flops, bytes_accessed=nbytes, transcendentals=0)


def head(ref, h):
    return ref[:, h * HD : (h + 1) * HD]


def causal(n):
    return lax.broadcasted_iota(jnp.int32, (n, n), 0) >= lax.broadcasted_iota(
        jnp.int32, (n, n), 1
    )


def state_body(k_ref, v_ref, s_ref):
    for h in range(HC):
        s_ref[h] = mm(head(k_ref, h), head(v_ref, h), 0, 0).astype(BF)


def local_state(k, v):
    t, f = k.shape
    w = f // CH
    blk = pl.BlockSpec((t, w), lambda g: (0, g))
    return pl.pallas_call(
        state_body,
        grid=(CH,),
        in_specs=[blk, blk],
        out_specs=pl.BlockSpec((HC, HD, HD), lambda g: (g, 0, 0)),
        out_shape=jax.ShapeDtypeStruct((CH * HC, HD, HD), BF),
        cost_estimate=cost(2 * t * f * HD, 4 * t * f),
        compiler_params=pltpu.CompilerParams(vmem_limit_bytes=6 << 20),
        name="local_state",
    )(k, v)


def small_call(body, where, args, outs):
    return pl.pallas_call(
        body,
        in_specs=[pl.BlockSpec(memory_space=pltpu.SMEM)]
        + [pl.BlockSpec(memory_space=pltpu.VMEM)] * len(args),
        out_specs=[pl.BlockSpec(memory_space=pltpu.VMEM)] * len(outs),
        out_shape=outs,
        compiler_params=pltpu.CompilerParams(vmem_limit_bytes=6 << 20),
        cost_estimate=cost(1 << 18, 1 << 20),
    )(where, *args)


def chip_body(w_ref, s_ref, r_ref, own_ref, *out_refs):
    y, c = w_ref[6], w_ref[7]
    n = s_ref.shape[1]
    for k in range(n):
        at = lax.rem(y + k, n)
        part = s_ref[c, at].astype(F32) + r_ref[at].astype(F32)
        if k == 0:
            own_ref[...] = part
        else:
            out_refs[k - 1][...] = part.astype(BF)


def row_body(w_ref, own_ref, *refs):
    total = own_ref[...]
    for ref in refs[:-1]:
        total = total + ref[...].astype(F32)
    refs[-1][...] = total.astype(BF)


def plane_body(reverse, w_ref, own_ref, t1, t2, t3, z1, z2, z3, o_ref, o1, o2, o3):
    z, y = w_ref[5], w_ref[6]
    terms = [own_ref[...]] + [t[...].astype(F32) for t in (t1, t2, t3)]
    n = len(terms)
    base = jnp.zeros_like(terms[0])
    for k, ref in enumerate((z1, z2, z3), 1):
        use = z < k if reverse else z >= k
        base = base + jnp.where(use, ref[...].astype(F32), 0.0)
    for k in range(n):
        to = lax.rem(y + k, n)
        total = base
        for j in range(n):
            source = lax.rem(y - j + n, n)
            use = source > to if reverse else source < to
            total = total + jnp.where(use, terms[j], 0.0)
        if k == 0:
            o_ref[...] = total
        else:
            (o1, o2, o3)[k - 1][...] = total.astype(BF)


def core_body(reverse, w_ref, s_ref, r_ref, p0, p1, p2, p3, mine_ref, give_ref):
    y, c = w_ref[6], w_ref[7]
    n = s_ref.shape[1]
    first = c == (1 if reverse else 0)
    for j, p in enumerate((p0, p1, p2, p3)):
        at = lax.rem(y - j + n, n)
        base = p[...].astype(F32)
        mine_ref[at] = (base + jnp.where(first, 0.0, r_ref[at].astype(F32))).astype(BF)
        give_ref[at] = (base + jnp.where(first, s_ref[c, at].astype(F32), 0.0)).astype(BF)


def partner(x, axis, bits):
    return lax.ppermute(x, axis, [(d, d ^ bits) for d in range(lax.axis_size(axis))])


def give_to(x, axis, by):
    n = lax.axis_size(axis)
    return lax.ppermute(x, axis, [(d, (d + by) % n) for d in range(n)])


def carry(state, where, core, reverse, fill_row, fill_plane, fill_core):
    heads, d, e = state.shape
    n = lax.axis_size("y")
    rows = heads * d // (2 * n)
    parts = state.reshape(2, n, rows, e)
    give = lax.dynamic_index_in_dim(parts, 1 - core, 0, False)
    other = give_to(give, "c", 1)
    one = jax.ShapeDtypeStruct((rows, e), F32)
    low = jax.ShapeDtypeStruct((rows, e), BF)
    half = jax.ShapeDtypeStruct((n, rows, e), BF)
    own, *out = small_call(chip_body, where, [parts, other], [one] + [low] * (n - 1))
    terms = [own] + [give_to(x, "y", k) for k, x in enumerate(out, 1)]
    filled_row = fill_row(out)
    terms = after(terms, filled_row)
    (row,) = small_call(row_body, where, terms, [low])
    rows_before = [give_to(row, "z", k) for k in range(1, n)]
    filled_plane = fill_plane(row, filled_row)
    rows_before = after(rows_before, filled_plane)
    own, *out = small_call(
        functools.partial(plane_body, reverse), where, terms + rows_before, [one] + [low] * (n - 1)
    )
    sums = [own] + [give_to(x, "y", k) for k, x in enumerate(out, 1)]
    filled_core = fill_core(out, filled_plane)
    sums = after(sums, filled_core[-1] if reverse else filled_core)
    mine, give = small_call(
        functools.partial(core_body, reverse), where, [parts, other] + sums, [half] * 2
    )
    got = give_to(give, "c", 1)
    shape = (heads // 2, d, e)
    return (mine.reshape(shape), got.reshape(shape)), filled_row, filled_plane, filled_core


def hbm(x):
    return pltpu.with_memory_space_constraint(x, pltpu.HBM)


def after(x, *others):
    return lax.optimization_barrier((x, others))[0]


def scores_body(q_ref, k_ref, v_ref, w_ref, o_ref):
    keep = causal(q_ref.shape[0])
    for h in range(HC):
        w = jnp.where(keep, mm(head(q_ref, h), head(k_ref, h), 1, 1), 0.0).astype(BF)
        w_ref[h] = w
        o_ref[:, h * HD : (h + 1) * HD] = mm(w, head(v_ref, h), 1, 0)


def local_scores(q, k, v):
    t, f = q.shape
    w = f // CH
    blk = pl.BlockSpec((t, w), lambda g: (0, g))
    return pl.pallas_call(
        scores_body,
        grid=(CH,),
        in_specs=[blk, blk, blk],
        out_specs=[pl.BlockSpec((HC, t, t), lambda g: (g, 0, 0)), blk],
        out_shape=[
            pltpu.HBM((CH * HC, t, t), BF),
            pltpu.HBM((t, f), F32),
        ],
        cost_estimate=cost(4 * t * t * f, 14 * t * f),
        compiler_params=pltpu.CompilerParams(vmem_limit_bytes=12 << 20),
        name="local_scores",
    )(q, k, v)


def pick(w_ref, chunk, m_ref, t_ref, h):
    return jnp.where(lax.div(chunk, CH // 2) == w_ref[7], m_ref[h], t_ref[h])


def attend_body(w_ref, q_ref, o_ref, m_ref, t_ref, g_ref, near_ref, far_ref, near_t_ref, far_t_ref, a_ref):
    g = pl.program_id(0)
    normed = []
    for h in range(HC):
        cols = slice(h * HD, (h + 1) * HD)
        state = pick(w_ref, w_ref[g], m_ref, t_ref, h)
        a = o_ref[:, cols] + mm(head(q_ref, h), state, 1, 0)
        a_ref[0, :, cols] = a
        inv = lax.rsqrt(jnp.mean(a * a, axis=-1, keepdims=True) + EPSILON)
        normed.append((a * inv * g_ref[:, cols]).astype(BF))
    normed = jnp.concatenate(normed, axis=1)

    @pl.when(g < CH // 2)
    def _():
        near_ref[...] = normed
        near_t_ref[...] = normed.T

    @pl.when(g >= CH // 2)
    def _():
        far_ref[...] = normed
        far_t_ref[...] = normed.T


def attend(where, q, out, carried, gain):
    t, f = q.shape
    w = f // CH
    two = CH // 2
    blk = pl.BlockSpec((t, w), lambda g, i: (0, i[g]))
    st = pl.BlockSpec((HC, HD, HD), lambda g, i: (lax.rem(i[g], two), 0, 0))
    return pl.pallas_call(
        attend_body,
        grid_spec=pltpu.PrefetchScalarGridSpec(
            num_scalar_prefetch=1,
            grid=(CH,),
            in_specs=[blk, blk, st, st, pl.BlockSpec((1, w), lambda g, i: (0, i[g]))],
            out_specs=[
                pl.BlockSpec((t, w), lambda g, i: (0, jnp.minimum(g, two - 1))),
                pl.BlockSpec((t, w), lambda g, i: (0, jnp.maximum(g - two, 0))),
                pl.BlockSpec((w, t), lambda g, i: (jnp.minimum(g, two - 1), 0)),
                pl.BlockSpec((w, t), lambda g, i: (jnp.maximum(g - two, 0), 0)),
                pl.BlockSpec((1, t, w), lambda g, i: (i[g], 0, 0)),
            ],
        ),
        out_shape=[jax.ShapeDtypeStruct((t, two * w), BF)] * 2
        + [jax.ShapeDtypeStruct((two * w, t), BF)] * 2
        + [pltpu.HBM((CH, t, w), F32)],
        cost_estimate=cost(2 * t * f * HD, 12 * t * f),
        compiler_params=pltpu.CompilerParams(vmem_limit_bytes=12 << 20),
        name="attend",
    )(where, q, out, *carried, gain)


PARTS = 1
SLOTS = 2


def grad_attn_body(
    i_ref, q_ref, a_ref, gn_ref, g_ref, go_hbm, w_hbm, ga_ref, lg_ref, go, w, go_sem, w_sem
):
    g = pl.program_id(0)
    _, blocks, rows, d = w.shape
    last = PARTS * (CH - 1)

    def load(t):
        at = pl.ds(lax.rem(t, PARTS) * blocks, blocks)
        slot = lax.rem(t, SLOTS)
        source = w_hbm.at[at, lax.div(t, PARTS)]
        return pltpu.make_async_copy(source, w.at[slot], w_sem.at[slot])

    whole = pltpu.make_async_copy(go_hbm, go, go_sem)

    def finish(gn):
        for h in range(HC // PARTS):
            cols = slice(h * HD, (h + 1) * HD)
            a = a_ref[0, :, cols]
            inv = lax.rsqrt(jnp.mean(a * a, axis=-1, keepdims=True) + EPSILON)
            unit = a * inv
            gu = gn[:, cols] * g_ref[:, cols]
            ga = inv * (gu - unit * jnp.mean(gu * unit, axis=-1, keepdims=True))
            ga = ga.astype(BF)
            ga_ref[0, :, cols] = ga
            lg_ref[h] = mm(head(q_ref, h), ga, 0, 0).astype(BF)

    @pl.when(g == 0)
    def _():
        whole.start()
        load(0).start()

    @pl.when(g < PARTS)
    def _():
        finish(gn_ref[...])

    @pl.when(g == PARTS)
    def _():
        whole.wait()

    @pl.when(g >= PARTS)
    def _():
        t = g - PARTS
        load(t).wait()

        @pl.when(t + 1 < last)
        def _():
            load(t + 1).start()

        finish(mm(go[...], w[lax.rem(t, SLOTS)].reshape(blocks * rows, d), 1, 1))


def grad_attn(order, q, attended, gn, gain, grad_rows, gathered):
    t, f = q.shape
    w = f // CH // PARTS
    n, _, r, d = gathered.shape

    def nat(g, i):
        return (0, i[lax.div(g, PARTS)] * PARTS + lax.rem(g, PARTS))

    return pl.pallas_call(
        grad_attn_body,
        grid_spec=pltpu.PrefetchScalarGridSpec(
            num_scalar_prefetch=1,
            grid=(CH * PARTS,),
            in_specs=[
                pl.BlockSpec((t, w), nat),
                pl.BlockSpec(
                    (1, t, w), lambda g, i: (i[lax.div(g, PARTS)], 0, lax.rem(g, PARTS))
                ),
                pl.BlockSpec((t, w), lambda g, i: (0, jnp.minimum(g, PARTS - 1))),
                pl.BlockSpec((1, w), nat),
                pl.BlockSpec(memory_space=pltpu.HBM),
                pl.BlockSpec(memory_space=pltpu.HBM),
            ],
            out_specs=[
                pl.BlockSpec((1, t, w), lambda g, i: (lax.div(g, PARTS), 0, lax.rem(g, PARTS))),
                pl.BlockSpec((HC // PARTS, HD, HD), lambda g, i: (g, 0, 0)),
            ],
            scratch_shapes=[
                pltpu.VMEM((t, d), BF),
                pltpu.VMEM((SLOTS, n // PARTS, r, d), BF),
                pltpu.SemaphoreType.DMA(()),
                pltpu.SemaphoreType.DMA((SLOTS,)),
            ],
        ),
        out_shape=[
            pltpu.HBM((CH, t, f // CH), BF),
            jax.ShapeDtypeStruct((CH * HC, HD, HD), BF),
        ],
        cost_estimate=cost(2 * t * f * HD + 6 * t * w * d, 12 * t * f + 6 * w * d),
        compiler_params=pltpu.CompilerParams(vmem_limit_bytes=26 << 20),
        name="grad_attn",
    )(order, q, attended, gn, gain, grad_rows, gathered)


def grads_body(i_ref, q_ref, k_ref, v_ref, w_ref, ga_ref, m_ref, t_ref, gq_ref, gk_ref, gv_ref):
    chunk = i_ref[pl.program_id(0)]
    keep = causal(q_ref.shape[0])
    for h in range(HC):
        cols = slice(h * HD, (h + 1) * HD)
        ga = ga_ref[0, :, cols]
        gs = jnp.where(keep, mm(ga, head(v_ref, h), 1, 1), 0.0).astype(BF)
        gq = mm(gs, head(k_ref, h), 1, 0) + mm(ga, pick(i_ref, chunk, m_ref, t_ref, h), 1, 1)
        gq_ref[:, cols] = gq.astype(BF)
        gk_ref[0, :, cols] = mm(gs, head(q_ref, h), 0, 0).astype(BF)
        gv_ref[0, :, cols] = mm(w_ref[h], ga, 0, 0).astype(BF)


def local_grads(order, q, k, v, weights, ga, carried):
    t, f = q.shape
    w = f // CH
    nat = pl.BlockSpec((t, w), lambda g, i: (0, i[g]))
    chunk = pl.BlockSpec((1, t, w), lambda g, i: (g, 0, 0))
    return pl.pallas_call(
        grads_body,
        grid_spec=pltpu.PrefetchScalarGridSpec(
            num_scalar_prefetch=1,
            grid=(CH,),
            in_specs=[
                nat,
                nat,
                nat,
                pl.BlockSpec((HC, t, t), lambda g, i: (i[g], 0, 0)),
                chunk,
            ]
            + [pl.BlockSpec((HC, HD, HD), lambda g, i: (lax.rem(i[g], CH // 2), 0, 0))] * 2,
            out_specs=[nat, chunk, chunk],
        ),
        out_shape=[
            jax.ShapeDtypeStruct((t, f), BF),
            pltpu.HBM((CH, t, w), BF),
            pltpu.HBM((CH, t, w), BF),
        ],
        cost_estimate=cost(8 * t * t * f, 24 * t * f),
        compiler_params=pltpu.CompilerParams(vmem_limit_bytes=20 << 20),
        name="local_grads",
    )(order, q, k, v, weights, ga, *carried)


def later_body(i_ref, k_ref, v_ref, m_ref, t_ref, pk_ref, pv_ref, gk_ref, gv_ref):
    for h in range(HC):
        cols = slice(h * HD, (h + 1) * HD)
        state = pick(i_ref, pl.program_id(0), m_ref, t_ref, h)
        gk = pk_ref[0, :, cols].astype(F32) + mm(head(v_ref, h), state, 1, 1)
        gv = pv_ref[0, :, cols].astype(F32) + mm(head(k_ref, h), state, 1, 0)
        gk_ref[:, cols] = gk.astype(BF)
        gv_ref[:, cols] = gv.astype(BF)


def later_grads(order, k, v, later, pk, pv):
    t, f = k.shape
    w = f // CH
    nat = pl.BlockSpec((t, w), lambda g, i: (0, i[g]))
    chunk = pl.BlockSpec((1, t, w), lambda g, i: (g, 0, 0))
    return pl.pallas_call(
        later_body,
        grid_spec=pltpu.PrefetchScalarGridSpec(
            num_scalar_prefetch=1,
            grid=(CH,),
            in_specs=[
                nat,
                nat,
                pl.BlockSpec((HC, HD, HD), lambda g, i: (lax.rem(g, CH // 2), 0, 0)),
                pl.BlockSpec((HC, HD, HD), lambda g, i: (lax.rem(g, CH // 2), 0, 0)),
                chunk,
                chunk,
            ],
            out_specs=[nat, nat],
        ),
        out_shape=[jax.ShapeDtypeStruct((t, f), BF)] * 2,
        cost_estimate=cost(4 * t * f * HD, 16 * t * f),
        compiler_params=pltpu.CompilerParams(vmem_limit_bytes=12 << 20),
        name="later_grads",
    )(order, k, v, *later, pk, pv)


def layer_body(i_ref, near_ref, far_ref, own_ref, w_ref, o_ref):
    w = own_ref.shape[0]
    mine = lax.div(i_ref[4], CH // 2)
    total = None
    for k in range(CH):
        chunk = i_ref[k]
        cols = pl.ds(pl.multiple_of(lax.rem(chunk, CH // 2) * w, w), w)
        is_near = lax.div(chunk, CH // 2) == mine
        rows = jnp.where(is_near, near_ref[:, cols], far_ref[:, cols])
        block = own_ref[...] if k == 0 else w_ref[:, k - 1].reshape(own_ref.shape)
        part = mm(rows, block, 1, 0)
        total = part if total is None else total + part
    o_ref[...] = total.astype(BF)


def layer_rows(where, near, far, own, gathered):
    t = near.shape[0]
    w = own.shape[0]
    n, c, r, d = gathered.shape
    tile = 1024
    half = pl.BlockSpec(near.shape, lambda g, i: (0, 0))
    return pl.pallas_call(
        layer_body,
        grid_spec=pltpu.PrefetchScalarGridSpec(
            num_scalar_prefetch=1,
            grid=(d // tile,),
            in_specs=[
                half,
                half,
                pl.BlockSpec((w, tile), lambda g, i: (0, g)),
                pl.BlockSpec((n, c, r, tile), lambda g, i: (0, 0, 0, g)),
            ],
            out_specs=pl.BlockSpec((t, tile), lambda g, i: (0, g)),
        ),
        out_shape=jax.ShapeDtypeStruct((t, d), BF),
        cost_estimate=cost(2 * t * CH * w * d, 2 * (CH * w * d + CH * t * w + t * d)),
        compiler_params=pltpu.CompilerParams(vmem_limit_bytes=20 << 20),
        name="layer_rows",
    )(where, near, far, own, gathered)


def weight_body(add, i_ref, *refs):
    rows, grads = refs[:CH], refs[CH : 2 * CH]
    o_ref = refs[-1]
    left = jnp.concatenate([n[...] for n in rows], axis=1)
    total = mm(left, jnp.concatenate([g[...] for g in grads], axis=0), 1, 0)
    chips, blocks, r, w = o_ref.shape
    span = chips * r
    for b in range(blocks):
        one = total[b * span : (b + 1) * span].reshape(chips, r, w)
        if add:
            one = one + refs[2 * CH][:, b].astype(F32)
        o_ref[:, b] = one.astype(BF)


def weight_half(half, rows, grads_all, shape, extra):
    t, d = grads_all[0].shape
    w = rows[0].shape[0]
    tile = 256
    steps = d // 2 // tile
    add = extra is not None
    own = pl.BlockSpec(shape[:-1] + (tile,), lambda g, i: (0, 0, 0, g))
    whole = pl.BlockSpec((w, t), lambda g, i: (0, 0))
    cols = pl.BlockSpec((t, tile), lambda g, i: (0, i[0] * steps + g))
    return pl.pallas_call(
        functools.partial(weight_body, add),
        grid_spec=pltpu.PrefetchScalarGridSpec(
            num_scalar_prefetch=1,
            grid=(steps,),
            in_specs=[whole] * CH + [cols] * CH + [own] * add,
            out_specs=own,
        ),
        out_shape=pltpu.HBM(shape, BF),
        cost_estimate=cost(CH * t * w * d, 2 * CH * t * d + 2 * CH * t * w + w * d),
        compiler_params=pltpu.CompilerParams(vmem_limit_bytes=20 << 20),
        name="weight_half",
    )(half, *rows, *grads_all, *([extra] if add else []))


def sum_body(scale, w_ref, s_ref, keep_ref, x_ref, c_ref, xc_ref, total):
    acc = s_ref[0].astype(F32)
    for step in range(1, s_ref.shape[0]):
        acc = acc + s_ref[step].astype(F32)
    total[...] = acc * scale
    rows = keep_ref.shape[0]
    block, c = lax.rem(w_ref[4], 2), w_ref[7]
    mine = pl.ds(pl.multiple_of(c * rows, rows), rows)
    other = pl.ds(pl.multiple_of((1 - c) * rows, rows), rows)
    keep_ref[...] = total[block, mine]
    x_ref[...] = total[1 - block, mine]
    c_ref[...] = total[block, other]
    xc_ref[...] = total[1 - block, other]


def sum_parts(where, parts, scale):
    _, b, r, w = parts.shape
    return pl.pallas_call(
        functools.partial(sum_body, scale),
        in_specs=[
            pl.BlockSpec(memory_space=pltpu.SMEM),
            pl.BlockSpec(memory_space=pltpu.VMEM),
        ],
        out_specs=[pl.BlockSpec(memory_space=pltpu.VMEM)] * 4,
        out_shape=[jax.ShapeDtypeStruct((r // 2, w), F32)] * 4,
        scratch_shapes=[pltpu.VMEM((b, r, w), F32)],
        cost_estimate=cost(parts.size, 2 * parts.size),
        compiler_params=pltpu.CompilerParams(vmem_limit_bytes=8 << 20),
        name="sum_parts",
    )(where, parts)


def join_body(w_ref, own_ref, x_ref, c_ref, xc_ref, o_ref):
    block, c = lax.rem(w_ref[4], 2), w_ref[7]
    w = own_ref.shape[1]
    for ref, b, h in (
        (own_ref, block, c),
        (x_ref, 1 - block, c),
        (c_ref, block, 1 - c),
        (xc_ref, 1 - block, 1 - c),
    ):
        o_ref[:, pl.ds(pl.multiple_of((2 * b + h) * w, w), w)] = ref[...]


def shift(x, axis, by):
    n = lax.axis_size(axis)
    return lax.ppermute(x, axis, [((d + by) % n, d) for d in range(n)])


def layer(queries, keys, values, gain, out_weight, grad_out):
    tok_rows, feat_width = queries.shape[1:]
    model_width = grad_out.shape[2]
    q = queries.reshape(tok_rows, feat_width)
    k = keys.reshape(tok_rows, feat_width)
    v = values.reshape(tok_rows, feat_width)
    grad_rows = grad_out.reshape(tok_rows, model_width)
    gain_row = gain.reshape(1, feat_width)
    seqs = lax.axis_size("x")
    blocks_n = lax.axis_size(CTX)
    at_x = lax.axis_index("x")
    at_ctx = lax.axis_index(CTX)
    at_core = lax.axis_index("c")
    places = [at_x, lax.axis_index("z"), lax.axis_index("y"), at_core]
    order = [(at_x + n) % CH for n in range(CH)]
    where = jnp.stack(order + places).astype(jnp.int32)
    row_half = at_x // 2
    turns = [2 * row_half, 2 * row_half + 1, 2 - 2 * row_half, 3 - 2 * row_half]
    turns = jnp.stack(turns + places).astype(jnp.int32)
    mine = at_core.reshape(1).astype(jnp.int32)
    others = 1 - mine

    piece = out_weight.shape[0] // blocks_n
    own_piece = lax.dynamic_slice_in_dim(out_weight, at_ctx * piece, piece, 0)
    pieces = [shift(own_piece, "x", by) for by in range(1, CH)]
    state = local_state(k, v)
    half_cols = model_width // 2
    side = at_x % 2
    pieces, sent_rows, q_next = lax.optimization_barrier((pieces, grad_rows, q, state))[:3]
    near_cols = lax.dynamic_slice_in_dim(sent_rows, side * half_cols, half_cols, 1)
    far_cols = lax.dynamic_slice_in_dim(sent_rows, (1 - side) * half_cols, half_cols, 1)
    gathered = lax.all_gather(jnp.concatenate(pieces, axis=0), CTX, axis=0, tiled=True)
    gathered = gathered.reshape(blocks_n, CH - 1, piece, model_width)
    gathered = pltpu.with_memory_space_constraint(gathered, pltpu.HBM)
    own_weight = pltpu.with_memory_space_constraint(out_weight, pltpu.HBM)

    grads_all = [
        near_cols,
        partner(far_cols, "x", 1),
        partner(near_cols, "x", 2),
        partner(far_cols, "x", 3),
    ]

    carried, (weights, local_out), _, _ = carry(
        state,
        where,
        at_core,
        False,
        lambda sent: local_scores(after(q_next, sent), k, v),
        lambda sent, done: (),
        lambda sent, done: (),
    )
    near, far, near_t, far_t, attended = attend(turns, q, hbm(local_out), carried, gain_row)
    normed_all = [near_t, partner(near_t, "x", 1), partner(far_t, "x", 2), partner(far_t, "x", 3)]
    gn = hbm(mm(after(sent_rows, near), out_weight, 1, 1))

    ga, lg = grad_attn(where, q, hbm(attended), gn, gain_row, hbm(grad_rows), gathered)
    chips = blocks_n // 2
    shape = (chips, 2, out_weight.shape[0] // chips, half_cols // 2)

    def first_half(sent):
        rows = after(normed_all, sent)
        return weight_half(others, rows, grads_all, shape, None)

    def second_half(sent, for_partner):
        extra = give_to(for_partner, "c", 1)
        rows = after(normed_all, sent)
        return weight_half(mine, rows, grads_all, shape, extra)

    def rest(sent, partial):
        parts = lax.all_to_all(partial, ("z", "y"), 0, 0, tiled=True)
        grads = local_grads(where, q, k, v, hbm(weights), hbm(after(ga, sent)), carried)
        rows = layer_rows(where, near, after(far, grads), own_weight, gathered)
        return parts, (grads, rows)

    later, _, _, (parts, (grads, layer_out)) = carry(
        lg, where, at_core, True, first_half, second_half, rest
    )
    grad_query, pk, pv = grads
    grad_key, grad_value = later_grads(where, k, v, later, hbm(pk), hbm(pv))

    parts = after(parts, layer_out, later[0])
    token_count = seqs * blocks_n * tok_rows
    own, to_x, to_c, to_both = sum_parts(where, parts, 1.0 / math.sqrt(token_count))
    both = lax.ppermute(to_both, ("x", "c"), [(d, d ^ 3) for d in range(2 * seqs)])
    (grad_weight,) = small_call(
        join_body,
        where,
        [own, partner(to_x, "x", 1), partner(to_c, "c", 1), both],
        [jax.ShapeDtypeStruct((own.shape[0], model_width), F32)],
    )
    out_shape = (1, tok_rows, feat_width)
    return (
        layer_out.reshape(1, tok_rows, model_width),
        grad_query.reshape(out_shape),
        grad_key.reshape(out_shape),
        grad_value.reshape(out_shape),
        grad_weight,
    )


def solution(mesh):
    mesh = Mesh(mesh.devices.reshape(4, 4, 4, 2), ("x",) + CTX)
    tokens = P("x", CTX, None)
    in_specs = (tokens, tokens, tokens, P(), P("x", None), tokens)
    out_specs = (tokens, tokens, tokens, tokens, P(("x",) + CTX, None))
    return jax.shard_map(layer, mesh=mesh, in_specs=in_specs, out_specs=out_specs, check_vma=False)
```
